256 devices in a mesh: gy: 16 (over y_hi, x, core), gx: 16 (over y_lo, z).
Axes of the slice: x: 4, y: 4 (y_hi: 2, y_lo: 2; y = y_hi * 2 + y_lo), z: 8, core: 2. Of those that a mesh axis runs over, the one named last changes fastest.
Arguments:
- stored_tiles: float32 [16, 128, 12288], P('gy', 'gx'), may hold values from -6 to 6
- tile_target: int32 [16, 128], P('gy', 'gx'), may hold values from 0 to 127, as said below
- tile_mask: int32 [16, 128], P('gy', 'gx'), may hold values 0 or 1
- stem_weight: float32 [48, 96], replicated, may hold values from -0.875 to 0.875
- stem_bias: float32 [96], replicated, may hold values from -3 to 3
- depth_weight: float32 [49, 96], replicated, may hold values from -0.875 to 0.875
- depth_bias: float32 [96], replicated, may hold values from -4 to 4
- norm_gain: float32 [96], replicated, may hold values from 0.5 to 1.5
- norm_bias: float32 [96], replicated, may hold values from -3 to 3
- expand_weight: float32 [96, 384], replicated, may hold values from -0.625 to 0.625
- expand_bias: float32 [384], replicated, may hold values from -3 to 3
- shrink_weight: float32 [384, 96], replicated, may hold values from -0.3125 to 0.3125
- shrink_bias: float32 [96], replicated, may hold values from -3 to 3
- cotangent: float32 [96, 256, 2048], P(None, 'gy', 'gx'), may hold values from -6 to 6
Outputs:
- block_out: float32 [96, 256, 2048], P(None, 'gy', 'gx')
- grad_stem_weight: float32 [48, 96], replicated
- grad_stem_bias: float32 [96], replicated
- grad_depth_weight: float32 [49, 96], replicated
- grad_depth_bias: float32 [96], replicated
- grad_norm_gain: float32 [96], replicated
- grad_norm_bias: float32 [96], replicated
- grad_expand_weight: float32 [96, 384], replicated
- grad_expand_bias: float32 [384], replicated
- grad_shrink_weight: float32 [384, 96], replicated
- grad_shrink_bias: float32 [96], replicated
The draws below stay inside these ranges and needn't reach their ends.
Inputs may be any that keep to these rules, and one draw needn't show every extreme that they name: `tile_target`: in each row r the 128 slots hold each target 0 to 127 once; the target's grid cell is row r, column target // 8. The 8 slots of the device in column i of gx send exactly 4 tiles to each cell of column (i + 1 + k * 8) mod 16, k < 2, and none to the others.
All inputs are finite; a program needn't handle non-finite values. No bound on the sum of `tile_mask` on one device may be relied on, other than what follows from the above.
Results may differ from the reference program's by a relative error of at most 0.0003.
Values sent between devices are 32-bit elements; how exact they have to be, the bound alone decides.
A program may use at most 128 MiB of HBM per device.

```python
import jax
import jax.numpy as jnp
from jax import lax

C = 96
HID = 384
TS = 64
TBX = 8
TBY = 1
SERVED = 2
GRID_ROWS = 16
GRID_COLS = 16
TPC = 8
CAP = 4
SLOTS = 128
PIX = 12288
CFH = 16
HF = 256
WF = 2048


def draw_tile_target(key, part):

    def one_row(row_key):
        keys = jax.random.split(row_key, 2)
        slot_perm = jax.vmap(lambda sub_key: jax.random.permutation(sub_key, TPC))(jax.random.split(keys[0], GRID_COLS)).astype(jnp.int32)
        bucket = slot_perm // CAP
        within = slot_perm % CAP
        sender = jnp.arange(GRID_COLS, dtype=jnp.int32)[:, None]
        target_col = (sender + 1 + bucket * (GRID_COLS // SERVED)) % GRID_COLS
        place_perms = jax.vmap(lambda sub_key: jax.random.permutation(sub_key, TPC))(jax.random.split(keys[1], GRID_COLS)).astype(jnp.int32)
        places = place_perms[target_col, bucket * CAP + within]
        targets = target_col * TPC + places
        return targets.reshape(GRID_COLS * TPC)
    row_keys = jax.random.split(jax.random.fold_in(key, 11), GRID_ROWS)
    return jax.vmap(one_row)(row_keys).astype(jnp.int32)


def with_ends(array, rng, smallest, high):
    dims = array.shape
    place = [jax.random.randint(jax.random.fold_in(rng, axis), (), 0, dims[axis]) for axis in range(len(dims))]
    array = array.at[tuple(place)].set(smallest)
    longest = dims.index(max(dims))
    place[longest] = (place[longest] + 1) % dims[longest]
    return array.at[tuple(place)].set(high)


def block_scale(rng, shape, shards, least, high):
    loudness = 1.0
    for axis_at, shards_of in shards:
        heights = jax.random.uniform(jax.random.fold_in(jax.random.fold_in(rng, 6), axis_at), (shards_of,), jnp.float32, least / len(shards), high / len(shards))
        loudness = loudness * jnp.repeat(jnp.exp(heights), shape[axis_at] // shards_of).reshape((-1,) + (1,) * (len(shape) - 1 - axis_at))
    return loudness


def scatter_about(key, shape, deviation, bound, cuts=(), held_as=jnp.bfloat16):
    loudness = block_scale(key, shape, cuts, -0.22, 0.18) if cuts else 1.0
    values = jax.random.normal(key, shape, jnp.float32) * deviation * loudness
    return jnp.minimum(jnp.maximum(values, -bound), bound).astype(held_as)


def setup_inputs(seed: int = 0) -> dict:
    key_list = jax.random.split(jax.random.key(seed), 15)
    stored_tiles = scatter_about(key_list[0], (GRID_ROWS, SLOTS, PIX), 1.0, 6.0, ((0, 16), (1, 16)), jnp.float32)
    tile_target = draw_tile_target(jax.random.fold_in(key_list[14], 71), 0)
    tile_mask = with_ends((jax.random.randint(key_list[2], (GRID_ROWS, SLOTS), 0, 4) < 3).astype(jnp.int32), jax.random.fold_in(key_list[2], 1), 0, 1)
    stem_weight = scatter_about(key_list[3], (48, C), 48 ** -0.5, 0.875, (), jnp.float32)
    stem_bias = scatter_about(key_list[4], (C,), 0.5, 3.0, (), jnp.float32)
    depth_weight = scatter_about(key_list[5], (49, C), 49 ** -0.5, 0.875, (), jnp.float32)
    depth_bias = scatter_about(key_list[6], (C,), 1.0, 4.0, (), jnp.float32)
    norm_gain = jnp.clip(1.0 + 0.1 * jax.random.normal(key_list[7], (C,), jnp.float32), 0.5, 1.5)
    norm_bias = scatter_about(key_list[8], (C,), 0.5, 3.0, (), jnp.float32)
    expand_weight = scatter_about(key_list[9], (C, HID), C ** -0.5, 0.625, (), jnp.float32)
    expand_bias = scatter_about(key_list[10], (HID,), 0.5, 3.0, (), jnp.float32)
    shrink_weight = scatter_about(key_list[11], (HID, C), HID ** -0.5, 0.3125, (), jnp.float32)
    shrink_bias = scatter_about(key_list[12], (C,), 0.5, 3.0, (), jnp.float32)
    cotangent = scatter_about(key_list[13], (C, HF, WF), 1.0, 6.0, ((1, 16), (2, 16)), jnp.float32)
    return dict(stored_tiles=stored_tiles, tile_target=tile_target, tile_mask=tile_mask, stem_weight=stem_weight, stem_bias=stem_bias, depth_weight=depth_weight, depth_bias=depth_bias, norm_gain=norm_gain, norm_bias=norm_bias, expand_weight=expand_weight, expand_bias=expand_bias, shrink_weight=shrink_weight, shrink_bias=shrink_bias, cotangent=cotangent)


precise = lax.Precision.HIGHEST
epsilon = 1e-06

def depth_conv(window, kernel, offset):
    height = window.shape[1] - 6
    breadth = window.shape[2] - 6
    result = jnp.broadcast_to(offset[:, None, None], (window.shape[0], height, breadth))
    for a in range(7):
        for b in range(7):
            result = result + kernel[7 * a + b][:, None, None] * window[:, a:a + height, b:b + breadth]
    return result

def kernel_grad(d_depth, window):
    height = d_depth.shape[1]
    breadth = d_depth.shape[2]
    return jnp.stack([lax.optimization_barrier(jnp.sum(d_depth * window[:, a:a + height, b:b + breadth], axis=(1, 2))) for a in range(7) for b in range(7)])

def spread_back(padded_grad, kernel, height, breadth):
    result = jnp.zeros((padded_grad.shape[0], height, breadth), jnp.float32)
    for a in range(7):
        for b in range(7):
            result = result + kernel[7 * a + b][:, None, None] * padded_grad[:, 6 - a:6 - a + height, 6 - b:6 - b + breadth]
    return result

def mix_block(depth_out, features, feat_mask, norm_gain, norm_bias, expand_weight, expand_bias, shrink_weight, shrink_bias):
    centre = lax.optimization_barrier(jnp.mean(depth_out, axis=0, keepdims=True))
    centred = depth_out - centre
    spread = lax.optimization_barrier(jnp.mean(centred * centred, axis=0, keepdims=True))
    normed = centred * lax.rsqrt(spread + epsilon) * norm_gain[:, None, None] + norm_bias[:, None, None]
    hidden = jnp.einsum('cj,chw->jhw', expand_weight, normed, precision=precise) + expand_bias[:, None, None]
    active = jax.nn.gelu(hidden, approximate=False)
    branch = jnp.einsum('jc,jhw->chw', shrink_weight, active, precision=precise) + shrink_bias[:, None, None]
    return feat_mask * (features + branch)

def reference(stored_tiles, tile_target, tile_mask, stem_weight, stem_bias, depth_weight, depth_bias, norm_gain, norm_bias, expand_weight, expand_bias, shrink_weight, shrink_bias, cotangent):
    foreground = tile_mask.astype(jnp.float32)
    pixels = stored_tiles * foreground[:, :, None]
    slot_order = jnp.argsort(tile_target, axis=1).astype(jnp.int32)
    placed = jnp.take_along_axis(pixels, slot_order[:, :, None], axis=1)
    placed_marks = jnp.take_along_axis(foreground, slot_order, axis=1)
    quarter = TS // 4
    tile_grid = placed.reshape(GRID_ROWS, GRID_COLS, TBY, TBX, 3, quarter, 4, quarter, 4)
    patches = tile_grid.transpose(4, 6, 8, 0, 2, 5, 1, 3, 7).reshape(48, HF, WF)
    features = jnp.einsum('kc,khw->chw', stem_weight, patches, precision=precise) + stem_bias[:, None, None]
    tile_marks = placed_marks.reshape(GRID_ROWS, GRID_COLS, TBY, TBX).transpose(0, 2, 1, 3)
    feat_mask = (tile_marks[:, :, None, :, :, None] * jnp.ones((1, 1, quarter, 1, 1, quarter), jnp.float32)).reshape(HF, WF)
    padded = jnp.pad(features, ((0, 0), (3, 3), (3, 3)))

    def row_block(row_index):
        offset = (row_index * CFH).astype(jnp.int32)
        window = lax.dynamic_slice_in_dim(padded, offset, CFH + 6, 1)
        feat_rows = lax.dynamic_slice_in_dim(features, offset, CFH, 1)
        mask_rows = lax.dynamic_slice_in_dim(feat_mask, offset, CFH, 0)
        cot_rows = lax.dynamic_slice_in_dim(cotangent, offset, CFH, 1)
        depth_out = depth_conv(window, depth_weight, depth_bias)

        def local_fn(depth_in, feat_in, gain_in, shift_in, up_in, up_shift, down_in, down_shift):
            return mix_block(depth_in, feat_in, mask_rows, gain_in, shift_in, up_in, up_shift, down_in, down_shift)
        result, pullback = jax.vjp(local_fn, depth_out, feat_rows, norm_gain, norm_bias, expand_weight, expand_bias, shrink_weight, shrink_bias)
        gradient = pullback(cot_rows)
        return (result, gradient[0], gradient[1], gradient[2:], kernel_grad(gradient[0], window))
    rows_out, rows_ddepth, rows_dfeat, rows_params, rows_kernel = lax.map(row_block, jnp.arange(GRID_ROWS, dtype=jnp.int32))
    block_out = rows_out.transpose(1, 0, 2, 3).reshape(C, HF, WF)
    d_depth = rows_ddepth.transpose(1, 0, 2, 3).reshape(C, HF, WF)
    d_resid = rows_dfeat.transpose(1, 0, 2, 3).reshape(C, HF, WF)
    param_grads = [lax.optimization_barrier(jnp.sum(item, axis=0)) for item in rows_params]
    grad_depth_weight = lax.optimization_barrier(jnp.sum(rows_kernel, axis=0))
    grad_depth_bias = lax.optimization_barrier(jnp.sum(d_depth, axis=(1, 2)))
    padded_grad = jnp.pad(d_depth, ((0, 0), (3, 3), (3, 3)))
    d_features = d_resid + spread_back(padded_grad, depth_weight, HF, WF)
    grad_stem_weight = jnp.einsum('khw,chw->kc', patches, d_features, precision=precise)
    grad_stem_bias = lax.optimization_barrier(jnp.sum(d_features, axis=(1, 2)))
    return (block_out, grad_stem_weight, grad_stem_bias, grad_depth_weight, grad_depth_bias, param_grads[0], param_grads[1], param_grads[2], param_grads[3], param_grads[4], param_grads[5])
```

```python
import functools

import jax
import jax.numpy as jnp
from jax import lax
from jax.experimental import pallas as pl
from jax.experimental.pallas import tpu as pltpu
from jax.sharding import PartitionSpec as P

C = 96
HID = 384
NB = C // 8
H = 16
W = 128
EXT = H + 6
KK = 48
f32 = jnp.float32
bf16 = jnp.bfloat16
EPS = 1e-6

NN = (((1,), (0,)), ((), ()))
NT = (((1,), (1,)), ((), ()))


def split(x):
    hi = x.astype(bf16)
    return hi, (x - hi.astype(f32)).astype(bf16)


def dot(a, b, dims=NN):
    return lax.dot_general(a, b, dims, preferred_element_type=f32)


def dot3(a, b, dims=NN):
    return dot(a[0], b[0], dims) + (dot(a[0], b[1], dims) + dot(a[1], b[0], dims))


def lanes(shape=(8, W)):
    return lax.broadcasted_iota(jnp.int32, shape, len(shape) - 1)


def roll(x, by):
    by = by % W
    return x if by == 0 else pltpu.roll(x, by, x.ndim - 1)


TAPS = 49
STEM_B, DEPTH_B, GAIN, NBIAS, SHRINK_B = 49, 50, 51, 52, 53
NCOLS = 56


def block_kernel(
    pat_ref,
    side_ref,
    fm_ref,
    cot_ref,
    cols_ref,
    stem_ref,
    up_hi_ref, up_lo_ref,
    upn_hi_ref, upn_lo_ref,
    dn_hi_ref, dn_lo_ref,
    dnn_hi_ref, dnn_lo_ref,
    out_ref,
    gexp_ref,
    gshr_ref,
    gstem_ref,
    gvec_ref,
    F, S, FS, PB, D, DF, DFS, U, DA, XH, XL, AH, AL, GH, GL, YH, YL, XN, ACC, RS,
):
    gy = lax.axis_index("gy")
    gx = lax.axis_index("gx")
    ny = lax.axis_size("gy")
    nx = lax.axis_size("gx")
    top_ok = (gy > 0).astype(f32)
    bot_ok = (gy < ny - 1).astype(f32)
    lane = lanes()
    pos = lane % 8
    prow = lane // 8
    left_ok = (gx > 0).astype(f32)
    right_ok = (gx < nx - 1).astype(f32)
    col_ok = jnp.where(pos < 3, left_ok, jnp.where(pos < 6, right_ok, 0.0))
    col_ok = jnp.where(prow < 11, col_ok, 0.0)
    ok0 = col_ok * jnp.where(prow < 3, top_ok, 1.0)
    ok1 = col_ok * jnp.where(prow >= 8, bot_ok, 1.0)

    for k in range(5):
        PB[k] = jnp.broadcast_to(cols_ref[:, STEM_B + k : STEM_B + k + 1], (C, W))

    def stem_of(p):
        hi, lo = split(p)
        return dot(stem_ref[...], jnp.concatenate([hi, lo, hi], axis=0))

    def stem_row(i, _):
        ok = jnp.where(i < 3, top_ok, jnp.where(i >= H + 3, bot_ok, 1.0))
        p = jnp.where(ok > 0.0, pat_ref[i], 0.0)
        F[i] = (stem_of(p) + PB[0]) * ok
        return 0

    lax.fori_loop(0, EXT, stem_row, 0)
    for i, ok in enumerate((ok0, ok1)):
        okk = jnp.concatenate([ok] * (KK // 8), axis=0)
        okc = jnp.concatenate([ok] * NB, axis=0)
        p = jnp.where(okk > 0.0, side_ref[i], 0.0)
        FS[i] = (stem_of(p) + PB[0]) * okc
    for r in range(EXT):
        S[r] = roll(FS[r // 11], 125 - (r % 11) * 8)

    def conv_block(cb, _):
        cs = pl.ds(pl.multiple_of(cb * 8, 8), 8)
        wc = cols_ref[cs, :]
        acc = [PB[1, cs, :] for _ in range(H)]
        for b in range(7):
            s = 3 - b
            rolled = []
            for r in range(EXT):
                v = F[r, cs, :]
                if s > 0:
                    v = jnp.where(lane >= W - s, S[r, cs, :], v)
                elif s < 0:
                    v = jnp.where(lane < -s, S[r, cs, :], v)
                rolled.append(roll(v, s))
            for a in range(7):
                w = jnp.broadcast_to(wc[:, 7 * a + b : 7 * a + b + 1], (8, W))
                for h in range(H):
                    acc[h] = acc[h] + w * rolled[h + a]
        for h in range(H):
            D[h, cs, :] = acc[h]
        return 0

    lax.fori_loop(0, NB, conv_block, 0)

    fm = fm_ref[...]
    fmc = jnp.concatenate([fm] * NB, axis=0)
    ones_row = jnp.where(lax.broadcasted_iota(jnp.int32, (16, 2 * W), 0) == 0, 1.0, 0.0)
    XH[C : C + 16, :] = ones_row.astype(bf16)
    XL[C : C + 16, :] = jnp.zeros((16, 2 * W), bf16)
    gexp_ref[...] = jnp.zeros_like(gexp_ref)
    gshr_ref[...] = jnp.zeros_like(gshr_ref)
    ACC[...] = jnp.zeros_like(ACC)
    CH = 16

    def tile(i, _):
        for q in range(2):
            h = 2 * i + q
            qs = slice(q * W, (q + 1) * W)
            x = D[h]
            m = jnp.mean(x, axis=0, keepdims=True)
            xc = x - m
            v = jnp.mean(xc * xc, axis=0, keepdims=True)
            rs = lax.rsqrt(v + EPS)
            xn = xc * rs
            XN[q] = xn
            RS[q] = jnp.broadcast_to(rs, (8, W))
            hi, lo = split(xn * PB[2] + PB[3])
            XH[0:C, qs] = hi
            XL[0:C, qs] = lo
            dy = cot_ref[pl.ds(h, C, stride=H), :] * fmc
            DF[h + 3] = dy
            ACC[3] += dy
            hi, lo = split(dy)
            YH[:, qs] = hi
            YL[:, qs] = lo
        U[...] = dot3((up_hi_ref[...], up_lo_ref[...]), (XH[...], XL[...]))
        DA[...] = dot3((dnn_hi_ref[...], dnn_lo_ref[...]), (YH[...], YL[...]))
        for k in range(HID // CH):
            ks = slice(k * CH, (k + 1) * CH)
            u = U[ks, :]
            z = jnp.abs(u)
            t = 1.0 / (1.0 + (0.3275911 * 0.7071067811865476) * z)
            e = jnp.exp(-0.5 * u * u)
            poly = t * (0.5 * 0.254829592 + t * (0.5 * -0.284496736 + t * (0.5 * 1.421413741 + t * (0.5 * -1.453152027 + t * (0.5 * 1.061405429)))))
            q = poly * e
            phi = jnp.where(u >= 0.0, 1.0 - q, q)
            act = u * phi
            g = phi + (0.3989422804014327 * u) * e
            hi, lo = split(act)
            AH[ks, :] = hi
            AL[ks, :] = lo
            hi, lo = split(DA[ks, :] * g)
            GH[ks, :] = hi
            GL[ks, :] = lo
        a = (AH[...], AL[...])
        g = (GH[...], GL[...])
        y = dot3((dn_hi_ref[...], dn_lo_ref[...]), a)
        for q in range(2):
            h = 2 * i + q
            out_ref[pl.ds(h, C, stride=H), :] = fmc * (F[h + 3] + (y[:, q * W : (q + 1) * W] + PB[4]))
        gshr_ref[...] += dot3((YH[...], YL[...]), a, NT)
        gexp_ref[...] += dot3((XH[...], XL[...]), g, NT)
        dx = dot3((upn_hi_ref[...], upn_lo_ref[...]), g)
        for q in range(2):
            h = 2 * i + q
            d = dx[:, q * W : (q + 1) * W]
            xn = XN[q]
            ACC[0] += d * xn
            ACC[1] += d
            d = d * PB[2]
            m1 = jnp.mean(d, axis=0, keepdims=True)
            m2 = jnp.mean(d * xn, axis=0, keepdims=True)
            d = (d - m1 - xn * m2) * RS[q, 0:1, :]
            D[h] = d
            ACC[2] += d
        return 0

    lax.fori_loop(0, H // 2, tile, 0)

    for r in (0, 1, 2, 19, 20, 21):
        DF[r] = jnp.zeros((C, W), f32)

    def back_block(cb, _):
        cs = pl.ds(pl.multiple_of(cb * 8, 8), 8)
        wc = cols_ref[cs, :]
        dd = [D[h, cs, :] for h in range(H)]
        grads = jnp.zeros((8, W), f32)
        for b in range(7):
            s = 3 - b
            part = [None] * 7
            for r in range(EXT):
                v = F[r, cs, :]
                if s > 0:
                    v = jnp.where(lane >= W - s, S[r, cs, :], v)
                elif s < 0:
                    v = jnp.where(lane < -s, S[r, cs, :], v)
                v = roll(v, s)
                for a in range(7):
                    if 0 <= r - a < H:
                        t = dd[r - a] * v
                        part[a] = t if part[a] is None else part[a] + t
            for a in range(7):
                total = jnp.sum(part[a], axis=1, keepdims=True)
                grads = jnp.where(lane == 7 * a + b, total, grads)
        for k, src in enumerate((2, 0, 1, 3)):
            total = jnp.sum(ACC[src, cs, :], axis=1, keepdims=True)
            grads = jnp.where(lane == DEPTH_B + k, total, grads)

        acc = [DF[r, cs, :] for r in range(EXT)]
        for b in range(7):
            s = b - 3
            rolled = []
            for h in range(H):
                v = dd[h]
                if s > 0:
                    v = jnp.where(lane >= W - s, 0.0, v)
                elif s < 0:
                    v = jnp.where(lane < -s, 0.0, v)
                rolled.append(roll(v, s))
            for a in range(7):
                w = jnp.broadcast_to(wc[:, 7 * a + b : 7 * a + b + 1], (8, W))
                for h in range(H):
                    acc[h + a] = acc[h + a] + w * rolled[h]
        total = None
        for r in range(EXT):
            v = acc[r]
            if r < 3:
                v = v * top_ok
            elif r >= H + 3:
                v = v * bot_ok
            DF[r, cs, :] = v
            total = v if total is None else total + v

        packed = jnp.zeros((8, W), f32)
        for h in range(H):
            packed = jnp.where(prow == h, roll(dd[h], 8 * h + 3), packed)
        packed = jnp.where(pos < 3, roll(packed, -3), jnp.where(pos < 6, roll(packed, 3), 0.0))
        left = pos < 3
        v0 = packed
        v1 = jnp.where(left, jnp.where(pos >= 1, roll(packed, 1), 0.0),
                       jnp.where(pos <= 4, roll(packed, -1), 0.0))
        v2 = jnp.where(left, jnp.where(pos >= 2, roll(packed, 2), 0.0),
                       jnp.where(pos == 3, roll(packed, -2), 0.0))
        o0 = jnp.zeros((8, W), f32)
        o1 = jnp.zeros((8, W), f32)
        for a in range(7):
            t = None
            for k, v in enumerate((v0, v1, v2)):
                w = jnp.where(left, wc[:, 7 * a + k : 7 * a + k + 1], wc[:, 7 * a + 6 - k : 7 * a + 7 - k])
                t = w * v if t is None else t + w * v
            o0 = o0 + jnp.where((prow >= a) & (prow < 11), roll(t, 8 * a), 0.0)
            o1 = o1 + jnp.where(prow < 5 + a, roll(t, 8 * (a - 11)), 0.0)
        o0 = o0 * ok0
        o1 = o1 * ok1
        DFS[0, cs, :] = o0
        DFS[1, cs, :] = o1
        total = jnp.sum(total + (o0 + o1), axis=1, keepdims=True)
        gvec_ref[cs, :] = jnp.where(lane == STEM_B, total, grads)
        return 0

    lax.fori_loop(0, NB, back_block, 0)

    def okpat(p, ok):
        return jnp.where(ok > 0.0, p, 0.0)

    g = None
    for i, ok in enumerate((ok0, ok1)):
        okk = jnp.concatenate([ok] * (KK // 8), axis=0)
        t = dot3(split(okpat(side_ref[i], okk)), split(DFS[i]), NT)
        g = t if g is None else g + t
    gstem_ref[...] = g

    def stem_back(i, _):
        r = 2 * i
        ok = jnp.where(i == 0, top_ok, jnp.where(i == 10, bot_ok, 1.0))
        ok_b = jnp.where(i == 0, top_ok, jnp.where(i == 10, bot_ok, 1.0))
        ok = jnp.where(i == 1, top_ok, ok)
        ok_b = jnp.where(i == 9, bot_ok, ok_b)
        p = jnp.concatenate([okpat(pat_ref[r], ok), okpat(pat_ref[r + 1], ok_b)], axis=1)
        d = jnp.concatenate([DF[r], DF[r + 1]], axis=1)
        gstem_ref[...] += dot3(split(p), split(d), NT)
        return 0

    lax.fori_loop(0, EXT // 2, stem_back, 0)


def block_call(pat, side, fm, cot, params):
    vm = pl.BlockSpec(memory_space=pltpu.VMEM)
    s = jax.ShapeDtypeStruct
    return pl.pallas_call(
        block_kernel,
        out_shape=(
            s((C * H, W), f32), s((C + 16, HID), f32), s((C, HID), f32), s((KK, C), f32), s((C, W), f32),
        ),
        in_specs=[vm] * (4 + len(params)),
        out_specs=[vm] * 5,
        scratch_shapes=[
            pltpu.VMEM((EXT, C, W), f32),
            pltpu.VMEM((EXT, C, W), f32),
            pltpu.VMEM((2, C, W), f32),
            pltpu.VMEM((5, C, W), f32),
            pltpu.VMEM((H, C, W), f32),
            pltpu.VMEM((EXT, C, W), f32),
            pltpu.VMEM((2, C, W), f32),
            pltpu.VMEM((HID, 2 * W), f32),
            pltpu.VMEM((HID, 2 * W), f32),
            pltpu.VMEM((C + 16, 2 * W), bf16),
            pltpu.VMEM((C + 16, 2 * W), bf16),
            pltpu.VMEM((HID, 2 * W), bf16),
            pltpu.VMEM((HID, 2 * W), bf16),
            pltpu.VMEM((HID, 2 * W), bf16),
            pltpu.VMEM((HID, 2 * W), bf16),
            pltpu.VMEM((C, 2 * W), bf16),
            pltpu.VMEM((C, 2 * W), bf16),
            pltpu.VMEM((2, C, W), f32),
            pltpu.VMEM((4, C, W), f32),
            pltpu.VMEM((2, 8, W), f32),
        ],
        compiler_params=pltpu.CompilerParams(vmem_limit_bytes=48 * 1024 * 1024),
        name="block",
    )(pat, side, fm, cot, *params)


def wsplit(x):
    hi = lax.reduce_precision(x, 8, 7)
    return hi.astype(bf16), (x - hi).astype(bf16)


def prepare(stem_weight, stem_bias, depth_weight, depth_bias, norm_gain, norm_bias,
            expand_weight, expand_bias, shrink_weight, shrink_bias):
    cols = jnp.concatenate(
        [depth_weight, stem_bias[None], depth_bias[None], norm_gain[None], norm_bias[None],
         shrink_bias[None], jnp.zeros((NCOLS - 54, C), f32)], axis=0).T
    hi, lo = wsplit(stem_weight.T)
    stem = jnp.concatenate([hi, hi, lo], axis=1)
    up = jnp.concatenate([expand_weight, expand_bias[None], jnp.zeros((15, HID), f32)], axis=0).T
    return (cols, stem, *wsplit(up), *wsplit(expand_weight), *wsplit(shrink_weight.T), *wsplit(shrink_weight))

MESH = pl.DeviceIdType.MESH
CHUNKS = ((0, 4), (4, 8), (8, 12), (12, 16))
INFO = 2


def payload_range(chunk):
    lo, hi = CHUNKS[chunk]
    return (0 if chunk == 0 else INFO + 3 * lo), INFO + 3 * hi


def take(x, index, axis):
    return jnp.take_along_axis(x, index, axis=axis)


NEAR = ((0, -1), (0, 1), (-1, -1), (-1, 1), (1, -1), (1, 1))


def route_kernel(
    tiles_ref,
    target_ref,
    marks_ref,
    pat_ref,
    side_ref,
    fm_ref,
    send, recv, edge, edges, tile_send, tile_recv, row_send, row_recv, edge_send, edge_recv,
):
    gy = lax.axis_index("gy")
    gx = lax.axis_index("gx")
    ny = lax.axis_size("gy")
    nx = lax.axis_size("gx")

    def device(dy, dx):
        return (lax.rem(gy + dy + ny, ny), lax.rem(gx + dx + nx, nx))

    barrier = pltpu.get_barrier_semaphore()
    peers = [(0, 1), (0, -1), (0, 9), (0, -9)] + [(dy, dx) for dy in (-1, 1) for dx in (-1, 0, 1)]
    for dy, dx in peers:
        pl.semaphore_signal(barrier, inc=1, device_id=device(dy, dx), device_id_type=MESH)

    sub = lax.broadcasted_iota(jnp.int32, (8, W), 0)
    lane = lanes()
    row8 = lax.broadcasted_iota(jnp.int32, (8, 8), 0)
    col8 = lax.broadcasted_iota(jnp.int32, (8, 8), 1)
    eye = row8 == col8

    def down_column(row):
        return jnp.sum(jnp.where(eye, row, 0.0), axis=1, keepdims=True)

    codes = jnp.broadcast_to(target_ref[...], (8, 8))
    bucket = ((((codes >> 3) - gx - 1) & 15) >> 3).astype(f32)
    place = (codes & 7).astype(f32)
    mark = jnp.broadcast_to(marks_ref[...], (8, 8)).astype(f32)
    bucket_col = down_column(bucket)
    rank = jnp.sum(jnp.where((bucket_col == bucket) & (row8 < col8), 1.0, 0.0), axis=0, keepdims=True)
    slot_pos = bucket[0:1, :] * 4.0 + rank

    def sources(wanted):
        return jnp.sum(jnp.where(slot_pos == wanted.astype(f32), col8.astype(f32), 0.0), axis=1, keepdims=True)

    order = jnp.broadcast_to(sources(row8), (8, W)).astype(jnp.int32)
    turned = jnp.broadcast_to(sources((row8 + 4) & 7), (8, W)).astype(jnp.int32)
    place_col = jnp.broadcast_to(down_column(place), (8, W))
    mark_col = jnp.broadcast_to(down_column(mark), (8, W))
    low = sub < 4

    def put(q, x0, x1):
        g0 = take(x0, order, 0)
        g1 = take(x1, turned, 0)
        send[0, q] = jnp.where(low, g0, g1)
        send[1, q] = jnp.where(low, g1, g0)

    def tile_copy(bucket_at, chunk):
        lo, hi = payload_range(chunk)
        return pltpu.make_async_remote_copy(
            src_ref=send.at[bucket_at, pl.ds(lo, hi - lo)],
            dst_ref=recv.at[bucket_at, pl.ds(lo, hi - lo)],
            send_sem=tile_send.at[bucket_at, chunk],
            recv_sem=tile_recv.at[bucket_at, chunk],
            device_id=device(0, 1 + 8 * bucket_at),
            device_id_type=MESH,
        )

    put(0, place_col, place_col)
    put(1, mark_col, mark_col)
    for chunk, (lo, hi) in enumerate(CHUNKS):
        for h in range(lo, hi):
            for k in range(3):
                r = k * 32 + h * 2
                x0 = tiles_ref[:, r * W : (r + 1) * W] * mark_col
                x1 = tiles_ref[:, (r + 1) * W : (r + 2) * W] * mark_col
                put(INFO + 3 * h + k, x0, x1)
        if chunk == 0:
            pl.semaphore_wait(barrier, len(peers))
        for bucket_at in range(2):
            tile_copy(bucket_at, chunk).start()

    w16 = lane & 15
    beta = lane >> 4
    for chunk, (lo, hi) in enumerate(CHUNKS):
        for bucket_at in range(2):
            tile_copy(bucket_at, chunk).wait_recv()
        if chunk == 0:
            places = (recv[0, 0], recv[1, 0])
            marks = (recv[0, 1], recv[1, 1])
            first = []
            for p in places:
                g = (beta - p.astype(jnp.int32)) & 7
                first.append((g >> 2) * 64 + w16 * 4 + (g & 3))
            wanted = ((beta - sub) & 7).astype(f32)
            wanted_t = beta.astype(f32)
            found = []
            fm = jnp.zeros((8, W), f32)
            for j, off in ((0, 0), (1, 4)):
                at = jnp.zeros((8, W), f32)
                hit = jnp.zeros((8, W), f32)
                for k in range(4):
                    p = jnp.broadcast_to(places[j][off + k : off + k + 1, :], (8, W))
                    m = jnp.broadcast_to(marks[j][off + k : off + k + 1, :], (8, W))
                    at = jnp.where(p == wanted, float(k), at)
                    hit = jnp.where(p == wanted, 1.0, hit)
                    fm = jnp.where(p == wanted_t, m, fm)
                found.append((at.astype(jnp.int32), hit))
            fm_ref[...] = fm
            in_a = found[0][1] > 0.0
            second = [(found[0][0] + 4 * a, found[1][0] + 4 * (1 - a)) for a in range(2)]
            third = ((sub + beta) & 7) * 16 + w16
        for h in range(lo, hi):
            for k in range(3):
                q = INFO + 3 * h + k
                ya = take(recv[0, q], first[0], 1)
                yb = take(recv[1, q], first[1], 1)
                for a in range(2):
                    v = jnp.where(in_a, take(ya, second[a][0], 0), take(yb, second[a][1], 0))
                    pat_ref[h + 3, pl.ds(16 * k + 8 * a, 8), :] = take(v, third, 1)

    def row_copy(up):
        src, dst, dy = (3, H + 3, -1) if up else (H, 0, 1)
        return pltpu.make_async_remote_copy(
            src_ref=pat_ref.at[pl.ds(src, 3)],
            dst_ref=pat_ref.at[pl.ds(dst, 3)],
            send_sem=row_send.at[int(up)],
            recv_sem=row_recv.at[int(up)],
            device_id=device(dy, 0),
            device_id_type=MESH,
        )

    row_copy(True).start()
    row_copy(False).start()
    prow = lane >> 3
    pos = lane & 7
    for j in range(KK // 8):
        js = pl.ds(8 * j, 8)
        v = jnp.zeros((8, W), f32)
        for h in range(H):
            v = jnp.where(prow == h, roll(pat_ref[h + 3, js, :], 8 * h + 3), v)
        edge[js, :] = v

    def edge_copy(i):
        dy, dx = NEAR[i]
        return pltpu.make_async_remote_copy(
            src_ref=edge,
            dst_ref=edges.at[i],
            send_sem=edge_send.at[i],
            recv_sem=edge_recv.at[i],
            device_id=device(dy, dx),
            device_id_type=MESH,
        )

    for i in range(len(NEAR)):
        edge_copy(i).start()
    for i in range(len(NEAR)):
        edge_copy(i).wait_recv()
    from_left, from_right = edges.at[1], edges.at[0]
    up_left, up_right = edges.at[5], edges.at[4]
    down_left, down_right = edges.at[3], edges.at[2]
    left = pos < 3
    for j in range(KK // 8):
        js = pl.ds(8 * j, 8)
        mid = jnp.where(left, from_left[js, :], from_right[js, :])
        top = jnp.where(left, up_left[js, :], up_right[js, :])
        bottom = jnp.where(left, down_left[js, :], down_right[js, :])
        side_ref[0, js, :] = jnp.where(prow < 3, roll(top, -104), roll(mid, 24))
        side_ref[1, js, :] = jnp.where(prow < 8, roll(mid, -64), roll(bottom, 64))
    row_copy(True).wait_recv()
    row_copy(False).wait_recv()
    for chunk in range(len(CHUNKS)):
        for bucket_at in range(2):
            tile_copy(bucket_at, chunk).wait_send()
    row_copy(True).wait_send()
    row_copy(False).wait_send()
    for i in range(len(NEAR)):
        edge_copy(i).wait_send()


def route_call(tiles, target, marks):
    vm = pl.BlockSpec(memory_space=pltpu.VMEM)
    s = jax.ShapeDtypeStruct
    sem = pltpu.SemaphoreType.DMA
    return pl.pallas_call(
        route_kernel,
        out_shape=(s((EXT, KK, W), f32), s((2, KK, W), f32), s((8, W), f32)),
        in_specs=[vm] * 3,
        out_specs=[vm] * 3,
        scratch_shapes=[
            pltpu.VMEM((2, INFO + 3 * H, 8, W), f32),
            pltpu.VMEM((2, INFO + 3 * H, 8, W), f32),
            pltpu.VMEM((KK, W), f32),
            pltpu.VMEM((len(NEAR), KK, W), f32),
            sem((2, len(CHUNKS))), sem((2, len(CHUNKS))), sem((2,)), sem((2,)),
            sem((len(NEAR),)), sem((len(NEAR),)),
        ],
        compiler_params=pltpu.CompilerParams(
            collective_id=0, has_side_effects=True, vmem_limit_bytes=16 * 1024 * 1024),
        name="route",
    )(tiles, target, marks)

SLOTS = 6


def owner_of(slot):
    return 2 * slot + 1


def reduce_kernel(
    gexp_ref, gshr_ref, gstem_ref, gvec_ref, out_ref,
    mine, rb1, part, rb2, s1, r1, s2, r2, s3, r3, s4, r4,
):
    gy = lax.axis_index("gy")
    gx = lax.axis_index("gx")
    ny = lax.axis_size("gy")
    nx = lax.axis_size("gx")

    def along(axis, i):
        return (lax.rem(gy + i, ny), gx) if axis == 0 else (gy, lax.rem(gx + i, nx))

    barrier = pltpu.get_barrier_semaphore()
    for axis, n in ((0, ny), (1, nx)):
        def greet(i, _, axis=axis):
            pl.semaphore_signal(barrier, inc=1, device_id=along(axis, i), device_id_type=MESH)
            return 0
        lax.fori_loop(1, n, greet, 0)

    blocks = [gexp_ref.at[pl.ds(8 * i, 8), pl.ds(W * j, W)] for j in range(3) for i in range(13)]
    blocks += [gshr_ref.at[pl.ds(8 * i, 8), pl.ds(W * j, W)] for j in range(3) for i in range(12)]
    for v, block in enumerate(blocks):
        mine[v % 16, v // 16] = block[...]
    v = len(blocks)
    zero = jnp.zeros((8, W - C), f32)
    for i in range(KK // 8):
        mine[v % 16, v // 16] = jnp.concatenate([gstem_ref[pl.ds(8 * i, 8), :], zero], axis=1)
        v += 1
    vec = jnp.concatenate([gvec_ref[...], jnp.zeros((W - C, W), f32)], axis=0).T
    for i in range(NCOLS // 8):
        mine[v % 16, v // 16] = vec[8 * i : 8 * i + 8, :]
        v += 1
    while v < 16 * SLOTS:
        mine[v % 16, v // 16] = jnp.zeros((8, W), f32)
        v += 1
    pl.semaphore_wait(barrier, ny + nx - 2)

    def copy1(i):
        to = lax.rem(gy + i, ny)
        return pltpu.make_async_remote_copy(
            src_ref=mine.at[to], dst_ref=rb1.at[i], send_sem=s1.at[i], recv_sem=r1.at[i],
            device_id=(to, gx), device_id_type=MESH)

    lax.fori_loop(1, ny, lambda i, _: (copy1(i).start(), 0)[1], 0)
    rb1[0] = mine[gy]

    def add1(i, acc):
        copy1(i).wait_recv()
        return tuple(a + rb1[i, s] for s, a in enumerate(acc))

    acc = lax.fori_loop(1, ny, add1, tuple(rb1[0, s] for s in range(SLOTS)))
    for s in range(SLOTS):
        part[s] = acc[s]

    def copy2(slot):
        return pltpu.make_async_remote_copy(
            src_ref=part.at[slot], dst_ref=rb2.at[gx], send_sem=s2.at[slot], recv_sem=r2.at[gx],
            device_id=(gy, owner_of(slot)), device_id_type=MESH)

    def got2(i):
        return pltpu.make_async_remote_copy(
            src_ref=part.at[0], dst_ref=rb2.at[i], send_sem=s2.at[0], recv_sem=r2.at[i],
            device_id=(gy, gx), device_id_type=MESH)

    def copy3(slot, i):
        return pltpu.make_async_remote_copy(
            src_ref=out_ref.at[gy, slot], dst_ref=out_ref.at[gy, slot], send_sem=s3.at[i], recv_sem=r3.at[slot],
            device_id=(gy, lax.rem(gx + i, nx)), device_id_type=MESH)

    for slot in range(SLOTS):
        @pl.when(gx != owner_of(slot))
        def _():
            copy2(slot).start()

    for slot in range(SLOTS):
        @pl.when(gx == owner_of(slot))
        def _():
            def add2(i, acc):
                j = lax.rem(gx + i, nx)
                got2(j).wait_recv()
                return acc + rb2[j]

            out_ref[gy, slot] = lax.fori_loop(1, nx, add2, part[slot])
            lax.fori_loop(1, nx, lambda i, _: (copy3(slot, i).start(), 0)[1], 0)

    for slot in range(SLOTS):
        @pl.when(gx != owner_of(slot))
        def _():
            copy3(slot, 1).wait_recv()

    def copy4(i):
        return pltpu.make_async_remote_copy(
            src_ref=out_ref.at[gy], dst_ref=out_ref.at[gy], send_sem=s4.at[i], recv_sem=r4.at[i],
            device_id=(lax.rem(gy + i, ny), gx), device_id_type=MESH)

    def got4(i):
        j = lax.rem(gy - i + ny, ny)
        return pltpu.make_async_remote_copy(
            src_ref=out_ref.at[j], dst_ref=out_ref.at[j], send_sem=s4.at[i], recv_sem=r4.at[i],
            device_id=(gy, gx), device_id_type=MESH)

    lax.fori_loop(1, ny, lambda i, _: (copy4(i).start(), 0)[1], 0)
    lax.fori_loop(1, ny, lambda i, _: (copy1(i).wait_send(), 0)[1], 0)
    for slot in range(SLOTS):
        @pl.when(gx != owner_of(slot))
        def _():
            copy2(slot).wait_send()

        @pl.when(gx == owner_of(slot))
        def _():
            lax.fori_loop(1, nx, lambda i, _: (copy3(slot, i).wait_send(), 0)[1], 0)

    lax.fori_loop(1, ny, lambda i, _: (got4(i).wait_recv(), 0)[1], 0)
    lax.fori_loop(1, ny, lambda i, _: (copy4(i).wait_send(), 0)[1], 0)


def reduce_call(gexp, gshr, gstem, gvec):
    vm = pl.BlockSpec(memory_space=pltpu.VMEM)
    s = jax.ShapeDtypeStruct
    sem = pltpu.SemaphoreType.DMA
    return pl.pallas_call(
        reduce_kernel,
        out_shape=s((16, SLOTS, 8, W), f32),
        in_specs=[vm] * 4,
        out_specs=vm,
        scratch_shapes=[
            pltpu.VMEM((16, SLOTS, 8, W), f32),
            pltpu.VMEM((16, SLOTS, 8, W), f32),
            pltpu.VMEM((SLOTS, 8, W), f32),
            pltpu.VMEM((16, 8, W), f32),
            sem((16,)), sem((16,)), sem((SLOTS,)), sem((16,)),
            sem((16,)), sem((SLOTS,)), sem((16,)), sem((16,)),
        ],
        compiler_params=pltpu.CompilerParams(
            collective_id=1, has_side_effects=True, vmem_limit_bytes=16 * 1024 * 1024),
        name="reduce",
    )(gexp, gshr, gstem, gvec)


def unpack_kernel(
    sum_ref, gstem_ref, gstem_b_ref, gdepth_ref, gdepth_b_ref, ggain_ref, gnbias_ref,
    gexp_ref, gexp_b_ref, gshr_ref, gshr_b_ref,
):
    def at(v):
        return sum_ref[v % 16, v // 16]

    v = 0
    for j in range(3):
        for i in range(12):
            gexp_ref[8 * i : 8 * i + 8, W * j : W * j + W] = at(v)
            v += 1
        gexp_b_ref[:, W * j : W * j + W] = at(v)[0:1, :]
        v += 1
    for j in range(3):
        t = jnp.concatenate([at(v + i) for i in range(12)] + [jnp.zeros((W - C, W), f32)], axis=0)
        v += 12
        gshr_ref[W * j : W * j + W, :] = t.T[:, :C]
    for i in range(KK // 8):
        gstem_ref[8 * i : 8 * i + 8, :] = at(v)[:, :C]
        v += 1
    for i in range(6):
        gdepth_ref[8 * i : 8 * i + 8, :] = at(v)[:, :C]
        v += 1
    last = at(v)[:, :C]
    gdepth_ref[48:49, :] = last[0:1]
    gstem_b_ref[...] = last[1:2]
    gdepth_b_ref[...] = last[2:3]
    ggain_ref[...] = last[3:4]
    gnbias_ref[...] = last[4:5]
    gshr_b_ref[...] = last[5:6]


def unpack_call(total):
    vm = pl.BlockSpec(memory_space=pltpu.VMEM)
    shapes = ((KK, C), (1, C), (TAPS, C), (1, C), (1, C), (1, C), (C, HID), (1, HID), (HID, C), (1, C))
    outs = pl.pallas_call(
        unpack_kernel,
        out_shape=tuple(jax.ShapeDtypeStruct(s, f32) for s in shapes),
        in_specs=[vm],
        out_specs=[vm] * len(shapes),
        name="unpack",
    )(total)
    return tuple(o[0] if o.shape[0] == 1 else o for o in outs)


def local(
    stored_tiles, tile_target, tile_mask,
    stem_weight, stem_bias, depth_weight, depth_bias, norm_gain, norm_bias,
    expand_weight, expand_bias, shrink_weight, shrink_bias, cotangent,
):
    pat, side, fm = route_call(stored_tiles[0], tile_target, tile_mask)
    params = prepare(stem_weight, stem_bias, depth_weight, depth_bias, norm_gain, norm_bias,
                     expand_weight, expand_bias, shrink_weight, shrink_bias)
    out, *grads = block_call(pat, side, fm, cotangent.reshape(C * H, W), params)
    return (out.reshape(C, H, W), *unpack_call(reduce_call(*grads)))


def solution(mesh):
    placed = (P("gy", "gx", None), P("gy", "gx"), P("gy", "gx")) + (P(),) * 10 + (P(None, "gy", "gx"),)
    return jax.shard_map(
        local, mesh=mesh, in_specs=placed,
        out_specs=(P(None, "gy", "gx"),) + (P(),) * 10,
        check_vma=False,
    )
```

```python
import jax
import jax.numpy as jnp
from jax import lax
from jax.experimental import pallas as pl
from jax.experimental.pallas import tpu as pltpu
from jax.sharding import PartitionSpec as P

C = 96
HID = 384
NB = C // 8
H = 16
W = 128
EXT = H + 6
KK = 48
TAPS = 49
PIX = 12288
f32 = jnp.float32
bf16 = jnp.bfloat16
EPS = 1e-6
MESH = pl.DeviceIdType.MESH
DMA = pltpu.SemaphoreType.DMA

NN = (((1,), (0,)), ((), ()))
NT = (((1,), (1,)), ((), ()))


def split(x):
    hi = x.astype(bf16)
    return hi, (x - hi.astype(f32)).astype(bf16)


def dot(a, b, dims=NN):
    return lax.dot_general(a, b, dims, preferred_element_type=f32)


def lanes(shape=(8, W)):
    return lax.broadcasted_iota(jnp.int32, shape, len(shape) - 1)


def roll(x, by):
    by = by % W
    return x if by == 0 else pltpu.roll(x, by, x.ndim - 1)


STEM_B, DEPTH_B, GAIN, NBIAS, SHRINK_B = 49, 50, 51, 52, 53
GROUPS = ((0, 1, 2, 13, 14, 15), (3, 4, 5, 6, 7), (8, 9, 10, 11, 12))
ORDER = tuple(h for group in GROUPS for h in group)
INFO = 2
NEAR = ((0, -1), (0, 1), (-1, -1), (-1, 1), (1, -1), (1, 1))


def payload_range(group):
    before = sum(len(g) for g in GROUPS[:group])
    after = before + len(GROUPS[group])
    return (0 if group == 0 else INFO + 3 * before), INFO + 3 * after


def row_ranges(group):
    rows = GROUPS[group]
    if group == 0:
        return ((rows[0], 3), (rows[3], 3))
    return ((rows[0], len(rows)),)


def take(x, index, axis):
    return jnp.take_along_axis(x, index, axis=axis)


def each(low, high, f):
    def one(i, _):
        f(i)
        return 0
    lax.fori_loop(low, high, one, 0)


XR = C + 16
CH = 16
SLOTS = 96
TAIL = 16
SHIFTS = (0, 1, 2, 4, 5, 6)
STEPS = (3,)

def validity(gy, gx):
    ny = lax.axis_size("gy")
    nx = lax.axis_size("gx")
    lane = lanes()
    pos = lane & 7
    prow = lane >> 3
    top_ok = (gy > 0).astype(f32)
    bot_ok = (gy < ny - 1).astype(f32)
    left_ok = (gx > 0).astype(f32)
    right_ok = (gx < nx - 1).astype(f32)
    col_ok = jnp.where(pos < 3, left_ok, jnp.where(pos < 6, right_ok, 0.0))
    col_ok = jnp.where(prow < 11, col_ok, 0.0)
    ok0 = col_ok * jnp.where(prow < 3, top_ok, 1.0)
    ok1 = col_ok * jnp.where(prow >= 8, bot_ok, 1.0)
    return top_ok, bot_ok, ok0, ok1


def whole_kernel(
    tiles_hbm, target_hbm, marks_hbm, stem_hbm, dw_hbm, sb_hbm, db_hbm, ga_hbm, nb_hbm, ew_hbm, eb_hbm, sw_hbm, hb_hbm, cot_hbm,
    out_hbm, sum_ref, tail_ref,
    pat_ref, side_ref, fm_ref, wb_ref, wbs_ref, pb_ref, stem3_ref, up2_ref, dnn2_ref, dn3_ref, upn3_ref, tiles,
    target, marks, stem_v, dw_v, sb_v, db_v, ga_v, nb_v, ew_v, eb_v, sw_v, hb_v, send, recv, edge, edges,
    edges_mid, ct, cot_ref, in_sem, par_sem, tile_send, tile_recv, row_send, row_recv, edge_send, edge_recv,
    mid_send, mid_recv, cot_sem, out_sem, F, FS, D, DSH, DY, GE, GS, ACC, FHL, FSH, SH, OUT, G, R0, B0, R1, B1,
    R2, TG, TR, TP, TX, DF, DFS, GV, s0, r0, s1, r1, s2, r2, s3, r3, s4, r4, ts1, tr1, ts2, tr2, ts3, tr3, *bufs,
):
    gy = lax.axis_index("gy")
    gx = lax.axis_index("gx")
    ny = lax.axis_size("gy")
    nx = lax.axis_size("gx")

    def device(dy, dx):
        return (lax.rem(gy + dy + ny, ny), lax.rem(gx + dx + nx, nx))

    y_hi, xx, core = gy >> 3, (gy >> 1) & 3, gy & 1
    y_lo, z = gx >> 3, gx & 7
    plane = (y_hi * 2 + y_lo) * 4 + xx

    def at_plane(m, c):
        return ((m >> 3) * 8 + (m & 3) * 2 + c, ((m >> 2) & 1) * 8 + z)

    def at_z(j):
        return (gy, y_lo * 8 + j)

    barrier = pltpu.get_barrier_semaphore()

    def greet(to):
        pl.semaphore_signal(barrier, inc=1, device_id=to, device_id_type=MESH)

    peers = [(0, 1), (0, -1), (0, 9), (0, -9)] + [(dy, dx) for dy in (-1, 1) for dx in (-1, 0, 1)]
    for dy, dx in peers:
        greet(device(dy, dx))
    each(1, 16, lambda i: greet(at_plane((plane + i) & 15, core)))
    each(0, 16, lambda i: greet(at_plane((plane + i) & 15, 1 - core)))
    each(1, 8, lambda i: greet(at_z((z + i) & 7)))
    greetings = len(peers) + 15 + 16 + 7

    params = [
        pltpu.make_async_copy(src, dst, par_sem.at[i])
        for i, (src, dst) in enumerate((
            (target_hbm, target), (marks_hbm, marks), (stem_hbm, stem_v), (dw_hbm, dw_v), (sb_hbm, sb_v),
            (db_hbm, db_v), (ga_hbm, ga_v), (nb_hbm, nb_v), (ew_hbm, ew_v), (eb_hbm, eb_v), (sw_hbm, sw_v),
            (hb_hbm, hb_v)))
    ]
    params[0].start()
    params[1].start()
    loads = []
    for group in range(len(GROUPS)):
        for lo, n in row_ranges(group):
            for k in range(3):
                at = pl.ds(k * 4096 + lo * 256, n * 256)
                loads.append((group, pltpu.make_async_copy(
                    tiles_hbm.at[:, at], tiles.at[:, at], in_sem.at[len(loads)])))
                loads[-1][1].start()
    for copy in params[2:]:
        copy.start()
    cot_copy = pltpu.make_async_copy(cot_hbm, cot_ref, cot_sem)
    cot_copy.start()

    sub = lax.broadcasted_iota(jnp.int32, (8, W), 0)
    lane = lanes()
    row8 = lax.broadcasted_iota(jnp.int32, (8, 8), 0)
    col8 = lax.broadcasted_iota(jnp.int32, (8, 8), 1)
    eye = row8 == col8
    params[0].wait()
    params[1].wait()

    def down_column(row):
        return jnp.sum(jnp.where(eye, row, 0.0), axis=1, keepdims=True)

    codes = jnp.broadcast_to(target[...], (8, 8))
    bucket = ((((codes >> 3) - gx - 1) & 15) >> 3).astype(f32)
    place = (codes & 7).astype(f32)
    mark = jnp.broadcast_to(marks[...], (8, 8)).astype(f32)
    bucket_col = down_column(bucket)
    rank = jnp.sum(jnp.where((bucket_col == bucket) & (row8 < col8), 1.0, 0.0), axis=0, keepdims=True)
    slot_pos = bucket[0:1, :] * 4.0 + rank

    def sources(wanted):
        return jnp.sum(jnp.where(slot_pos == wanted.astype(f32), col8.astype(f32), 0.0), axis=1, keepdims=True)

    order = jnp.broadcast_to(sources(row8), (8, W)).astype(jnp.int32)
    turned = jnp.broadcast_to(sources((row8 + 4) & 7), (8, W)).astype(jnp.int32)
    place_col = jnp.broadcast_to(down_column(place), (8, W))
    mark_col = jnp.broadcast_to(down_column(mark), (8, W))
    low = sub < 4

    def put(q, x0, x1):
        g0 = take(x0, order, 0)
        g1 = take(x1, turned, 0)
        send[0, q] = jnp.where(low, g0, g1)
        send[1, q] = jnp.where(low, g1, g0)

    def tile_copy(bucket_at, group):
        lo, hi = payload_range(group)
        return pltpu.make_async_remote_copy(
            src_ref=send.at[bucket_at, pl.ds(lo, hi - lo)],
            dst_ref=recv.at[bucket_at, pl.ds(lo, hi - lo)],
            send_sem=tile_send.at[bucket_at, group],
            recv_sem=tile_recv.at[bucket_at, group],
            device_id=device(0, 1 + 8 * bucket_at),
            device_id_type=MESH,
        )

    pos = lane & 7
    left = pos < 3

    def prepare():
        src = lax.broadcasted_iota(jnp.int32, (2 * W, W), 0) & (W - 1)
        dst = lax.broadcasted_iota(jnp.int32, (2 * W, W), 1)
        for n, b in enumerate(SHIFTS):
            SH[:, n * W : (n + 1) * W] = jnp.where(src == dst + (b - 3), 1.0, 0.0).astype(bf16)

        for copy in params[2:]:
            copy.wait()
        ct[...] = jnp.zeros_like(ct)
        ct[0:TAPS, 0:C] = dw_v[...]
        for k, ref in enumerate((sb_v, db_v, ga_v, nb_v, hb_v)):
            ct[STEM_B + k : STEM_B + k + 1, 0:C] = ref[...]
        cols = ct[...].T
        ct[...] = cols

        def spread(cb, _):
            cs = pl.ds(pl.multiple_of(cb * 8, 8), 8)
            wc = ct[cs, :]
            for a in range(7):
                taps = []
                for b in range(7):
                    t = 7 * a + b
                    taps.append(jnp.broadcast_to(wc[:, t : t + 1], (8, W)))
                    wb_ref[cb, t] = taps[-1]
                for k in range(3):
                    wbs_ref[cb, 3 * a + k] = jnp.where(left, taps[k], taps[6 - k])
            for k in range(5):
                pb_ref[k, cs, :] = jnp.broadcast_to(wc[:, STEM_B + k : STEM_B + k + 1], (8, W))
            return 0

        lax.fori_loop(0, NB, spread, 0)

        def turned_over(x):
            n = x.shape[0]
            return jnp.concatenate([x, jnp.zeros((W - n, x.shape[1]), f32)], axis=0).T

        stem_pad = jnp.concatenate([stem_v[...], jnp.zeros((KK, W - C), f32)], axis=1)
        hi, lo = split(turned_over(stem_pad)[:C, :KK])
        stem3_ref[:, 0:KK] = hi
        stem3_ref[:, KK : 2 * KK] = hi
        stem3_ref[:, 2 * KK :] = lo
        ew = ew_v[...]
        sw = sw_v[...]
        for src, ref in ((sw, dn3_ref), (ew, upn3_ref)):
            hi, lo = split(src)
            ref[:, 0:HID] = hi
            ref[:, HID : 2 * HID] = hi
            ref[:, 2 * HID :] = lo
        hi, lo = split(turned_over(sw)[:, :C])
        dnn2_ref[0:HID, 0:C] = hi
        dnn2_ref[0:HID, C : 2 * C] = hi
        dnn2_ref[HID:, 0:C] = lo
        dnn2_ref[HID:, C : 2 * C] = jnp.zeros((HID, C), bf16)
        up = jnp.concatenate([ew, eb_v[...], jnp.zeros((W - C - 1, HID), f32)], axis=0).T
        hi, lo = split(up[:, : C + 16])
        up2_ref[0:HID, 0 : C + 16] = hi
        up2_ref[0:HID, C + 16 :] = hi
        up2_ref[HID:, 0 : C + 16] = lo
        up2_ref[HID:, C + 16 :] = jnp.zeros((HID, C + 16), bf16)


    put(0, place_col, place_col)
    put(1, mark_col, mark_col)
    for group, rows in enumerate(GROUPS):
        for at, copy in loads:
            if at == group:
                copy.wait()
        for h in rows:
            for k in range(3):
                r = k * 32 + h * 2
                x0 = tiles[:, r * W : (r + 1) * W] * mark_col
                x1 = tiles[:, (r + 1) * W : (r + 2) * W] * mark_col
                put(INFO + 3 * ORDER.index(h) + k, x0, x1)
        if group > 0:
            for bucket_at in range(2):
                tile_copy(bucket_at, group).start()
            continue
        prepare()
        pl.semaphore_wait(barrier, greetings)
        for bucket_at in range(2):
            tile_copy(bucket_at, group).start()

    w16 = lane & 15
    beta = lane >> 4
    prow = lane >> 3

    def row_copy(up):
        src, dst, dy = (3, H + 3, -1) if up else (H, 0, 1)
        return pltpu.make_async_remote_copy(
            src_ref=pat_ref.at[pl.ds(src, 3)],
            dst_ref=pat_ref.at[pl.ds(dst, 3)],
            send_sem=row_send.at[int(up)],
            recv_sem=row_recv.at[int(up)],
            device_id=device(dy, 0),
            device_id_type=MESH,
        )

    def edge_copy(i):
        dy, dx = NEAR[i]
        return pltpu.make_async_remote_copy(
            src_ref=edge.at[0], dst_ref=edges.at[i], send_sem=edge_send.at[i], recv_sem=edge_recv.at[i],
            device_id=device(dy, dx), device_id_type=MESH)

    def mid_copy(group, i):
        dy, dx = NEAR[i]
        return pltpu.make_async_remote_copy(
            src_ref=edge.at[group], dst_ref=edges_mid.at[group - 1, i],
            send_sem=mid_send.at[group - 1, i], recv_sem=mid_recv.at[group - 1, i],
            device_id=device(dy, dx), device_id_type=MESH)

    for group, rows in enumerate(GROUPS):
        for bucket_at in range(2):
            tile_copy(bucket_at, group).wait_recv()
        if group == 0:
            places = (recv[0, 0], recv[1, 0])
            marks_in = (recv[0, 1], recv[1, 1])
            first = []
            for p in places:
                g = (beta - p.astype(jnp.int32)) & 7
                first.append((g >> 2) * 64 + w16 * 4 + (g & 3))
            wanted = ((beta - sub) & 7).astype(f32)
            wanted_t = beta.astype(f32)
            found = []
            fm = jnp.zeros((8, W), f32)
            for j, off in ((0, 0), (1, 4)):
                at = jnp.zeros((8, W), f32)
                hit = jnp.zeros((8, W), f32)
                for k in range(4):
                    p = jnp.broadcast_to(places[j][off + k : off + k + 1, :], (8, W))
                    m = jnp.broadcast_to(marks_in[j][off + k : off + k + 1, :], (8, W))
                    at = jnp.where(p == wanted, float(k), at)
                    hit = jnp.where(p == wanted, 1.0, hit)
                    fm = jnp.where(p == wanted_t, m, fm)
                found.append((at.astype(jnp.int32), hit))
            fm_ref[...] = fm
            in_a = found[0][1] > 0.0
            second = [(found[0][0] + 4 * a, found[1][0] + 4 * (1 - a)) for a in range(2)]
            third = ((sub + beta) & 7) * 16 + w16
        for h in rows:
            for k in range(3):
                q = INFO + 3 * ORDER.index(h) + k
                ya = take(recv[0, q], first[0], 1)
                yb = take(recv[1, q], first[1], 1)
                for a in range(2):
                    v = jnp.where(in_a, take(ya, second[a][0], 0), take(yb, second[a][1], 0))
                    pat_ref[h + 3, pl.ds(16 * k + 8 * a, 8), :] = take(v, third, 1)
        if group == 0:
            row_copy(True).start()
            row_copy(False).start()
        for j in range(KK // 8):
            js = pl.ds(8 * j, 8)
            v = jnp.zeros((8, W), f32)
            for h in rows:
                v = jnp.where(prow == h, roll(pat_ref[h + 3, js, :], 8 * h + 3), v)
            edge[group, js, :] = v
        if group == 0:
            for i in range(len(NEAR)):
                edge_copy(i).start()
        else:
            for i in range(2):
                mid_copy(group, i).start()

    for i in range(len(NEAR)):
        edge_copy(i).wait_recv()
    for group in (1, 2):
        for i in range(2):
            mid_copy(group, i).wait_recv()
    up_left, up_right = edges.at[5], edges.at[4]
    down_left, down_right = edges.at[3], edges.at[2]
    for j in range(KK // 8):
        js = pl.ds(8 * j, 8)
        from_left = edges[1, js, :] + (edges_mid[0, 1, js, :] + edges_mid[1, 1, js, :])
        from_right = edges[0, js, :] + (edges_mid[0, 0, js, :] + edges_mid[1, 0, js, :])
        mid = jnp.where(left, from_left, from_right)
        top = jnp.where(left, up_left[js, :], up_right[js, :])
        bottom = jnp.where(left, down_left[js, :], down_right[js, :])
        side_ref[0, js, :] = jnp.where(prow < 3, roll(top, -104), roll(mid, 24))
        side_ref[1, js, :] = jnp.where(prow < 8, roll(mid, -64), roll(bottom, 64))
    row_copy(True).wait_recv()
    row_copy(False).wait_recv()
    top_ok, bot_ok, ok0, ok1 = validity(gy, gx)
    def stem_of(p, bias):
        hi, lo = split(p)
        return dot(stem3_ref[...], jnp.concatenate([hi, lo, hi], axis=0)) + bias

    bias2 = jnp.concatenate([pb_ref[0], pb_ref[0]], axis=1)

    def row_ok(r):
        return top_ok if r < 3 else bot_ok if r >= H + 3 else None

    for r in range(0, EXT, 2):
        parts = []
        for q in range(2):
            ok = row_ok(r + q)
            p = pat_ref[r + q]
            parts.append(p if ok is None else jnp.where(ok > 0.0, p, 0.0))
        y = stem_of(jnp.concatenate(parts, axis=1), bias2)
        for q in range(2):
            ok = row_ok(r + q)
            v = y[:, q * W : (q + 1) * W]
            if ok is not None:
                v = v * ok
            F[r + q] = v
            hi, lo = split(v)
            FHL[(r + q) * C : (r + q + 1) * C, 0:W] = hi
            FHL[(r + q) * C : (r + q + 1) * C, W:] = lo
    parts = []
    for i, ok in enumerate((ok0, ok1)):
        okk = jnp.concatenate([ok] * (KK // 8), axis=0)
        parts.append(jnp.where(okk > 0.0, side_ref[i], 0.0))
    y = stem_of(jnp.concatenate(parts, axis=1), bias2)
    for i, ok in enumerate((ok0, ok1)):
        FS[i] = y[:, i * W : (i + 1) * W] * jnp.concatenate([ok] * NB, axis=0)

    def shift_rows(rows, count, put):
        for n in range(3):
            def some(i, _, n=n):
                rs = pl.ds(pl.multiple_of(i * rows, rows), rows)
                y = dot(FHL[rs, :], SH[:, 2 * n * W : (2 * n + 2) * W])
                put(2 * n, rs, y[:, :W])
                put(2 * n + 1, rs, y[:, W:])
                return 0
            lax.fori_loop(0, count, some, 0)

    def put_features(n, rs, y):
        FSH[n, rs, :] = y

    shift_rows(4 * C, 5, put_features)
    for n in range(3):
        rs = slice(20 * C, 22 * C)
        y = dot(FHL[rs, :], SH[:, 2 * n * W : (2 * n + 2) * W])
        FSH[2 * n, rs, :] = y[:, :W]
        FSH[2 * n + 1, rs, :] = y[:, W:]

    edge_lane = (lane < 3) | (lane >= W - 3)

    def conv_block(cb, _):
        cs = pl.ds(pl.multiple_of(cb * 8, 8), 8)
        part = [None] * 3
        fs0 = FS[0, cs, :]
        fs1 = FS[1, cs, :]
        for a in range(7):
            win = jnp.where(prow < 11 - a, roll(fs0, -8 * a), roll(fs1, 8 * (11 - a)))
            for k in range(3):
                t = wbs_ref[cb, 3 * a + k] * win
                part[k] = t if part[k] is None else part[k] + t
        q = part[0]
        for k in (1, 2):
            q = q + jnp.where(left, jnp.where(pos < 3 - k, roll(part[k], -k), 0.0),
                              jnp.where((pos >= 3 + k) & (pos < 6), roll(part[k], k), 0.0))
        q = jnp.where(left, roll(q, -3), roll(q, 3))
        bias = pb_ref[1, cs, :]
        acc = [bias + jnp.where(edge_lane, roll(q, 125 - 8 * h), 0.0) for h in range(H)]
        for b in range(7):
            if b == 3:
                rows = [F[r, cs, :] for r in range(EXT)]
            else:
                rows = [FSH[SHIFTS.index(b), pl.ds(pl.multiple_of(r * C + cb * 8, 8), 8), :] for r in range(EXT)]
            for a in range(7):
                w = wb_ref[cb, 7 * a + b]
                for h in range(H):
                    acc[h] = acc[h] + w * rows[h + a]
        for h in range(H):
            D[h, cs, :] = acc[h]
        return 0

    lax.fori_loop(0, NB, conv_block, 0)

    fmc = jnp.concatenate([fm_ref[...]] * NB, axis=0)
    ones_row = jnp.where(lax.broadcasted_iota(jnp.int32, (16, 2 * W), 0) == 0, 1.0, 0.0)
    lanesets = [bufs[: len(bufs) // 2], bufs[len(bufs) // 2 :]]
    for XHL, *_ in lanesets:
        XHL[C:XR, :] = ones_row.astype(bf16)
        XHL[XR + C :, :] = jnp.zeros((16, 2 * W), bf16)
    GE[...] = jnp.zeros_like(GE)
    GS[...] = jnp.zeros_like(GS)
    ACC[...] = jnp.zeros_like(ACC)

    def stage_a(i, buf):
        XHL, YHL, U, DA, AHL, GHL, XN, RS = buf
        for q in range(2):
            h = 2 * i + q
            qs = slice(q * W, (q + 1) * W)
            x = D[h]
            m = jnp.mean(x, axis=0, keepdims=True)
            xc = x - m
            v = jnp.mean(xc * xc, axis=0, keepdims=True)
            rs = lax.rsqrt(v + EPS)
            xn = xc * rs
            XN[q] = xn
            RS[q] = jnp.broadcast_to(rs, (8, W))
            hi, lo = split(xn * pb_ref[2] + pb_ref[3])
            XHL[0:C, qs] = hi
            XHL[XR : XR + C, qs] = lo
            dy = cot_ref[pl.ds(h, C, stride=H), :] * fmc
            DY[h] = dy
            ACC[3] += dy
            hi, lo = split(dy)
            YHL[0:C, qs] = hi
            YHL[C:, qs] = lo
        t = dot(up2_ref[...], XHL[...])
        U[...] = t[:HID] + t[HID:]
        t = dot(dnn2_ref[...], YHL[...])
        DA[...] = t[:HID] + t[HID:]

    def stage_b(buf):
        XHL, YHL, U, DA, AHL, GHL, XN, RS = buf
        for k in range(HID // CH):
            ks = slice(k * CH, (k + 1) * CH)
            kl = slice(HID + k * CH, HID + (k + 1) * CH)
            u = U[ks, :]
            t = 1.0 / (1.0 + (0.3275911 * 0.7071067811865476) * jnp.abs(u))
            e = jnp.exp(-0.5 * (u * u))
            poly = t * (0.5 * 0.254829592 + t * (0.5 * -0.284496736 + t * (0.5 * 1.421413741 + t * (0.5 * -1.453152027 + t * (0.5 * 1.061405429)))))
            q = poly * e
            phi = jnp.where(u >= 0.0, 1.0 - q, q)
            g = phi + (0.3989422804014327 * u) * e
            hi, lo = split(u * phi)
            AHL[ks, :] = hi
            AHL[kl, :] = lo
            hi, lo = split(DA[ks, :] * g)
            GHL[ks, :] = hi
            GHL[kl, :] = lo

    def stage_c(i, buf):
        XHL, YHL, U, DA, AHL, GHL, XN, RS = buf
        y = dot(dn3_ref[:, : 2 * HID], AHL[...]) + dot(dn3_ref[:, 2 * HID :], AHL[0:HID, :])
        for q in range(2):
            h = 2 * i + q
            OUT[pl.ds(h, C, stride=H), :] = fmc * (F[h + 3] + (y[:, q * W : (q + 1) * W] + pb_ref[4]))
        t = dot(YHL[...], AHL[0:HID, :], NT)
        GS[...] += t[:C] + (t[C:] + dot(YHL[0:C, :], AHL[HID:, :], NT))
        t = dot(XHL[...], GHL[0:HID, :], NT)
        GE[...] += t[:XR] + (t[XR:] + dot(XHL[0:XR, :], GHL[HID:, :], NT))
        dx = dot(upn3_ref[:, : 2 * HID], GHL[...]) + dot(upn3_ref[:, 2 * HID :], GHL[0:HID, :])
        for q in range(2):
            h = 2 * i + q
            d = dx[:, q * W : (q + 1) * W]
            xn = XN[q]
            ACC[0] += d * xn
            ACC[1] += d
            d = d * pb_ref[2]
            m1 = jnp.mean(d, axis=0, keepdims=True)
            m2 = jnp.mean(d * xn, axis=0, keepdims=True)
            d = (d - m1 - xn * m2) * RS[q, 0:1, :]
            D[h] = d
            ACC[2] += d
            hi, lo = split(d)
            hs = pl.ds(pl.multiple_of(h * C, C), C)
            FHL[hs, 0:W] = hi
            FHL[hs, W:] = lo

    def tiles(i, _):
        b0, b1 = lanesets
        stage_a(2 * i, b0)
        stage_a(2 * i + 1, b1)
        stage_b(b0)
        stage_c(2 * i, b0)
        stage_b(b1)
        stage_c(2 * i + 1, b1)
        return 0

    cot_copy.wait()
    lax.fori_loop(0, H // 4, tiles, 0)
    out_copy = pltpu.make_async_copy(OUT, out_hbm, out_sem)
    out_copy.start()

    def put_gradient(n, rs, y):
        DSH[n, rs, :] = y

    def shift_gradient():
        shift_rows(4 * C, 4, put_gradient)

    def slot(v):
        return v // 48, v % 48 // 3, v % 3

    v = 0
    for j in range(3):
        for i in range(13):
            G[slot(v)] = GE[8 * i : 8 * i + 8, W * j : W * j + W]
            v += 1
    for j in range(3):
        for i in range(12):
            G[slot(v)] = GS[8 * i : 8 * i + 8, W * j : W * j + W]
            v += 1
    while v < SLOTS:
        G[slot(v)] = jnp.zeros((8, W), f32)
        v += 1

    def rdma(src, dst, send, recv, to):
        return pltpu.make_async_remote_copy(
            src_ref=src, dst_ref=dst, send_sem=send, recv_sem=recv, device_id=to, device_id_type=MESH)

    sibling = (gy + 1 - 2 * core, gx)

    def c0():
        return rdma(G.at[1 - core], R0, s0, r0, sibling)

    def c1(i):
        m = (plane + i) & 15
        return rdma(B0.at[m], R1.at[i], s1.at[i], r1.at[i], at_plane(m, core))

    def c2(i):
        return rdma(B1, R2.at[z], s2.at[i], r2.at[i], at_z((z + i) & 7))

    def g2(i):
        j = (z - i) & 7
        return rdma(B1, R2.at[j], s2.at[i], r2.at[i], at_z(j))

    def c3(i):
        ref = sum_ref.at[core, plane]
        return rdma(ref, ref, s3.at[i], r3.at[i], at_plane((plane + i) & 15, core))

    def g3(i):
        m = (plane - i) & 15
        ref = sum_ref.at[core, m]
        return rdma(ref, ref, s3.at[i], r3.at[i], at_plane(m, core))

    def c4():
        ref = sum_ref.at[core]
        return rdma(ref, ref, s4, r4, sibling)

    def g4():
        ref = sum_ref.at[1 - core]
        return rdma(ref, ref, s4, r4, sibling)

    def step(k):
        if k == 0:
            c0().start()
        elif k == 1:
            c0().wait_recv()
            B0[...] = G[core] + R0[...]
            each(1, 16, lambda i: c1(i).start())
        elif k == 2:
            each(1, 16, lambda i: c1(i).wait_recv())
            acc = B0[plane]
            for i in range(1, 16):
                acc = acc + R1[i]
            B1[...] = acc
            R2[z] = acc
            each(1, 8, lambda i: c2(i).start())
        elif k == 3:
            each(1, 8, lambda i: g2(i).wait_recv())
            acc = R2[0]
            for j in range(1, 8):
                acc = acc + R2[j]
            sum_ref[core, plane] = acc
            each(1, 16, lambda i: c3(i).start())
        elif k == 4:
            each(1, 16, lambda i: g3(i).wait_recv())
            c4().start()
        else:
            g4().wait_recv()
            c0().wait_send()
            each(1, 16, lambda i: c1(i).wait_send())
            each(1, 8, lambda i: c2(i).wait_send())
            each(1, 16, lambda i: c3(i).wait_send())
            c4().wait_send()

    right = (pos >= 3) & (pos < 6)

    def back_block(cb, _):
        for k, when in enumerate(STEPS):
            @pl.when(cb == when)
            def _(k=k):
                step(k + 1)

        cs = pl.ds(pl.multiple_of(cb * 8, 8), 8)
        packed = jnp.zeros((8, W), f32)
        for h in range(H):
            packed = jnp.where(prow == h, roll(D[h, cs, :], 8 * h + 3), packed)
        packed = jnp.where(left, roll(packed, -3), jnp.where(right, roll(packed, 3), 0.0))
        vs = [packed]
        for k in (1, 2):
            vs.append(jnp.where(left, jnp.where(pos >= k, roll(packed, k), 0.0),
                                jnp.where(right & (pos < 6 - k), roll(packed, -k), 0.0)))
        fs0 = FS[0, cs, :]
        fs1 = FS[1, cs, :]
        o0 = jnp.zeros((8, W), f32)
        o1 = jnp.zeros((8, W), f32)
        spill = {}
        for a in range(7):
            win = jnp.where(prow < 11 - a, roll(fs0, -8 * a), roll(fs1, 8 * (11 - a)))
            t = None
            for k in range(3):
                w = wbs_ref[cb, 3 * a + k]
                t = w * vs[k] if t is None else t + w * vs[k]
                x = vs[k] * win
                spill[a, k] = jnp.where(left, x, 0.0)
                spill[a, 6 - k] = jnp.where(left, 0.0, x)
            o0 = o0 + jnp.where((prow >= a) & (prow < 11), roll(t, 8 * a), 0.0)
            o1 = o1 + jnp.where(prow < 5 + a, roll(t, 8 * (a - 11)), 0.0)
        o0 = o0 * ok0
        o1 = o1 * ok1
        DFS[0, cs, :] = o0
        DFS[1, cs, :] = o1

        def gradient_rows(b):
            if b == 3:
                return [D[h, cs, :] for h in range(H)]
            n = SHIFTS.index(6 - b)
            return [DSH[n, pl.ds(pl.multiple_of(h * C + cb * 8, 8), 8), :] for h in range(H)]

        grads = jnp.zeros((8, W), f32)
        rows = [F[r, cs, :] for r in range(EXT)]
        for b in range(7):
            dd = gradient_rows(b)
            for a in range(7):
                part = spill.get((a, b))
                for h in range(H):
                    t = dd[h] * rows[h + a]
                    part = t if part is None else part + t
                total = jnp.sum(part, axis=1, keepdims=True)
                grads = jnp.where(lane == 7 * a + b, total, grads)
        acc = [DY[r - 3, cs, :] if 3 <= r < H + 3 else None for r in range(EXT)]
        for b in range(7):
            dd = gradient_rows(b)
            for a in range(7):
                w = wb_ref[cb, 7 * a + b]
                for h in range(H):
                    t = w * dd[h]
                    acc[h + a] = t if acc[h + a] is None else acc[h + a] + t
        for k, src in enumerate((2, 0, 1, 3)):
            total = jnp.sum(ACC[src, cs, :], axis=1, keepdims=True)
            grads = jnp.where(lane == DEPTH_B + k, total, grads)
        total = o0 + o1
        for r in range(EXT):
            t = acc[r]
            if r < 3:
                t = t * top_ok
            elif r >= H + 3:
                t = t * bot_ok
            DF[r, cs, :] = t
            total = total + t
        total = jnp.sum(total, axis=1, keepdims=True)
        GV[cs, :] = jnp.where(lane == STEM_B, total, grads)
        return 0

    step(0)
    shift_gradient()
    lax.fori_loop(0, NB, back_block, 0)
    step(len(STEPS) + 1)

    def rows2(p0, p1, d0, d1):
        ph, plo = split(jnp.concatenate([p0, p1], axis=1))
        dh, dlo = split(jnp.concatenate([d0, d1], axis=1))
        t = dot(jnp.concatenate([ph, plo], axis=0), dh, NT)
        return t[:KK] + (t[KK:] + dot(ph, dlo, NT))

    def okpat(p, ok):
        return p if ok is None else jnp.where(ok > 0.0, p, 0.0)

    def row_ok(r):
        return top_ok if r < 3 else bot_ok if r >= H + 3 else None

    okk = [jnp.concatenate([ok] * (KK // 8), axis=0) for ok in (ok0, ok1)]
    gstem = rows2(okpat(side_ref[0], okk[0]), okpat(side_ref[1], okk[1]), DFS[0], DFS[1])
    for r in range(0, EXT, 2):
        gstem = gstem + rows2(
            okpat(pat_ref[r], row_ok(r)), okpat(pat_ref[r + 1], row_ok(r + 1)), DF[r], DF[r + 1])

    zero = jnp.zeros((KK, W - C), f32)
    gs = jnp.concatenate([gstem, zero], axis=1)
    vec = jnp.concatenate([GV[...], jnp.zeros((W - C, W), f32)], axis=0).T
    tail = [gs[8 * i : 8 * i + 8, :] for i in range(6)] + [vec[8 * i : 8 * i + 8, :] for i in range(7)]
    for i, v in enumerate(tail):
        TG[i] = v
    for i in range(len(tail), TAIL):
        TG[i] = jnp.zeros((8, W), f32)

    def owner(v):
        return at_plane(v, v & 1)

    mine = (plane & 1) == core

    def t1(v):
        return rdma(TG.at[v], TR.at[plane, core], ts1.at[v], tr1.at[plane, core], owner(v))

    def w1(m, c):
        return rdma(TP, TR.at[m, c], ts1.at[0], tr1.at[m, c], at_plane(m, c))

    def t2(i):
        return rdma(TP, TX.at[z], ts2.at[i], tr2.at[i], at_z((z + i) & 7))

    def w2(i):
        j = (z - i) & 7
        return rdma(TP, TX.at[j], ts2.at[i], tr2.at[i], at_z(j))

    def t3(m, c):
        ref = tail_ref.at[plane]
        return rdma(ref, ref, ts3.at[m, c], tr3.at[plane], at_plane(m, c))

    def w3(v):
        ref = tail_ref.at[v]
        return rdma(ref, ref, ts3.at[0, 0], tr3.at[v], owner(v))

    def others(f):
        def one(i):
            m, c = i >> 1, i & 1
            @pl.when((m != plane) | (c != core))
            def _():
                f(m, c)
        each(0, 32, one)

    def foreign(f):
        def one(v):
            @pl.when((v != plane) | ((v & 1) != core))
            def _():
                f(v)
        each(0, TAIL, one)

    foreign(lambda v: t1(v).start())

    @pl.when(mine)
    def _():
        TR[plane, core] = TG[plane]
        others(lambda m, c: w1(m, c).wait_recv())
        acc = TR[0, 0]
        for i in range(1, 32):
            acc = acc + TR[i >> 1, i & 1]
        TP[...] = acc
        TX[z] = acc
        each(1, 8, lambda i: t2(i).start())

    step(len(STEPS) + 2)

    @pl.when(mine)
    def _():
        each(1, 8, lambda i: w2(i).wait_recv())
        acc = TX[0]
        for j in range(1, 8):
            acc = acc + TX[j]
        tail_ref[plane] = acc
        others(lambda m, c: t3(m, c).start())

    step(len(STEPS) + 3)
    foreign(lambda v: t1(v).wait_send())
    step(len(STEPS) + 4)
    foreign(lambda v: w3(v).wait_recv())

    @pl.when(mine)
    def _():
        each(1, 8, lambda i: t2(i).wait_send())
        others(lambda m, c: t3(m, c).wait_send())

    out_copy.wait()
    for group in range(len(GROUPS)):
        for bucket_at in range(2):
            tile_copy(bucket_at, group).wait_send()
    row_copy(True).wait_send()
    row_copy(False).wait_send()
    for i in range(len(NEAR)):
        edge_copy(i).wait_send()
    for group in (1, 2):
        for i in range(2):
            mid_copy(group, i).wait_send()


def whole_call(*args):
    vm = pl.BlockSpec(memory_space=pltpu.VMEM)
    hbm = pl.BlockSpec(memory_space=pltpu.HBM)
    s = jax.ShapeDtypeStruct
    n_send = INFO + 3 * H
    near = len(NEAR)

    def v(*shape, dtype=f32):
        return pltpu.VMEM(shape, dtype)

    buf = [
        v(2 * XR, 2 * W, dtype=bf16), v(2 * C, 2 * W, dtype=bf16), v(HID, 2 * W), v(HID, 2 * W),
        v(2 * HID, 2 * W, dtype=bf16), v(2 * HID, 2 * W, dtype=bf16), v(2, C, W), v(2, 8, W),
    ]
    return pl.pallas_call(
        whole_kernel,
        out_shape=(s((C * H, W), f32), s((2, 16, 3, 8, W), f32), s((TAIL, 8, W), f32)),
        in_specs=[hbm] * 14,
        out_specs=[hbm, vm, vm],
        scratch_shapes=[
            v(EXT, KK, W), v(2, KK, W), v(8, W), v(NB, TAPS, 8, W), v(NB, 21, 8, W), v(5, C, W),
            v(C, 3 * KK, dtype=bf16), v(2 * HID, 2 * XR, dtype=bf16), v(2 * HID, 2 * C, dtype=bf16),
            v(C, 3 * HID, dtype=bf16), v(C, 3 * HID, dtype=bf16),
            v(8, PIX), v(1, 8, dtype=jnp.int32), v(1, 8, dtype=jnp.int32),
            v(KK, C), v(TAPS, C), v(1, C), v(1, C), v(1, C), v(1, C), v(C, HID), v(1, HID), v(C, HID), v(1, C),
            v(2, n_send, 8, W), v(2, n_send, 8, W), v(3, KK, W), v(near, KK, W), v(2, 2, KK, W), v(W, W), v(C * H, W),
            DMA((12,)), DMA((12,)), DMA((2, 3)), DMA((2, 3)), DMA((2,)), DMA((2,)),
            DMA((near,)), DMA((near,)), DMA((2, 2)), DMA((2, 2)), DMA(()), DMA(()),
            v(EXT, C, W), v(2, C, W), v(H, C, W), v(6, H * C, W), v(H, C, W), v(XR, HID), v(C, HID), v(4, C, W),
            v(EXT * C, 2 * W, dtype=bf16), v(6, EXT * C, W), v(2 * W, 6 * W, dtype=bf16), v(C * H, W),
            v(2, 16, 3, 8, W), v(16, 3, 8, W), v(16, 3, 8, W), v(16, 3, 8, W), v(3, 8, W), v(8, 3, 8, W),
            v(TAIL, 8, W), v(16, 2, 8, W), v(8, W), v(8, 8, W), v(EXT, C, W), v(2, C, W), v(C, W),
            DMA(()), DMA(()), DMA((16,)), DMA((16,)), DMA((8,)), DMA((8,)), DMA((16,)), DMA((16,)), DMA(()), DMA(()),
            DMA((TAIL,)), DMA((16, 2)), DMA((8,)), DMA((8,)), DMA((16, 2)), DMA((TAIL,)),
            *buf, *buf,
        ],
        compiler_params=pltpu.CompilerParams(
            collective_id=0, has_side_effects=True, vmem_limit_bytes=56 * 1024 * 1024),
        name="whole",
    )(*args)


def unpack_kernel(
    sum_ref, tail_ref, block_hbm, out_hbm, gstem_ref, gstem_b_ref, gdepth_ref, gdepth_b_ref, ggain_ref, gnbias_ref,
    gexp_ref, gexp_b_ref, gshr_ref, gshr_b_ref, held, sem,
):
    into = pltpu.make_async_copy(block_hbm, held, sem.at[0])
    into.start()

    def at(v):
        return sum_ref[v // 48, v % 48 // 3, v % 3]

    v = 0
    for j in range(3):
        for i in range(12):
            gexp_ref[8 * i : 8 * i + 8, W * j : W * j + W] = at(v)
            v += 1
        gexp_b_ref[:, W * j : W * j + W] = at(v)[0:1, :]
        v += 1
    for j in range(3):
        for i in range(12):
            gshr_ref[8 * i : 8 * i + 8, W * j : W * j + W] = at(v)
            v += 1
    into.wait()
    back = pltpu.make_async_copy(held, out_hbm, sem.at[1])
    back.start()
    for i in range(6):
        gstem_ref[8 * i : 8 * i + 8, :] = tail_ref[i][:, :C]
        gdepth_ref[8 * i : 8 * i + 8, :] = tail_ref[6 + i][:, :C]
    last = tail_ref[12][:, :C]
    gdepth_ref[48:49, :] = last[0:1]
    for k, ref in enumerate((gstem_b_ref, gdepth_b_ref, ggain_ref, gnbias_ref, gshr_b_ref)):
        ref[...] = last[k + 1 : k + 2]
    back.wait()


def unpack_call(block, total, tail):
    vm = pl.BlockSpec(memory_space=pltpu.VMEM)
    hbm = pl.BlockSpec(memory_space=pltpu.HBM)
    shapes = ((KK, C), (1, C), (TAPS, C), (1, C), (1, C), (1, C), (C, HID), (1, HID), (C, HID), (1, C))
    return pl.pallas_call(
        unpack_kernel,
        out_shape=tuple(jax.ShapeDtypeStruct(s, f32) for s in ((C * H, W),) + shapes),
        in_specs=[vm, vm, hbm],
        out_specs=[hbm] + [vm] * len(shapes),
        scratch_shapes=[pltpu.VMEM((C * H, W), f32), DMA((2,))],
        compiler_params=pltpu.CompilerParams(vmem_limit_bytes=56 * 1024 * 1024),
        name="unpack",
    )(total, tail, block)


def local(
    stored_tiles, tile_target, tile_mask,
    stem_weight, stem_bias, depth_weight, depth_bias, norm_gain, norm_bias,
    expand_weight, expand_bias, shrink_weight, shrink_bias, cotangent,
):
    def row(v):
        return v.reshape(1, -1)

    block, total, tail = whole_call(
        stored_tiles[0], tile_target, tile_mask, stem_weight, depth_weight, row(stem_bias), row(depth_bias),
        row(norm_gain), row(norm_bias), expand_weight, row(expand_bias), shrink_weight.T, row(shrink_bias),
        cotangent.reshape(C * H, W))
    out, gs, gsb, gd, gdb, gg, gn, ge, geb, gh, ghb = unpack_call(block, total, tail)
    return (
        out.reshape(C, H, W), gs, gsb[0], gd, gdb[0], gg[0], gn[0], ge, geb[0], gh.T, ghb[0],
    )


def solution(mesh):
    placed = (P("gy", "gx", None), P("gy", "gx"), P("gy", "gx")) + (P(),) * 10 + (P(None, "gy", "gx"),)
    return jax.shard_map(
        local, mesh=mesh, in_specs=placed,
        out_specs=(P(None, "gy", "gx"),) + (P(),) * 10,
        check_vma=False,
    )
```

```python
import jax
import jax.numpy as jnp
from jax import lax
from jax.experimental import pallas as pl
from jax.experimental.pallas import tpu as pltpu
from jax.sharding import PartitionSpec as P

C = 96
HID = 384
NB = C // 8
H = 16
W = 128
EXT = H + 6
KK = 48
TAPS = 49
PIX = 12288
f32 = jnp.float32
bf16 = jnp.bfloat16
EPS = 1e-6
MESH = pl.DeviceIdType.MESH
DMA = pltpu.SemaphoreType.DMA

NN = (((1,), (0,)), ((), ()))
NT = (((1,), (1,)), ((), ()))


def split(x):
    hi = x.astype(bf16)
    return hi, (x - hi.astype(f32)).astype(bf16)


def dot(a, b, dims=NN):
    return lax.dot_general(a, b, dims, preferred_element_type=f32)


def lanes(shape=(8, W)):
    return lax.broadcasted_iota(jnp.int32, shape, len(shape) - 1)


def roll(x, by):
    by = by % W
    return x if by == 0 else pltpu.roll(x, by, x.ndim - 1)


STEM_B, DEPTH_B, GAIN, NBIAS, SHRINK_B = 49, 50, 51, 52, 53
GROUPS = ((0, 1, 2, 13, 14, 15), (3, 4, 5, 6, 7), (8, 9, 10, 11, 12))
ORDER = tuple(h for group in GROUPS for h in group)
INFO = 2
NEAR = ((0, -1), (0, 1), (-1, -1), (-1, 1), (1, -1), (1, 1))


def payload_range(group):
    before = sum(len(g) for g in GROUPS[:group])
    after = before + len(GROUPS[group])
    return (0 if group == 0 else INFO + 3 * before), INFO + 3 * after


def row_ranges(group):
    rows = GROUPS[group]
    if group == 0:
        return ((rows[0], 3), (rows[3], 3))
    return ((rows[0], len(rows)),)


def take(x, index, axis):
    return jnp.take_along_axis(x, index, axis=axis)


def each(low, high, f):
    def one(i, _):
        f(i)
        return 0
    lax.fori_loop(low, high, one, 0)


XR = W
CH = 16
SLOTS = 96
TAIL = 16
SHIFTS = (0, 1, 2, 4, 5, 6)
STEPS = (3,)

def validity(gy, gx):
    ny = lax.axis_size("gy")
    nx = lax.axis_size("gx")
    lane = lanes()
    pos = lane & 7
    prow = lane >> 3
    top_ok = (gy > 0).astype(f32)
    bot_ok = (gy < ny - 1).astype(f32)
    left_ok = (gx > 0).astype(f32)
    right_ok = (gx < nx - 1).astype(f32)
    col_ok = jnp.where(pos < 3, left_ok, jnp.where(pos < 6, right_ok, 0.0))
    col_ok = jnp.where(prow < 11, col_ok, 0.0)
    ok0 = col_ok * jnp.where(prow < 3, top_ok, 1.0)
    ok1 = col_ok * jnp.where(prow >= 8, bot_ok, 1.0)
    return top_ok, bot_ok, ok0, ok1


def whole_kernel(
    tiles_hbm, target_hbm, marks_hbm, stem_hbm, dw_hbm, sb_hbm, db_hbm, ga_hbm, nb_hbm, ew_hbm, eb_hbm, sw_hbm, hb_hbm, cot_hbm,
    out_hbm, sum_ref, tail_ref,
    pat_ref, side_ref, fm_ref, wb_ref, wbs_ref, pb_ref, stem3_ref, up2_ref, dnn2_ref, dn3_ref, upn3_ref, tiles,
    target, marks, stem_v, dw_v, sb_v, db_v, ga_v, nb_v, ew_v, eb_v, sw_v, hb_v, send, recv, edge, edges,
    edges_mid, ct, cot_ref, in_sem, par_sem, tile_send, tile_recv, row_send, row_recv, edge_send, edge_recv,
    mid_send, mid_recv, cot_sem, out_sem, F, FS, D, DSH, DY, GE, GS, ACC, FHL, FSH, SH, OUT, G, R0, B0, R1, B1,
    R2, TG, TR, TP, TX, DF, DFS, GV, s0, r0, s1, r1, s2, r2, s3, r3, s4, r4, ts1, tr1, ts2, tr2, ts3, tr3, HALO, SPX, *bufs,
):
    gy = lax.axis_index("gy")
    gx = lax.axis_index("gx")
    ny = lax.axis_size("gy")
    nx = lax.axis_size("gx")

    def device(dy, dx):
        return (lax.rem(gy + dy + ny, ny), lax.rem(gx + dx + nx, nx))

    y_hi, xx, core = gy >> 3, (gy >> 1) & 3, gy & 1
    y_lo, z = gx >> 3, gx & 7
    plane = (y_hi * 2 + y_lo) * 4 + xx

    def at_plane(m, c):
        return ((m >> 3) * 8 + (m & 3) * 2 + c, ((m >> 2) & 1) * 8 + z)

    def at_z(j):
        return (gy, y_lo * 8 + j)

    barrier = pltpu.get_barrier_semaphore()

    def greet(to):
        pl.semaphore_signal(barrier, inc=1, device_id=to, device_id_type=MESH)

    peers = [(0, 1), (0, -1), (0, 9), (0, -9)] + [(dy, dx) for dy in (-1, 1) for dx in (-1, 0, 1)]
    for dy, dx in peers:
        greet(device(dy, dx))
    each(1, 16, lambda i: greet(at_plane((plane + i) & 15, core)))
    each(0, 16, lambda i: greet(at_plane((plane + i) & 15, 1 - core)))
    each(1, 8, lambda i: greet(at_z((z + i) & 7)))
    greetings = len(peers) + 15 + 16 + 7

    params = [
        pltpu.make_async_copy(src, dst, par_sem.at[i])
        for i, (src, dst) in enumerate((
            (target_hbm, target), (marks_hbm, marks), (stem_hbm, stem_v), (dw_hbm, dw_v), (sb_hbm, sb_v),
            (db_hbm, db_v), (ga_hbm, ga_v), (nb_hbm, nb_v), (ew_hbm, ew_v), (eb_hbm, eb_v), (sw_hbm, sw_v),
            (hb_hbm, hb_v)))
    ]
    params[0].start()
    params[1].start()
    loads = []
    for group in range(len(GROUPS)):
        for lo, n in row_ranges(group):
            for k in range(3):
                at = pl.ds(k * 4096 + lo * 256, n * 256)
                loads.append((group, pltpu.make_async_copy(
                    tiles_hbm.at[:, at], tiles.at[:, at], in_sem.at[len(loads)])))
                loads[-1][1].start()
    for copy in params[2:]:
        copy.start()
    cot_copy = pltpu.make_async_copy(cot_hbm, cot_ref, cot_sem)
    cot_copy.start()

    sub = lax.broadcasted_iota(jnp.int32, (8, W), 0)
    lane = lanes()
    row8 = lax.broadcasted_iota(jnp.int32, (8, 8), 0)
    col8 = lax.broadcasted_iota(jnp.int32, (8, 8), 1)
    eye = row8 == col8
    params[0].wait()
    params[1].wait()

    def down_column(row):
        return jnp.sum(jnp.where(eye, row, 0.0), axis=1, keepdims=True)

    codes = jnp.broadcast_to(target[...], (8, 8))
    bucket = ((((codes >> 3) - gx - 1) & 15) >> 3).astype(f32)
    place = (codes & 7).astype(f32)
    mark = jnp.broadcast_to(marks[...], (8, 8)).astype(f32)
    bucket_col = down_column(bucket)
    rank = jnp.sum(jnp.where((bucket_col == bucket) & (row8 < col8), 1.0, 0.0), axis=0, keepdims=True)
    slot_pos = bucket[0:1, :] * 4.0 + rank

    def sources(wanted):
        return jnp.sum(jnp.where(slot_pos == wanted.astype(f32), col8.astype(f32), 0.0), axis=1, keepdims=True)

    order = jnp.broadcast_to(sources(row8), (8, W)).astype(jnp.int32)
    turned = jnp.broadcast_to(sources((row8 + 4) & 7), (8, W)).astype(jnp.int32)
    place_col = jnp.broadcast_to(down_column(place), (8, W))
    mark_col = jnp.broadcast_to(down_column(mark), (8, W))
    low = sub < 4

    def put(q, x0, x1):
        g0 = take(x0, order, 0)
        g1 = take(x1, turned, 0)
        send[0, q] = jnp.where(low, g0, g1)
        send[1, q] = jnp.where(low, g1, g0)

    def tile_copy(bucket_at, group):
        lo, hi = payload_range(group)
        return pltpu.make_async_remote_copy(
            src_ref=send.at[bucket_at, pl.ds(lo, hi - lo)],
            dst_ref=recv.at[bucket_at, pl.ds(lo, hi - lo)],
            send_sem=tile_send.at[bucket_at, group],
            recv_sem=tile_recv.at[bucket_at, group],
            device_id=device(0, 1 + 8 * bucket_at),
            device_id_type=MESH,
        )

    pos = lane & 7
    left = pos < 3

    def prepare():
        src = lax.broadcasted_iota(jnp.int32, (2 * W, W), 0) & (W - 1)
        dst = lax.broadcasted_iota(jnp.int32, (2 * W, W), 1)
        for n, b in enumerate(SHIFTS):
            SH[:, n * W : (n + 1) * W] = jnp.where(src == dst + (b - 3), 1.0, 0.0).astype(bf16)

        for copy in params[2:]:
            copy.wait()
        ct[...] = jnp.zeros_like(ct)
        ct[0:TAPS, 0:C] = dw_v[...]
        for k, ref in enumerate((sb_v, db_v, ga_v, nb_v, hb_v)):
            ct[STEM_B + k : STEM_B + k + 1, 0:C] = ref[...]
        cols = ct[...].T
        ct[...] = cols

        def spread(cb, _):
            cs = pl.ds(pl.multiple_of(cb * 8, 8), 8)
            wc = ct[cs, :]
            for a in range(7):
                taps = []
                for b in range(7):
                    t = 7 * a + b
                    taps.append(jnp.broadcast_to(wc[:, t : t + 1], (8, W)))
                    wb_ref[t, cs, :] = taps[-1]
                for k in range(3):
                    wbs_ref[3 * a + k, cs, :] = jnp.where(left, taps[k], taps[6 - k])
            for k in range(5):
                pb_ref[k, cs, :] = jnp.broadcast_to(wc[:, STEM_B + k : STEM_B + k + 1], (8, W))
            return 0

        lax.fori_loop(0, NB, spread, 0)

        def turned_over(x):
            n = x.shape[0]
            return jnp.concatenate([x, jnp.zeros((W - n, x.shape[1]), f32)], axis=0).T

        stem_pad = jnp.concatenate([stem_v[...], jnp.zeros((KK, W - C), f32)], axis=1)
        hi, lo = split(turned_over(stem_pad)[:C, :KK])
        stem3_ref[:, 0:KK] = hi
        stem3_ref[:, KK : 2 * KK] = hi
        stem3_ref[:, 2 * KK :] = lo
        ew = ew_v[...]
        sw = sw_v[...]
        for src, ref in ((sw, dn3_ref), (ew, upn3_ref)):
            hi, lo = split(src)
            ref[:, 0:HID] = hi
            ref[:, HID : 2 * HID] = hi
            ref[:, 2 * HID :] = lo
        hi, lo = split(turned_over(sw)[:, :C])
        dnn2_ref[0:HID, 0:C] = hi
        dnn2_ref[0:HID, W : W + C] = hi
        dnn2_ref[HID:, 0:C] = lo
        dnn2_ref[HID:, W:] = jnp.zeros((HID, W), bf16)
        dnn2_ref[:, C:W] = jnp.zeros((2 * HID, W - C), bf16)
        dnn2_ref[0:HID, W + C :] = jnp.zeros((HID, W - C), bf16)
        up = jnp.concatenate([ew, eb_v[...].reshape(1, HID), jnp.zeros((W - C - 1, HID), f32)], axis=0).T
        hi, lo = split(up[:, : W])
        up2_ref[0:HID, 0 : W] = hi
        up2_ref[0:HID, W :] = hi
        up2_ref[HID:, 0 : W] = lo
        up2_ref[HID:, W :] = jnp.zeros((HID, W), bf16)


    put(0, place_col, place_col)
    put(1, mark_col, mark_col)
    for group, rows in enumerate(GROUPS):
        for at, copy in loads:
            if at == group:
                copy.wait()
        for h in rows:
            for k in range(3):
                r = k * 32 + h * 2
                x0 = tiles[:, r * W : (r + 1) * W] * mark_col
                x1 = tiles[:, (r + 1) * W : (r + 2) * W] * mark_col
                put(INFO + 3 * ORDER.index(h) + k, x0, x1)
        if group > 0:
            for bucket_at in range(2):
                tile_copy(bucket_at, group).start()
            continue
        prepare()
        pl.semaphore_wait(barrier, greetings)
        for bucket_at in range(2):
            tile_copy(bucket_at, group).start()

    w16 = lane & 15
    beta = lane >> 4
    prow = lane >> 3

    def row_copy(up):
        src, dst, dy = (3, H + 3, -1) if up else (H, 0, 1)
        return pltpu.make_async_remote_copy(
            src_ref=pat_ref.at[pl.ds(src, 3)],
            dst_ref=pat_ref.at[pl.ds(dst, 3)],
            send_sem=row_send.at[int(up)],
            recv_sem=row_recv.at[int(up)],
            device_id=device(dy, 0),
            device_id_type=MESH,
        )

    def edge_copy(i):
        dy, dx = NEAR[i]
        return pltpu.make_async_remote_copy(
            src_ref=edge.at[0], dst_ref=edges.at[i], send_sem=edge_send.at[i], recv_sem=edge_recv.at[i],
            device_id=device(dy, dx), device_id_type=MESH)

    def mid_copy(group, i):
        dy, dx = NEAR[i]
        return pltpu.make_async_remote_copy(
            src_ref=edge.at[group], dst_ref=edges_mid.at[group - 1, i],
            send_sem=mid_send.at[group - 1, i], recv_sem=mid_recv.at[group - 1, i],
            device_id=device(dy, dx), device_id_type=MESH)

    for group, rows in enumerate(GROUPS):
        for bucket_at in range(2):
            tile_copy(bucket_at, group).wait_recv()
        if group == 0:
            places = (recv[0, 0], recv[1, 0])
            marks_in = (recv[0, 1], recv[1, 1])
            first = []
            for p in places:
                g = (beta - p.astype(jnp.int32)) & 7
                first.append((g >> 2) * 64 + w16 * 4 + (g & 3))
            wanted = ((beta - sub) & 7).astype(f32)
            wanted_t = beta.astype(f32)
            found = []
            fm = jnp.zeros((8, W), f32)
            for j, off in ((0, 0), (1, 4)):
                at = jnp.zeros((8, W), f32)
                hit = jnp.zeros((8, W), f32)
                for k in range(4):
                    p = jnp.broadcast_to(places[j][off + k : off + k + 1, :], (8, W))
                    m = jnp.broadcast_to(marks_in[j][off + k : off + k + 1, :], (8, W))
                    at = jnp.where(p == wanted, float(k), at)
                    hit = jnp.where(p == wanted, 1.0, hit)
                    fm = jnp.where(p == wanted_t, m, fm)
                found.append((at.astype(jnp.int32), hit))
            fm_ref[...] = fm
            in_a = found[0][1] > 0.0
            second = [(found[0][0] + 4 * a, found[1][0] + 4 * (1 - a)) for a in range(2)]
            third = ((sub + beta) & 7) * 16 + w16
        for h in rows:
            for k in range(3):
                q = INFO + 3 * ORDER.index(h) + k
                ya = take(recv[0, q], first[0], 1)
                yb = take(recv[1, q], first[1], 1)
                for a in range(2):
                    v = jnp.where(in_a, take(ya, second[a][0], 0), take(yb, second[a][1], 0))
                    pat_ref[h + 3, pl.ds(16 * k + 8 * a, 8), :] = take(v, third, 1)
        if group == 0:
            row_copy(True).start()
            row_copy(False).start()
        for j in range(KK // 8):
            js = pl.ds(8 * j, 8)
            v = jnp.zeros((8, W), f32)
            for h in rows:
                v = jnp.where(prow == h, roll(pat_ref[h + 3, js, :], 8 * h + 3), v)
            edge[group, js, :] = v
        if group == 0:
            for i in range(len(NEAR)):
                edge_copy(i).start()
        else:
            for i in range(2):
                mid_copy(group, i).start()

    for i in range(len(NEAR)):
        edge_copy(i).wait_recv()
    for group in (1, 2):
        for i in range(2):
            mid_copy(group, i).wait_recv()
    up_left, up_right = edges.at[5], edges.at[4]
    down_left, down_right = edges.at[3], edges.at[2]
    for j in range(KK // 8):
        js = pl.ds(8 * j, 8)
        from_left = edges[1, js, :] + (edges_mid[0, 1, js, :] + edges_mid[1, 1, js, :])
        from_right = edges[0, js, :] + (edges_mid[0, 0, js, :] + edges_mid[1, 0, js, :])
        mid = jnp.where(left, from_left, from_right)
        top = jnp.where(left, up_left[js, :], up_right[js, :])
        bottom = jnp.where(left, down_left[js, :], down_right[js, :])
        side_ref[0, js, :] = jnp.where(prow < 3, roll(top, -104), roll(mid, 24))
        side_ref[1, js, :] = jnp.where(prow < 8, roll(mid, -64), roll(bottom, 64))
    row_copy(True).wait_recv()
    row_copy(False).wait_recv()
    top_ok, bot_ok, ok0, ok1 = validity(gy, gx)
    def stem_of(p, bias):
        hi, lo = split(p)
        return dot(stem3_ref[...], jnp.concatenate([hi, lo, hi], axis=0)) + bias

    bias2 = jnp.concatenate([pb_ref[0], pb_ref[0]], axis=1)

    def row_ok(r):
        return top_ok if r < 3 else bot_ok if r >= H + 3 else None

    for r in range(0, EXT, 2):
        parts = []
        for q in range(2):
            ok = row_ok(r + q)
            p = pat_ref[r + q]
            parts.append(p if ok is None else jnp.where(ok > 0.0, p, 0.0))
        y = stem_of(jnp.concatenate(parts, axis=1), bias2)
        for q in range(2):
            ok = row_ok(r + q)
            v = y[:, q * W : (q + 1) * W]
            if ok is not None:
                v = v * ok
            F[r + q] = v
            hi, lo = split(v)
            FHL[(r + q) * C : (r + q + 1) * C, 0:W] = hi
            FHL[(r + q) * C : (r + q + 1) * C, W:] = lo
    parts = []
    for i, ok in enumerate((ok0, ok1)):
        okk = jnp.concatenate([ok] * (KK // 8), axis=0)
        parts.append(jnp.where(okk > 0.0, side_ref[i], 0.0))
    y = stem_of(jnp.concatenate(parts, axis=1), bias2)
    for i, ok in enumerate((ok0, ok1)):
        FS[i] = y[:, i * W : (i + 1) * W] * jnp.concatenate([ok] * NB, axis=0)

    def shift_rows(ref, starts, rows):
        for n in range(3):
            for at in starts:
                y = dot(FHL[at : at + rows, :], SH[:, 2 * n * W : (2 * n + 2) * W])
                for r in range(rows // C):
                    ref[2 * n, at // C + r] = y[r * C : (r + 1) * C, :W]
                    ref[2 * n + 1, at // C + r] = y[r * C : (r + 1) * C, W:]

    shift_rows(FSH, (0, 11 * C), 11 * C)

    def window(a, lo, hi):
        return jnp.where(prow96 < 11 - a, roll(lo, -8 * a), roll(hi, 8 * (11 - a)))

    lane96 = lanes((C, W))
    pos96 = lane96 & 7
    prow96 = lane96 >> 3
    left96 = pos96 < 3
    right96 = (pos96 >= 3) & (pos96 < 6)
    edge96 = (lane96 < 3) | (lane96 >= W - 3)
    part = [None] * 3
    for a in range(7):
        win = window(a, FS[0], FS[1])
        for k in range(3):
            t = wbs_ref[3 * a + k] * win
            part[k] = t if part[k] is None else part[k] + t
    q = part[0]
    for k in (1, 2):
        q = q + jnp.where(left96, jnp.where(pos96 < 3 - k, roll(part[k], -k), 0.0),
                          jnp.where((pos96 >= 3 + k) & (pos96 < 6), roll(part[k], k), 0.0))
    q = jnp.where(left96, roll(q, -3), roll(q, 3))
    for h in range(H):
        HALO[h] = pb_ref[1] + jnp.where(edge96, roll(q, 125 - 8 * h), 0.0)

    def conv_block(cb, _):
        cs = pl.ds(pl.multiple_of(cb * 8, 8), 8)
        acc = [HALO[h, cs, :] for h in range(H)]
        for b in range(7):
            if b == 3:
                rows = [F[r, cs, :] for r in range(EXT)]
            else:
                rows = [FSH[SHIFTS.index(b), r, cs, :] for r in range(EXT)]
            for a in range(7):
                w = wb_ref[7 * a + b, cs, :]
                for h in range(H):
                    acc[h] = acc[h] + w * rows[h + a]
        for h in range(H):
            D[h, cs, :] = acc[h]
        return 0

    lax.fori_loop(0, NB, conv_block, 0)

    fmc = jnp.concatenate([fm_ref[...]] * NB, axis=0)
    ones_row = jnp.where(lax.broadcasted_iota(jnp.int32, (W - C, 2 * W), 0) == 0, 1.0, 0.0)
    lanesets = [bufs[: len(bufs) // 2], bufs[len(bufs) // 2 :]]
    none = jnp.zeros((W - C, 2 * W), bf16)
    for XHL, YHL, *_ in lanesets:
        YHL[C:W, :] = none
        YHL[W + C :, :] = none
        XHL[C:XR, :] = ones_row.astype(bf16)
        XHL[XR + C :, :] = none
    GE[...] = jnp.zeros_like(GE)
    GS[...] = jnp.zeros_like(GS)
    ACC[...] = jnp.zeros_like(ACC)

    def stage_a(i, buf):
        XHL, YHL, U, DA, AHL, GHL, XN, RS = buf
        for q in range(2):
            h = 2 * i + q
            qs = slice(q * W, (q + 1) * W)
            x = D[h]
            m = jnp.mean(x, axis=0, keepdims=True)
            xc = x - m
            v = jnp.mean(xc * xc, axis=0, keepdims=True)
            rs = lax.rsqrt(v + EPS)
            xn = xc * rs
            XN[q] = xn
            RS[q] = jnp.broadcast_to(rs, (8, W))
            hi, lo = split(xn * pb_ref[2] + pb_ref[3])
            XHL[0:C, qs] = hi
            XHL[XR : XR + C, qs] = lo
            dy = cot_ref[pl.ds(h, C, stride=H), :] * fmc
            DY[h] = dy
            ACC[3] += dy
            hi, lo = split(dy)
            YHL[0:C, qs] = hi
            YHL[W : W + C, qs] = lo
        t = dot(up2_ref[...], XHL[...])
        U[...] = t[:HID] + t[HID:]
        t = dot(dnn2_ref[...], YHL[...])
        DA[...] = t[:HID] + t[HID:]

    def stage_b(buf):
        XHL, YHL, U, DA, AHL, GHL, XN, RS = buf
        for k in range(HID // CH):
            ks = slice(k * CH, (k + 1) * CH)
            kl = slice(HID + k * CH, HID + (k + 1) * CH)
            u = U[ks, :]
            x = 1.0 + (0.3275911 * 0.7071067811865476) * jnp.abs(u)
            t = pl.reciprocal(x, approx=True)
            t = t * (2.0 - x * t)
            e = jnp.exp2(-0.7213475204444817 * (u * u))
            poly = t * (0.5 * 0.254829592 + t * (0.5 * -0.284496736 + t * (0.5 * 1.421413741 + t * (0.5 * -1.453152027 + t * (0.5 * 1.061405429)))))
            q = poly * e
            phi = jnp.where(u >= 0.0, 1.0 - q, q)
            g = phi + (0.3989422804014327 * u) * e
            hi, lo = split(u * phi)
            AHL[ks, :] = hi
            AHL[kl, :] = lo
            hi, lo = split(DA[ks, :] * g)
            GHL[ks, :] = hi
            GHL[kl, :] = lo

    def stage_c(i, buf):
        XHL, YHL, U, DA, AHL, GHL, XN, RS = buf
        y = dot(dn3_ref[:, : 2 * HID], AHL[...]) + dot(dn3_ref[:, 2 * HID :], AHL[0:HID, :])
        for q in range(2):
            h = 2 * i + q
            OUT[pl.ds(h, C, stride=H), :] = fmc * (F[h + 3] + (y[:, q * W : (q + 1) * W] + pb_ref[4]))
        for total, wide, tall in ((GS, YHL, AHL), (GE, XHL, GHL)):
            t = dot(tall[0:HID, :], wide[...], NT)
            total[...] += t[:, :W] + (t[:, W:] + dot(tall[HID:, :], wide[0:W, :], NT))
        dx = dot(upn3_ref[:, : 2 * HID], GHL[...]) + dot(upn3_ref[:, 2 * HID :], GHL[0:HID, :])
        for q in range(2):
            h = 2 * i + q
            d = dx[:, q * W : (q + 1) * W]
            xn = XN[q]
            ACC[0] += d * xn
            ACC[1] += d
            d = d * pb_ref[2]
            m1 = jnp.mean(d, axis=0, keepdims=True)
            m2 = jnp.mean(d * xn, axis=0, keepdims=True)
            d = (d - m1 - xn * m2) * RS[q, 0:1, :]
            D[h] = d
            ACC[2] += d
            hi, lo = split(d)
            hs = pl.ds(pl.multiple_of(h * C, C), C)
            FHL[hs, 0:W] = hi
            FHL[hs, W:] = lo

    def tiles(i, _):
        b0, b1 = lanesets
        stage_a(2 * i, b0)
        stage_a(2 * i + 1, b1)
        stage_b(b0)
        stage_c(2 * i, b0)
        stage_b(b1)
        stage_c(2 * i + 1, b1)
        return 0

    cot_copy.wait()
    lax.fori_loop(0, H // 4, tiles, 0)
    out_copy = pltpu.make_async_copy(OUT, out_hbm, out_sem)
    out_copy.start()

    def shift_gradient():
        shift_rows(DSH, (0, 8 * C), 8 * C)

    def slot(v):
        return v // 48, v % 48 // 3, v % 3

    v = 0
    for total, count in ((GE, 13), (GS, 12)):
        for j in range(3):
            t = total[W * j : W * j + W, :].T
            for i in range(count):
                G[slot(v)] = t[8 * i : 8 * i + 8, :]
                v += 1
    while v < SLOTS:
        G[slot(v)] = jnp.zeros((8, W), f32)
        v += 1

    def rdma(src, dst, send, recv, to):
        return pltpu.make_async_remote_copy(
            src_ref=src, dst_ref=dst, send_sem=send, recv_sem=recv, device_id=to, device_id_type=MESH)

    sibling = (gy + 1 - 2 * core, gx)

    def c0():
        return rdma(G.at[1 - core], R0, s0, r0, sibling)

    def c1(i):
        m = (plane + i) & 15
        return rdma(B0.at[m], R1.at[i], s1.at[i], r1.at[i], at_plane(m, core))

    def c2(i):
        return rdma(B1, R2.at[z], s2.at[i], r2.at[i], at_z((z + i) & 7))

    def g2(i):
        j = (z - i) & 7
        return rdma(B1, R2.at[j], s2.at[i], r2.at[i], at_z(j))

    def c3(i):
        ref = sum_ref.at[core, plane]
        return rdma(ref, ref, s3.at[i], r3.at[i], at_plane((plane + i) & 15, core))

    def g3(i):
        m = (plane - i) & 15
        ref = sum_ref.at[core, m]
        return rdma(ref, ref, s3.at[i], r3.at[i], at_plane(m, core))

    def c4():
        ref = sum_ref.at[core]
        return rdma(ref, ref, s4, r4, sibling)

    def g4():
        ref = sum_ref.at[1 - core]
        return rdma(ref, ref, s4, r4, sibling)

    def step(k):
        if k == 0:
            c0().start()
        elif k == 1:
            c0().wait_recv()
            B0[...] = G[core] + R0[...]
            each(1, 16, lambda i: c1(i).start())
        elif k == 2:
            each(1, 16, lambda i: c1(i).wait_recv())
            acc = B0[plane]
            for i in range(1, 16):
                acc = acc + R1[i]
            B1[...] = acc
            R2[z] = acc
            each(1, 8, lambda i: c2(i).start())
        elif k == 3:
            each(1, 8, lambda i: g2(i).wait_recv())
            acc = R2[0]
            for j in range(1, 8):
                acc = acc + R2[j]
            sum_ref[core, plane] = acc
            each(1, 16, lambda i: c3(i).start())
        elif k == 4:
            each(1, 16, lambda i: g3(i).wait_recv())
            c4().start()
        else:
            g4().wait_recv()
            c0().wait_send()
            each(1, 16, lambda i: c1(i).wait_send())
            each(1, 8, lambda i: c2(i).wait_send())
            each(1, 16, lambda i: c3(i).wait_send())
            c4().wait_send()


    def back_block(cb, _):
        for k, when in enumerate(STEPS):
            @pl.when(cb == when)
            def _(k=k):
                step(k + 1)

        cs = pl.ds(pl.multiple_of(cb * 8, 8), 8)
        def gradient_rows(b):
            if b == 3:
                return [D[h, cs, :] for h in range(H)]
            n = SHIFTS.index(6 - b)
            return [DSH[n, h, cs, :] for h in range(H)]

        grads = jnp.zeros((8, W), f32)
        rows = [F[r, cs, :] for r in range(EXT)]
        for b in range(7):
            dd = gradient_rows(b)
            for a in range(7):
                if b == 3:
                    part = None
                elif b < 3:
                    part = jnp.where(left, SPX[3 * a + b, cs, :], 0.0)
                else:
                    part = jnp.where(left, 0.0, SPX[3 * a + 6 - b, cs, :])
                for h in range(H):
                    t = dd[h] * rows[h + a]
                    part = t if part is None else part + t
                total = jnp.sum(part, axis=1, keepdims=True)
                grads = jnp.where(lane == 7 * a + b, total, grads)
        acc = [DY[r - 3, cs, :] if 3 <= r < H + 3 else None for r in range(EXT)]
        for b in range(7):
            dd = gradient_rows(b)
            for a in range(7):
                w = wb_ref[7 * a + b, cs, :]
                for h in range(H):
                    t = w * dd[h]
                    acc[h + a] = t if acc[h + a] is None else acc[h + a] + t
        for k, src in enumerate((2, 0, 1, 3)):
            total = jnp.sum(ACC[src, cs, :], axis=1, keepdims=True)
            grads = jnp.where(lane == DEPTH_B + k, total, grads)
        total = DFS[0, cs, :] + DFS[1, cs, :]
        for r in range(EXT):
            t = acc[r]
            if r < 3:
                t = t * top_ok
            elif r >= H + 3:
                t = t * bot_ok
            DF[r, cs, :] = t
            total = total + t
        total = jnp.sum(total, axis=1, keepdims=True)
        GV[cs, :] = jnp.where(lane == STEM_B, total, grads)
        return 0

    step(0)
    shift_gradient()

    packed = jnp.zeros((C, W), f32)
    for h in range(H):
        packed = jnp.where(prow96 == h, roll(D[h], 8 * h + 3), packed)
    packed = jnp.where(left96, roll(packed, -3), jnp.where(right96, roll(packed, 3), 0.0))
    vs = [packed]
    for k in (1, 2):
        vs.append(jnp.where(left96, jnp.where(pos96 >= k, roll(packed, k), 0.0),
                            jnp.where(right96 & (pos96 < 6 - k), roll(packed, -k), 0.0)))
    o0 = jnp.zeros((C, W), f32)
    o1 = jnp.zeros((C, W), f32)
    for a in range(7):
        win = window(a, FS[0], FS[1])
        t = None
        for k in range(3):
            u = wbs_ref[3 * a + k] * vs[k]
            t = u if t is None else t + u
            SPX[3 * a + k] = vs[k] * win
        o0 = o0 + jnp.where((prow96 >= a) & (prow96 < 11), roll(t, 8 * a), 0.0)
        o1 = o1 + jnp.where(prow96 < 5 + a, roll(t, 8 * (a - 11)), 0.0)
    DFS[0] = o0 * jnp.concatenate([ok0] * NB, axis=0)
    DFS[1] = o1 * jnp.concatenate([ok1] * NB, axis=0)

    lax.fori_loop(0, NB, back_block, 0)
    step(len(STEPS) + 1)

    def rows2(p0, p1, d0, d1):
        ph, plo = split(jnp.concatenate([p0, p1], axis=1))
        dh, dlo = split(jnp.concatenate([d0, d1], axis=1))
        t = dot(jnp.concatenate([ph, plo], axis=0), dh, NT)
        return t[:KK] + (t[KK:] + dot(ph, dlo, NT))

    def okpat(p, ok):
        return p if ok is None else jnp.where(ok > 0.0, p, 0.0)

    def row_ok(r):
        return top_ok if r < 3 else bot_ok if r >= H + 3 else None

    okk = [jnp.concatenate([ok] * (KK // 8), axis=0) for ok in (ok0, ok1)]
    gstem = rows2(okpat(side_ref[0], okk[0]), okpat(side_ref[1], okk[1]), DFS[0], DFS[1])
    for r in range(0, EXT, 2):
        gstem = gstem + rows2(
            okpat(pat_ref[r], row_ok(r)), okpat(pat_ref[r + 1], row_ok(r + 1)), DF[r], DF[r + 1])

    zero = jnp.zeros((KK, W - C), f32)
    gs = jnp.concatenate([gstem, zero], axis=1)
    vec = jnp.concatenate([GV[...], jnp.zeros((W - C, W), f32)], axis=0).T
    tail = [gs[8 * i : 8 * i + 8, :] for i in range(6)] + [vec[8 * i : 8 * i + 8, :] for i in range(7)]
    for i, v in enumerate(tail):
        TG[i] = v
    for i in range(len(tail), TAIL):
        TG[i] = jnp.zeros((8, W), f32)

    def owner(v):
        return at_plane(v, v & 1)

    mine = (plane & 1) == core

    def t1(v):
        return rdma(TG.at[v], TR.at[plane, core], ts1.at[v], tr1.at[plane, core], owner(v))

    def w1(m, c):
        return rdma(TP, TR.at[m, c], ts1.at[0], tr1.at[m, c], at_plane(m, c))

    def t2(i):
        return rdma(TP, TX.at[z], ts2.at[i], tr2.at[i], at_z((z + i) & 7))

    def w2(i):
        j = (z - i) & 7
        return rdma(TP, TX.at[j], ts2.at[i], tr2.at[i], at_z(j))

    def t3(m, c):
        ref = tail_ref.at[plane]
        return rdma(ref, ref, ts3.at[m, c], tr3.at[plane], at_plane(m, c))

    def w3(v):
        ref = tail_ref.at[v]
        return rdma(ref, ref, ts3.at[0, 0], tr3.at[v], owner(v))

    def others(f):
        def one(i):
            m, c = i >> 1, i & 1
            @pl.when((m != plane) | (c != core))
            def _():
                f(m, c)
        each(0, 32, one)

    def foreign(f):
        def one(v):
            @pl.when((v != plane) | ((v & 1) != core))
            def _():
                f(v)
        each(0, TAIL, one)

    foreign(lambda v: t1(v).start())

    @pl.when(mine)
    def _():
        TR[plane, core] = TG[plane]
        others(lambda m, c: w1(m, c).wait_recv())
        acc = TR[0, 0]
        for i in range(1, 32):
            acc = acc + TR[i >> 1, i & 1]
        TP[...] = acc
        TX[z] = acc
        each(1, 8, lambda i: t2(i).start())

    step(len(STEPS) + 2)

    @pl.when(mine)
    def _():
        each(1, 8, lambda i: w2(i).wait_recv())
        acc = TX[0]
        for j in range(1, 8):
            acc = acc + TX[j]
        tail_ref[plane] = acc
        others(lambda m, c: t3(m, c).start())

    step(len(STEPS) + 3)
    foreign(lambda v: t1(v).wait_send())
    step(len(STEPS) + 4)
    foreign(lambda v: w3(v).wait_recv())

    @pl.when(mine)
    def _():
        each(1, 8, lambda i: t2(i).wait_send())
        others(lambda m, c: t3(m, c).wait_send())

    out_copy.wait()
    for group in range(len(GROUPS)):
        for bucket_at in range(2):
            tile_copy(bucket_at, group).wait_send()
    row_copy(True).wait_send()
    row_copy(False).wait_send()
    for i in range(len(NEAR)):
        edge_copy(i).wait_send()
    for group in (1, 2):
        for i in range(2):
            mid_copy(group, i).wait_send()


def whole_call(*args):
    vm = pl.BlockSpec(memory_space=pltpu.VMEM)
    hbm = pl.BlockSpec(memory_space=pltpu.HBM)
    s = jax.ShapeDtypeStruct
    n_send = INFO + 3 * H
    near = len(NEAR)

    def v(*shape, dtype=f32):
        return pltpu.VMEM(shape, dtype)

    buf = [
        v(2 * XR, 2 * W, dtype=bf16), v(2 * W, 2 * W, dtype=bf16), v(HID, 2 * W), v(HID, 2 * W),
        v(2 * HID, 2 * W, dtype=bf16), v(2 * HID, 2 * W, dtype=bf16), v(2, C, W), v(2, 8, W),
    ]
    return pl.pallas_call(
        whole_kernel,
        out_shape=(s((C * H, W), f32), s((2, 16, 3, 8, W), f32), s((TAIL, 8, W), f32)),
        in_specs=[hbm] * 14,
        out_specs=[hbm, vm, vm],
        scratch_shapes=[
            v(EXT, KK, W), v(2, KK, W), v(8, W), v(TAPS, C, W), v(21, C, W), v(5, C, W),
            v(C, 3 * KK, dtype=bf16), v(2 * HID, 2 * XR, dtype=bf16), v(2 * HID, 2 * W, dtype=bf16),
            v(C, 3 * HID, dtype=bf16), v(C, 3 * HID, dtype=bf16),
            v(8, PIX), v(1, 8, dtype=jnp.int32), v(1, 8, dtype=jnp.int32),
            v(KK, C), v(TAPS, C), v(1, C), v(1, C), v(1, C), v(1, C), v(C, HID), v(HID), v(C, HID), v(1, C),
            v(2, n_send, 8, W), v(2, n_send, 8, W), v(3, KK, W), v(near, KK, W), v(2, 2, KK, W), v(W, W), v(C * H, W),
            DMA((12,)), DMA((12,)), DMA((2, 3)), DMA((2, 3)), DMA((2,)), DMA((2,)),
            DMA((near,)), DMA((near,)), DMA((2, 2)), DMA((2, 2)), DMA(()), DMA(()),
            v(EXT, C, W), v(2, C, W), v(H, C, W), v(6, H, C, W), v(H, C, W), v(HID, W), v(HID, W), v(4, C, W),
            v(EXT * C, 2 * W, dtype=bf16), v(6, EXT, C, W), v(2 * W, 6 * W, dtype=bf16), v(C * H, W),
            v(2, 16, 3, 8, W), v(16, 3, 8, W), v(16, 3, 8, W), v(16, 3, 8, W), v(3, 8, W), v(8, 3, 8, W),
            v(TAIL, 8, W), v(16, 2, 8, W), v(8, W), v(8, 8, W), v(EXT, C, W), v(2, C, W), v(C, W),
            DMA(()), DMA(()), DMA((16,)), DMA((16,)), DMA((8,)), DMA((8,)), DMA((16,)), DMA((16,)), DMA(()), DMA(()),
            DMA((TAIL,)), DMA((16, 2)), DMA((8,)), DMA((8,)), DMA((16, 2)), DMA((TAIL,)), v(H, C, W), v(21, C, W),
            *buf, *buf,
        ],
        compiler_params=pltpu.CompilerParams(
            collective_id=0, has_side_effects=True, vmem_limit_bytes=56 * 1024 * 1024),
        name="whole",
    )(*args)


PIECES = 4


def unpack_kernel(
    sum_hbm, tail_hbm, block_hbm, out_hbm, gstem_ref, gstem_b_ref, gdepth_ref, gdepth_b_ref, ggain_ref, gnbias_ref,
    gexp_ref, gexp_b_ref, gshr_ref, gshr_b_ref, held, sum_ref, tail_ref, sem,
):
    rows = C * H // PIECES

    def piece(i, back):
        at = pl.ds(i * rows, rows)
        if back:
            return pltpu.make_async_copy(held.at[at], out_hbm.at[at], sem.at[1, i])
        return pltpu.make_async_copy(block_hbm.at[at], held.at[at], sem.at[0, i])

    total = pltpu.make_async_copy(sum_hbm, sum_ref, sem.at[2, 0])
    last = pltpu.make_async_copy(tail_hbm, tail_ref, sem.at[2, 1])
    total.start()
    last.start()
    for i in range(PIECES):
        piece(i, False).start()
    total.wait()
    last.wait()

    def at(v):
        return sum_ref[v // 48, v % 48 // 3, v % 3]

    v = 0
    for j in range(3):
        for i in range(12):
            gexp_ref[8 * i : 8 * i + 8, W * j : W * j + W] = at(v)
            v += 1
        gexp_b_ref[W * j : W * j + W] = at(v)[0]
        v += 1
    for j in range(3):
        for i in range(12):
            gshr_ref[8 * i : 8 * i + 8, W * j : W * j + W] = at(v)
            v += 1
    for i in range(PIECES):
        piece(i, False).wait()
        piece(i, True).start()
    for i in range(6):
        gstem_ref[8 * i : 8 * i + 8, :] = tail_ref[i][:, :C]
        gdepth_ref[8 * i : 8 * i + 8, :] = tail_ref[6 + i][:, :C]
    last = tail_ref[12][:, :C]
    gdepth_ref[48:49, :] = last[0:1]
    for k, ref in enumerate((gstem_b_ref, gdepth_b_ref, ggain_ref, gnbias_ref, gshr_b_ref)):
        ref[...] = last[k + 1 : k + 2]
    for i in range(PIECES):
        piece(i, True).wait()


def unpack_call(block, total, tail):
    vm = pl.BlockSpec(memory_space=pltpu.VMEM)
    hbm = pl.BlockSpec(memory_space=pltpu.HBM)
    shapes = ((KK, C), (1, C), (TAPS, C), (1, C), (1, C), (1, C), (C, HID), (HID,), (C, HID), (1, C))
    return pl.pallas_call(
        unpack_kernel,
        out_shape=tuple(jax.ShapeDtypeStruct(s, f32) for s in ((C * H, W),) + shapes),
        in_specs=[hbm] * 3,
        out_specs=[hbm] + [vm] * len(shapes),
        scratch_shapes=[
            pltpu.VMEM((C * H, W), f32), pltpu.VMEM((2, 16, 3, 8, W), f32), pltpu.VMEM((TAIL, 8, W), f32), DMA((3, PIECES))],
        compiler_params=pltpu.CompilerParams(vmem_limit_bytes=56 * 1024 * 1024),
        name="unpack",
    )(total, tail, block)


def local(
    stored_tiles, tile_target, tile_mask,
    stem_weight, stem_bias, depth_weight, depth_bias, norm_gain, norm_bias,
    expand_weight, expand_bias, shrink_weight, shrink_bias, cotangent,
):
    def row(v):
        return v.reshape(1, -1)

    block, total, tail = whole_call(
        stored_tiles[0], tile_target, tile_mask, stem_weight, depth_weight, row(stem_bias), row(depth_bias),
        row(norm_gain), row(norm_bias), expand_weight, expand_bias, shrink_weight.T, row(shrink_bias),
        cotangent.reshape(C * H, W))
    out, gs, gsb, gd, gdb, gg, gn, ge, geb, gh, ghb = unpack_call(block, total, tail)
    return (
        out.reshape(C, H, W), gs, gsb[0], gd, gdb[0], gg[0], gn[0], ge, geb, gh.T, ghb[0],
    )


def solution(mesh):
    placed = (P("gy", "gx", None), P("gy", "gx"), P("gy", "gx")) + (P(),) * 10 + (P(None, "gy", "gx"),)
    return jax.shard_map(
        local, mesh=mesh, in_specs=placed,
        out_specs=(P(None, "gy", "gx"),) + (P(),) * 10,
        check_vma=False,
    )
```

```python
import jax
import jax.numpy as jnp
from jax import lax
from jax.experimental import pallas as pl
from jax.experimental.pallas import tpu as pltpu
from jax.sharding import PartitionSpec as P

C = 96
HID = 384
NB = C // 8
H = 16
W = 128
EXT = H + 6
KK = 48
TAPS = 49
PIX = 12288
f32 = jnp.float32
bf16 = jnp.bfloat16
EPS = 1e-6
MESH = pl.DeviceIdType.MESH
DMA = pltpu.SemaphoreType.DMA

NN = (((1,), (0,)), ((), ()))
NT = (((1,), (1,)), ((), ()))


def split(x):
    hi = x.astype(bf16)
    return hi, (x - hi.astype(f32)).astype(bf16)


def dot(a, b, dims=NN):
    return lax.dot_general(a, b, dims, preferred_element_type=f32)


def lanes(shape=(8, W)):
    return lax.broadcasted_iota(jnp.int32, shape, len(shape) - 1)


def roll(x, by):
    by = by % W
    return x if by == 0 else pltpu.roll(x, by, x.ndim - 1)


STEM_B, DEPTH_B, GAIN, NBIAS, SHRINK_B = 49, 50, 51, 52, 53
GROUPS = ((0, 1, 2, 13, 14, 15), (3, 4, 5, 6, 7, 8), (9, 10, 11, 12))
ORDER = tuple(h for group in GROUPS for h in group)
INFO = 2
NEAR = ((0, -1), (0, 1), (-1, -1), (-1, 1), (1, -1), (1, 1))


def payload_range(group):
    before = sum(len(g) for g in GROUPS[:group])
    after = before + len(GROUPS[group])
    return (0 if group == 0 else INFO + 3 * before), INFO + 3 * after


def row_ranges(group):
    rows = GROUPS[group]
    if group == 0:
        return ((rows[0], 3), (rows[3], 3))
    return ((rows[0], len(rows)),)


def take(x, index, axis):
    return jnp.take_along_axis(x, index, axis=axis)


def each(low, high, f):
    def one(i, _):
        f(i)
        return 0
    lax.fori_loop(low, high, one, 0)


XR = W
CH = 16
SLOTS = 96
TAIL = 16
SHIFTS = (0, 1, 2, 4, 5, 6)
STEPS = (3,)

def validity(gy, gx):
    ny = lax.axis_size("gy")
    nx = lax.axis_size("gx")
    lane = lanes()
    pos = lane & 7
    prow = lane >> 3
    top_ok = (gy > 0).astype(f32)
    bot_ok = (gy < ny - 1).astype(f32)
    left_ok = (gx > 0).astype(f32)
    right_ok = (gx < nx - 1).astype(f32)
    col_ok = jnp.where(pos < 3, left_ok, jnp.where(pos < 6, right_ok, 0.0))
    col_ok = jnp.where(prow < 11, col_ok, 0.0)
    ok0 = col_ok * jnp.where(prow < 3, top_ok, 1.0)
    ok1 = col_ok * jnp.where(prow >= 8, bot_ok, 1.0)
    return top_ok, bot_ok, ok0, ok1


def whole_kernel(
    tiles_hbm, target_hbm, marks_hbm, stem_hbm, dw_hbm, sb_hbm, db_hbm, ga_hbm, nb_hbm, ew_hbm, eb_hbm, sw_hbm, hb_hbm, cot_hbm,
    out_hbm, sum_ref, tail_ref,
    pat_ref, side_ref, fm_ref, wb_ref, wbs_ref, pb_ref, stem3_ref, up2_ref, dnn2_ref, dn3_ref, upn3_ref, tiles,
    target, marks, stem_v, dw_v, sb_v, db_v, ga_v, nb_v, ew_v, eb_v, sw_v, hb_v, send, recv, edge, edges,
    edges_mid, ct, cot_ref, in_sem, par_sem, tile_send, tile_recv, row_send, row_recv, edge_send, edge_recv,
    mid_send, mid_recv, cot_sem, out_sem, F, FS, D, DSH, DY, GE, GS, ACC, FHL, FSH, SH, OUT, G, R0, B0, R1, B1,
    R2, TG, TR, TP, TX, DF, DFS, GV, s0, r0, s1, r1, s2, r2, s3, r3, s4, r4, ts1, tr1, ts2, tr2, ts3, tr3, SPX, *bufs,
):
    gy = lax.axis_index("gy")
    gx = lax.axis_index("gx")
    ny = lax.axis_size("gy")
    nx = lax.axis_size("gx")

    def device(dy, dx):
        return (lax.rem(gy + dy + ny, ny), lax.rem(gx + dx + nx, nx))

    y_hi, xx, core = gy >> 3, (gy >> 1) & 3, gy & 1
    y_lo, z = gx >> 3, gx & 7
    plane = (y_hi * 2 + y_lo) * 4 + xx

    def at_plane(m, c):
        return ((m >> 3) * 8 + (m & 3) * 2 + c, ((m >> 2) & 1) * 8 + z)

    def at_z(j):
        return (gy, y_lo * 8 + j)

    barrier = pltpu.get_barrier_semaphore()

    def greet(to):
        pl.semaphore_signal(barrier, inc=1, device_id=to, device_id_type=MESH)

    peers = [(0, 1), (0, -1), (0, 9), (0, -9)] + [(dy, dx) for dy in (-1, 1) for dx in (-1, 0, 1)]
    for dy, dx in peers:
        greet(device(dy, dx))
    each(1, 16, lambda i: greet(at_plane((plane + i) & 15, core)))
    each(0, 16, lambda i: greet(at_plane((plane + i) & 15, 1 - core)))
    each(1, 8, lambda i: greet(at_z((z + i) & 7)))
    greetings = len(peers) + 15 + 16 + 7

    params = [
        pltpu.make_async_copy(src, dst, par_sem.at[i])
        for i, (src, dst) in enumerate((
            (target_hbm, target), (marks_hbm, marks), (stem_hbm, stem_v), (dw_hbm, dw_v), (sb_hbm, sb_v),
            (db_hbm, db_v), (ga_hbm, ga_v), (nb_hbm, nb_v), (ew_hbm, ew_v), (eb_hbm, eb_v), (sw_hbm, sw_v),
            (hb_hbm, hb_v)))
    ]
    params[0].start()
    params[1].start()
    loads = []
    for group in range(len(GROUPS)):
        for lo, n in row_ranges(group):
            for k in range(3):
                at = pl.ds(k * 4096 + lo * 256, n * 256)
                loads.append((group, pltpu.make_async_copy(
                    tiles_hbm.at[:, at], tiles.at[:, at], in_sem.at[len(loads)])))
                loads[-1][1].start()
    for copy in params[2:]:
        copy.start()
    cot_copy = pltpu.make_async_copy(cot_hbm, cot_ref, cot_sem)
    cot_copy.start()

    sub = lax.broadcasted_iota(jnp.int32, (8, W), 0)
    lane = lanes()
    row8 = lax.broadcasted_iota(jnp.int32, (8, 8), 0)
    col8 = lax.broadcasted_iota(jnp.int32, (8, 8), 1)
    eye = row8 == col8
    params[0].wait()
    params[1].wait()

    def down_column(row):
        return jnp.sum(jnp.where(eye, row, 0.0), axis=1, keepdims=True)

    codes = jnp.broadcast_to(target[...], (8, 8))
    bucket = ((((codes >> 3) - gx - 1) & 15) >> 3).astype(f32)
    place = (codes & 7).astype(f32)
    mark = jnp.broadcast_to(marks[...], (8, 8)).astype(f32)
    bucket_col = down_column(bucket)
    rank = jnp.sum(jnp.where((bucket_col == bucket) & (row8 < col8), 1.0, 0.0), axis=0, keepdims=True)
    slot_pos = bucket[0:1, :] * 4.0 + rank

    def sources(wanted):
        return jnp.sum(jnp.where(slot_pos == wanted.astype(f32), col8.astype(f32), 0.0), axis=1, keepdims=True)

    order = jnp.broadcast_to(sources(row8), (8, W)).astype(jnp.int32)
    turned = jnp.broadcast_to(sources((row8 + 4) & 7), (8, W)).astype(jnp.int32)
    place_col = jnp.broadcast_to(down_column(place), (8, W))
    mark_col = jnp.broadcast_to(down_column(mark), (8, W))
    low = sub < 4

    def put(q, x0, x1):
        g0 = take(x0, order, 0)
        g1 = take(x1, turned, 0)
        send[0, q] = jnp.where(low, g0, g1)
        send[1, q] = jnp.where(low, g1, g0)

    def tile_copy(bucket_at, group):
        lo, hi = payload_range(group)
        return pltpu.make_async_remote_copy(
            src_ref=send.at[bucket_at, pl.ds(lo, hi - lo)],
            dst_ref=recv.at[bucket_at, pl.ds(lo, hi - lo)],
            send_sem=tile_send.at[bucket_at, group],
            recv_sem=tile_recv.at[bucket_at, group],
            device_id=device(0, 1 + 8 * bucket_at),
            device_id_type=MESH,
        )

    pos = lane & 7
    left = pos < 3

    def prepare():
        src = lax.broadcasted_iota(jnp.int32, (2 * W, W), 0) & (W - 1)
        dst = lax.broadcasted_iota(jnp.int32, (2 * W, W), 1)
        for n, b in enumerate(SHIFTS):
            SH[:, n * W : (n + 1) * W] = jnp.where(src == dst + (b - 3), 1.0, 0.0).astype(bf16)

        for copy in params[2:]:
            copy.wait()
        ct[...] = jnp.zeros_like(ct)
        ct[0:TAPS, 0:C] = dw_v[...]
        for k, ref in enumerate((sb_v, db_v, ga_v, nb_v, hb_v)):
            ct[STEM_B + k : STEM_B + k + 1, 0:C] = ref[...]
        cols = ct[...].T
        ct[...] = cols

        def spread(cb, _):
            cs = pl.ds(pl.multiple_of(cb * 8, 8), 8)
            wc = ct[cs, :]
            for a in range(7):
                taps = []
                for b in range(7):
                    t = 7 * a + b
                    taps.append(jnp.broadcast_to(wc[:, t : t + 1], (8, W)))
                    wb_ref[t, cs, :] = taps[-1]
                for k in range(3):
                    wbs_ref[3 * a + k, cs, :] = jnp.where(left, taps[k], taps[6 - k])
            for k in range(5):
                pb_ref[k, cs, :] = jnp.broadcast_to(wc[:, STEM_B + k : STEM_B + k + 1], (8, W))
            return 0

        lax.fori_loop(0, NB, spread, 0)

        def turned_over(x):
            n = x.shape[0]
            return jnp.concatenate([x, jnp.zeros((W - n, x.shape[1]), f32)], axis=0).T

        stem_pad = jnp.concatenate([stem_v[...], jnp.zeros((KK, W - C), f32)], axis=1)
        hi, lo = split(turned_over(stem_pad)[:C, :KK])
        stem3_ref[:, 0:KK] = hi
        stem3_ref[:, KK : 2 * KK] = hi
        stem3_ref[:, 2 * KK :] = lo
        ew = ew_v[...]
        sw = sw_v[...]
        for src, ref in ((sw, dn3_ref), (ew, upn3_ref)):
            hi, lo = split(src)
            ref[:, 0:HID] = hi
            ref[:, HID : 2 * HID] = hi
            ref[:, 2 * HID :] = lo
        hi, lo = split(turned_over(sw)[:, :C])
        dnn2_ref[0:HID, 0:C] = hi
        dnn2_ref[0:HID, W : W + C] = hi
        dnn2_ref[HID:, 0:C] = lo
        dnn2_ref[HID:, W:] = jnp.zeros((HID, W), bf16)
        dnn2_ref[:, C:W] = jnp.zeros((2 * HID, W - C), bf16)
        dnn2_ref[0:HID, W + C :] = jnp.zeros((HID, W - C), bf16)
        up = jnp.concatenate([ew, eb_v[...].reshape(1, HID), jnp.zeros((W - C - 1, HID), f32)], axis=0).T
        hi, lo = split(up[:, : W])
        up2_ref[0:HID, 0 : W] = hi
        up2_ref[0:HID, W :] = hi
        up2_ref[HID:, 0 : W] = lo
        up2_ref[HID:, W :] = jnp.zeros((HID, W), bf16)


    put(0, place_col, place_col)
    put(1, mark_col, mark_col)
    for group, rows in enumerate(GROUPS):
        for at, copy in loads:
            if at == group:
                copy.wait()
        for h in rows:
            for k in range(3):
                r = k * 32 + h * 2
                x0 = tiles[:, r * W : (r + 1) * W] * mark_col
                x1 = tiles[:, (r + 1) * W : (r + 2) * W] * mark_col
                put(INFO + 3 * ORDER.index(h) + k, x0, x1)
        if group > 0:
            for bucket_at in range(2):
                tile_copy(bucket_at, group).start()
            continue
        prepare()
        pl.semaphore_wait(barrier, greetings)
        for bucket_at in range(2):
            tile_copy(bucket_at, group).start()

    top_ok, bot_ok, ok0, ok1 = validity(gy, gx)

    def stem_of(p, bias):
        hi, lo = split(p)
        return dot(stem3_ref[...], jnp.concatenate([hi, lo, hi], axis=0)) + bias

    bias2 = jnp.concatenate([pb_ref[0], pb_ref[0]], axis=1)

    def row_ok(r):
        return top_ok if r < 3 else bot_ok if r >= H + 3 else None

    def stem_pair(pair):
        parts = []
        for q in range(2):
            ok = row_ok(pair[q])
            p = pat_ref[pair[q]]
            parts.append(p if ok is None else jnp.where(ok > 0.0, p, 0.0))
        y = stem_of(jnp.concatenate(parts, axis=1), bias2)
        for q in range(2):
            r = pair[q]
            ok = row_ok(r)
            v = y[:, q * W : (q + 1) * W]
            if ok is not None:
                v = v * ok
            F[r] = v
            hi, lo = split(v)
            FHL[r * C : (r + 1) * C, 0:W] = hi
            FHL[r * C : (r + 1) * C, W:] = lo
    def shift_rows(ref, starts, rows):
        for n in range(3):
            for at in starts:
                y = dot(FHL[at : at + rows, :], SH[:, 2 * n * W : (2 * n + 2) * W])
                for r in range(rows // C):
                    ref[2 * n, at // C + r] = y[r * C : (r + 1) * C, :W]
                    ref[2 * n + 1, at // C + r] = y[r * C : (r + 1) * C, W:]

    w16 = lane & 15
    beta = lane >> 4
    prow = lane >> 3

    def row_copy(up):
        src, dst, dy = (3, H + 3, -1) if up else (H, 0, 1)
        return pltpu.make_async_remote_copy(
            src_ref=pat_ref.at[pl.ds(src, 3)],
            dst_ref=pat_ref.at[pl.ds(dst, 3)],
            send_sem=row_send.at[int(up)],
            recv_sem=row_recv.at[int(up)],
            device_id=device(dy, 0),
            device_id_type=MESH,
        )

    def edge_copy(i):
        dy, dx = NEAR[i]
        return pltpu.make_async_remote_copy(
            src_ref=edge.at[0], dst_ref=edges.at[i], send_sem=edge_send.at[i], recv_sem=edge_recv.at[i],
            device_id=device(dy, dx), device_id_type=MESH)

    def mid_copy(group, i):
        dy, dx = NEAR[i]
        return pltpu.make_async_remote_copy(
            src_ref=edge.at[group], dst_ref=edges_mid.at[group - 1, i],
            send_sem=mid_send.at[group - 1, i], recv_sem=mid_recv.at[group - 1, i],
            device_id=device(dy, dx), device_id_type=MESH)

    for group, rows in enumerate(GROUPS):
        for bucket_at in range(2):
            tile_copy(bucket_at, group).wait_recv()
        if group == 0:
            places = (recv[0, 0], recv[1, 0])
            marks_in = (recv[0, 1], recv[1, 1])
            first = []
            for p in places:
                g = (beta - p.astype(jnp.int32)) & 7
                first.append((g >> 2) * 64 + w16 * 4 + (g & 3))
            wanted = ((beta - sub) & 7).astype(f32)
            wanted_t = beta.astype(f32)
            found = []
            fm = jnp.zeros((8, W), f32)
            for j, off in ((0, 0), (1, 4)):
                at = jnp.zeros((8, W), f32)
                hit = jnp.zeros((8, W), f32)
                for k in range(4):
                    p = jnp.broadcast_to(places[j][off + k : off + k + 1, :], (8, W))
                    m = jnp.broadcast_to(marks_in[j][off + k : off + k + 1, :], (8, W))
                    at = jnp.where(p == wanted, float(k), at)
                    hit = jnp.where(p == wanted, 1.0, hit)
                    fm = jnp.where(p == wanted_t, m, fm)
                found.append((at.astype(jnp.int32), hit))
            fm_ref[...] = fm
            in_a = found[0][1] > 0.0
            second = [(found[0][0] + 4 * a, found[1][0] + 4 * (1 - a)) for a in range(2)]
            third = ((sub + beta) & 7) * 16 + w16
        for h in rows:
            for k in range(3):
                q = INFO + 3 * ORDER.index(h) + k
                ya = take(recv[0, q], first[0], 1)
                yb = take(recv[1, q], first[1], 1)
                for a in range(2):
                    v = jnp.where(in_a, take(ya, second[a][0], 0), take(yb, second[a][1], 0))
                    pat_ref[h + 3, pl.ds(16 * k + 8 * a, 8), :] = take(v, third, 1)
        if group == 0:
            row_copy(True).start()
            row_copy(False).start()
        for j in range(KK // 8):
            js = pl.ds(8 * j, 8)
            v = jnp.zeros((8, W), f32)
            for h in rows:
                v = jnp.where(prow == h, roll(pat_ref[h + 3, js, :], 8 * h + 3), v)
            edge[group, js, :] = v
        if group == 0:
            for i in range(len(NEAR)):
                edge_copy(i).start()
        else:
            for i in range(2):
                mid_copy(group, i).start()
        for n in range(0, len(rows), 2):
            stem_pair((rows[n] + 3, rows[n + 1] + 3))
        for lo, n in row_ranges(group):
            shift_rows(FSH, ((lo + 3) * C,), n * C)

    def feature_rows(b, which, cs):
        if b == 3:
            return {r: F[r, cs, :] for r in which}
        return {r: FSH[SHIFTS.index(b), r, cs, :] for r in which}

    def conv_block(cb, _):
        cs = pl.ds(pl.multiple_of(cb * 8, 8), 8)
        acc = [pb_ref[1, cs, :]] * H
        for b in range(7):
            rows = feature_rows(b, range(3, H + 3), cs)
            for a in range(7):
                w = wb_ref[7 * a + b, cs, :]
                for h in range(H):
                    if h + a in rows:
                        acc[h] = acc[h] + w * rows[h + a]
        for h in range(H):
            D[h, cs, :] = acc[h]
        return 0

    lax.fori_loop(0, NB, conv_block, 0)

    for i in range(len(NEAR)):
        edge_copy(i).wait_recv()
    for group in (1, 2):
        for i in range(2):
            mid_copy(group, i).wait_recv()
    up_left, up_right = edges.at[5], edges.at[4]
    down_left, down_right = edges.at[3], edges.at[2]
    for j in range(KK // 8):
        js = pl.ds(8 * j, 8)
        from_left = edges[1, js, :] + (edges_mid[0, 1, js, :] + edges_mid[1, 1, js, :])
        from_right = edges[0, js, :] + (edges_mid[0, 0, js, :] + edges_mid[1, 0, js, :])
        mid = jnp.where(left, from_left, from_right)
        top = jnp.where(left, up_left[js, :], up_right[js, :])
        bottom = jnp.where(left, down_left[js, :], down_right[js, :])
        side_ref[0, js, :] = jnp.where(prow < 3, roll(top, -104), roll(mid, 24))
        side_ref[1, js, :] = jnp.where(prow < 8, roll(mid, -64), roll(bottom, 64))
    row_copy(True).wait_recv()
    row_copy(False).wait_recv()
    for r in (0, 2, 20):
        stem_pair((r, r + 1) if r != 2 else (2, 19))
    parts = []
    for i, ok in enumerate((ok0, ok1)):
        okk = jnp.concatenate([ok] * (KK // 8), axis=0)
        parts.append(jnp.where(okk > 0.0, side_ref[i], 0.0))
    y = stem_of(jnp.concatenate(parts, axis=1), bias2)
    for i, ok in enumerate((ok0, ok1)):
        FS[i] = y[:, i * W : (i + 1) * W] * jnp.concatenate([ok] * NB, axis=0)

    for r in (0, H + 3):
        shift_rows(FSH, (r * C,), 3 * C)

    def window(a, lo, hi):
        return jnp.where(prow96 < 11 - a, roll(lo, -8 * a), roll(hi, 8 * (11 - a)))

    lane96 = lanes((C, W))
    pos96 = lane96 & 7
    prow96 = lane96 >> 3
    left96 = pos96 < 3
    right96 = (pos96 >= 3) & (pos96 < 6)
    edge96 = (lane96 < 3) | (lane96 >= W - 3)
    part = [None] * 3
    for a in range(7):
        win = window(a, FS[0], FS[1])
        for k in range(3):
            t = wbs_ref[3 * a + k] * win
            part[k] = t if part[k] is None else part[k] + t
    q = part[0]
    for k in (1, 2):
        q = q + jnp.where(left96, jnp.where(pos96 < 3 - k, roll(part[k], -k), 0.0),
                          jnp.where((pos96 >= 3 + k) & (pos96 < 6), roll(part[k], k), 0.0))
    q = jnp.where(left96, roll(q, -3), roll(q, 3))
    for h in range(H):
        D[h] += jnp.where(edge96, roll(q, 125 - 8 * h), 0.0)

    def conv_edge(cb, _):
        cs = pl.ds(pl.multiple_of(cb * 8, 8), 8)
        inner = (0, 1, 2, H - 3, H - 2, H - 1)
        outer = (0, 1, 2, H + 3, H + 4, H + 5)
        acc = {h: D[h, cs, :] for h in inner}
        for b in range(7):
            rows = feature_rows(b, outer, cs)
            for a in range(7):
                w = wb_ref[7 * a + b, cs, :]
                for h in inner:
                    if h + a in rows:
                        acc[h] = acc[h] + w * rows[h + a]
        for h in inner:
            D[h, cs, :] = acc[h]
        return 0

    lax.fori_loop(0, NB, conv_edge, 0)

    fmc = jnp.concatenate([fm_ref[...]] * NB, axis=0)
    ones_row = jnp.where(lax.broadcasted_iota(jnp.int32, (W - C, 2 * W), 0) == 0, 1.0, 0.0)
    lanesets = [bufs[: len(bufs) // 2], bufs[len(bufs) // 2 :]]
    none = jnp.zeros((W - C, 2 * W), bf16)
    for XHL, YHL, *_ in lanesets:
        YHL[C:W, :] = none
        YHL[W + C :, :] = none
        XHL[C:XR, :] = ones_row.astype(bf16)
        XHL[XR + C :, :] = none
    GE[...] = jnp.zeros_like(GE)
    GS[...] = jnp.zeros_like(GS)
    ACC[...] = jnp.zeros_like(ACC)

    def stage_a(i, buf):
        XHL, YHL, U, DA, AHL, GHL, XN, RS = buf
        for q in range(2):
            h = 2 * i + q
            qs = slice(q * W, (q + 1) * W)
            x = D[h]
            m = jnp.mean(x, axis=0, keepdims=True)
            xc = x - m
            v = jnp.mean(xc * xc, axis=0, keepdims=True)
            rs = lax.rsqrt(v + EPS)
            xn = xc * rs
            XN[q] = xn
            RS[q] = jnp.broadcast_to(rs, (8, W))
            hi, lo = split(xn * pb_ref[2] + pb_ref[3])
            XHL[0:C, qs] = hi
            XHL[XR : XR + C, qs] = lo
            dy = cot_ref[pl.ds(h, C, stride=H), :] * fmc
            DY[h] = dy
            ACC[3] += dy
            hi, lo = split(dy)
            YHL[0:C, qs] = hi
            YHL[W : W + C, qs] = lo
        t = dot(up2_ref[...], XHL[...])
        U[...] = t[:HID] + t[HID:]
        t = dot(dnn2_ref[...], YHL[...])
        DA[...] = t[:HID] + t[HID:]

    def stage_b(buf):
        XHL, YHL, U, DA, AHL, GHL, XN, RS = buf
        for k in range(HID // CH):
            ks = slice(k * CH, (k + 1) * CH)
            kl = slice(HID + k * CH, HID + (k + 1) * CH)
            u = U[ks, :]
            x = 1.0 + (0.3275911 * 0.7071067811865476) * jnp.abs(u)
            t = pl.reciprocal(x, approx=True)
            t = t * (2.0 - x * t)
            e = jnp.exp2(-0.7213475204444817 * (u * u))
            poly = t * (0.5 * 0.254829592 + t * (0.5 * -0.284496736 + t * (0.5 * 1.421413741 + t * (0.5 * -1.453152027 + t * (0.5 * 1.061405429)))))
            q = poly * e
            phi = jnp.where(u >= 0.0, 1.0 - q, q)
            g = phi + (0.3989422804014327 * u) * e
            hi, lo = split(u * phi)
            AHL[ks, :] = hi
            AHL[kl, :] = lo
            hi, lo = split(DA[ks, :] * g)
            GHL[ks, :] = hi
            GHL[kl, :] = lo

    def stage_c(i, buf):
        XHL, YHL, U, DA, AHL, GHL, XN, RS = buf
        y = dot(dn3_ref[:, : 2 * HID], AHL[...]) + dot(dn3_ref[:, 2 * HID :], AHL[0:HID, :])
        for q in range(2):
            h = 2 * i + q
            OUT[pl.ds(h, C, stride=H), :] = fmc * (F[h + 3] + (y[:, q * W : (q + 1) * W] + pb_ref[4]))
        for total, wide, tall in ((GS, YHL, AHL), (GE, XHL, GHL)):
            t = dot(tall[0:HID, :], wide[...], NT)
            total[...] += t[:, :W] + (t[:, W:] + dot(tall[HID:, :], wide[0:W, :], NT))
        dx = dot(upn3_ref[:, : 2 * HID], GHL[...]) + dot(upn3_ref[:, 2 * HID :], GHL[0:HID, :])
        for q in range(2):
            h = 2 * i + q
            d = dx[:, q * W : (q + 1) * W]
            xn = XN[q]
            ACC[0] += d * xn
            ACC[1] += d
            d = d * pb_ref[2]
            m1 = jnp.mean(d, axis=0, keepdims=True)
            m2 = jnp.mean(d * xn, axis=0, keepdims=True)
            d = (d - m1 - xn * m2) * RS[q, 0:1, :]
            D[h] = d
            ACC[2] += d
            hi, lo = split(d)
            hs = pl.ds(pl.multiple_of(h * C, C), C)
            FHL[hs, 0:W] = hi
            FHL[hs, W:] = lo

    def tiles(i, _):
        b0, b1 = lanesets
        stage_a(2 * i, b0)
        stage_a(2 * i + 1, b1)
        stage_b(b0)
        stage_c(2 * i, b0)
        stage_b(b1)
        stage_c(2 * i + 1, b1)
        return 0

    cot_copy.wait()
    lax.fori_loop(0, H // 4, tiles, 0)
    out_copy = pltpu.make_async_copy(OUT, out_hbm, out_sem)
    out_copy.start()

    def shift_gradient():
        shift_rows(DSH, (0, 8 * C), 8 * C)

    def slot(v):
        return v // 48, v % 48 // 3, v % 3

    v = 0
    for total, count in ((GE, 13), (GS, 12)):
        for j in range(3):
            t = total[W * j : W * j + W, :].T
            for i in range(count):
                G[slot(v)] = t[8 * i : 8 * i + 8, :]
                v += 1
    while v < SLOTS:
        G[slot(v)] = jnp.zeros((8, W), f32)
        v += 1

    def rdma(src, dst, send, recv, to):
        return pltpu.make_async_remote_copy(
            src_ref=src, dst_ref=dst, send_sem=send, recv_sem=recv, device_id=to, device_id_type=MESH)

    sibling = (gy + 1 - 2 * core, gx)

    def c0():
        return rdma(G.at[1 - core], R0, s0, r0, sibling)

    def c1(i):
        m = (plane + i) & 15
        return rdma(B0.at[m], R1.at[i], s1.at[i], r1.at[i], at_plane(m, core))

    def c2(i):
        return rdma(B1, R2.at[z], s2.at[i], r2.at[i], at_z((z + i) & 7))

    def g2(i):
        j = (z - i) & 7
        return rdma(B1, R2.at[j], s2.at[i], r2.at[i], at_z(j))

    def c3(i):
        ref = sum_ref.at[core, plane]
        return rdma(ref, ref, s3.at[i], r3.at[i], at_plane((plane + i) & 15, core))

    def g3(i):
        m = (plane - i) & 15
        ref = sum_ref.at[core, m]
        return rdma(ref, ref, s3.at[i], r3.at[i], at_plane(m, core))

    def c4():
        ref = sum_ref.at[core]
        return rdma(ref, ref, s4, r4, sibling)

    def g4():
        ref = sum_ref.at[1 - core]
        return rdma(ref, ref, s4, r4, sibling)

    def step(k):
        if k == 0:
            c0().start()
        elif k == 1:
            c0().wait_recv()
            B0[...] = G[core] + R0[...]
            each(1, 16, lambda i: c1(i).start())
        elif k == 2:
            each(1, 16, lambda i: c1(i).wait_recv())
            acc = B0[plane]
            for i in range(1, 16):
                acc = acc + R1[i]
            B1[...] = acc
            R2[z] = acc
            each(1, 8, lambda i: c2(i).start())
        elif k == 3:
            each(1, 8, lambda i: g2(i).wait_recv())
            acc = R2[0]
            for j in range(1, 8):
                acc = acc + R2[j]
            sum_ref[core, plane] = acc
            each(1, 16, lambda i: c3(i).start())
        elif k == 4:
            each(1, 16, lambda i: g3(i).wait_recv())
            c4().start()
        else:
            g4().wait_recv()
            c0().wait_send()
            each(1, 16, lambda i: c1(i).wait_send())
            each(1, 8, lambda i: c2(i).wait_send())
            each(1, 16, lambda i: c3(i).wait_send())
            c4().wait_send()


    def back_block(cb, _):
        for k, when in enumerate(STEPS):
            @pl.when(cb == when)
            def _(k=k):
                step(k + 1)

        cs = pl.ds(pl.multiple_of(cb * 8, 8), 8)
        def gradient_rows(b):
            if b == 3:
                return [D[h, cs, :] for h in range(H)]
            n = SHIFTS.index(6 - b)
            return [DSH[n, h, cs, :] for h in range(H)]

        grads = jnp.zeros((8, W), f32)
        rows = [F[r, cs, :] for r in range(EXT)]
        for b in range(7):
            dd = gradient_rows(b)
            for a in range(7):
                if b == 3:
                    part = None
                elif b < 3:
                    part = jnp.where(left, SPX[3 * a + b, cs, :], 0.0)
                else:
                    part = jnp.where(left, 0.0, SPX[3 * a + 6 - b, cs, :])
                for h in range(H):
                    t = dd[h] * rows[h + a]
                    part = t if part is None else part + t
                total = jnp.sum(part, axis=1, keepdims=True)
                grads = jnp.where(lane == 7 * a + b, total, grads)
        acc = [DY[r - 3, cs, :] if 3 <= r < H + 3 else None for r in range(EXT)]
        for b in range(7):
            dd = gradient_rows(b)
            for a in range(7):
                w = wb_ref[7 * a + b, cs, :]
                for h in range(H):
                    t = w * dd[h]
                    acc[h + a] = t if acc[h + a] is None else acc[h + a] + t
        for k, src in enumerate((2, 0, 1, 3)):
            total = jnp.sum(ACC[src, cs, :], axis=1, keepdims=True)
            grads = jnp.where(lane == DEPTH_B + k, total, grads)
        total = DFS[0, cs, :] + DFS[1, cs, :]
        for r in range(EXT):
            t = acc[r]
            if r < 3:
                t = t * top_ok
            elif r >= H + 3:
                t = t * bot_ok
            DF[r, cs, :] = t
            total = total + t
        total = jnp.sum(total, axis=1, keepdims=True)
        GV[cs, :] = jnp.where(lane == STEM_B, total, grads)
        return 0

    step(0)
    shift_gradient()

    packed = jnp.zeros((C, W), f32)
    for h in range(H):
        packed = jnp.where(prow96 == h, roll(D[h], 8 * h + 3), packed)
    packed = jnp.where(left96, roll(packed, -3), jnp.where(right96, roll(packed, 3), 0.0))
    vs = [packed]
    for k in (1, 2):
        vs.append(jnp.where(left96, jnp.where(pos96 >= k, roll(packed, k), 0.0),
                            jnp.where(right96 & (pos96 < 6 - k), roll(packed, -k), 0.0)))
    o0 = jnp.zeros((C, W), f32)
    o1 = jnp.zeros((C, W), f32)
    for a in range(7):
        win = window(a, FS[0], FS[1])
        t = None
        for k in range(3):
            u = wbs_ref[3 * a + k] * vs[k]
            t = u if t is None else t + u
            SPX[3 * a + k] = vs[k] * win
        o0 = o0 + jnp.where((prow96 >= a) & (prow96 < 11), roll(t, 8 * a), 0.0)
        o1 = o1 + jnp.where(prow96 < 5 + a, roll(t, 8 * (a - 11)), 0.0)
    DFS[0] = o0 * jnp.concatenate([ok0] * NB, axis=0)
    DFS[1] = o1 * jnp.concatenate([ok1] * NB, axis=0)

    lax.fori_loop(0, NB, back_block, 0)
    step(len(STEPS) + 1)

    def rows2(p0, p1, d0, d1):
        ph, plo = split(jnp.concatenate([p0, p1], axis=1))
        dh, dlo = split(jnp.concatenate([d0, d1], axis=1))
        t = dot(jnp.concatenate([ph, plo], axis=0), dh, NT)
        return t[:KK] + (t[KK:] + dot(ph, dlo, NT))

    def okpat(p, ok):
        return p if ok is None else jnp.where(ok > 0.0, p, 0.0)

    def row_ok(r):
        return top_ok if r < 3 else bot_ok if r >= H + 3 else None

    okk = [jnp.concatenate([ok] * (KK // 8), axis=0) for ok in (ok0, ok1)]
    gstem = rows2(okpat(side_ref[0], okk[0]), okpat(side_ref[1], okk[1]), DFS[0], DFS[1])
    for r in range(0, EXT, 2):
        gstem = gstem + rows2(
            okpat(pat_ref[r], row_ok(r)), okpat(pat_ref[r + 1], row_ok(r + 1)), DF[r], DF[r + 1])

    zero = jnp.zeros((KK, W - C), f32)
    gs = jnp.concatenate([gstem, zero], axis=1)
    vec = jnp.concatenate([GV[...], jnp.zeros((W - C, W), f32)], axis=0).T
    tail = [gs[8 * i : 8 * i + 8, :] for i in range(6)] + [vec[8 * i : 8 * i + 8, :] for i in range(7)]
    for i, v in enumerate(tail):
        TG[i] = v
    for i in range(len(tail), TAIL):
        TG[i] = jnp.zeros((8, W), f32)

    def owner(v):
        return at_plane(v, v & 1)

    mine = (plane & 1) == core

    def t1(v):
        return rdma(TG.at[v], TR.at[plane, core], ts1.at[v], tr1.at[plane, core], owner(v))

    def w1(m, c):
        return rdma(TP, TR.at[m, c], ts1.at[0], tr1.at[m, c], at_plane(m, c))

    def t2(i):
        return rdma(TP, TX.at[z], ts2.at[i], tr2.at[i], at_z((z + i) & 7))

    def w2(i):
        j = (z - i) & 7
        return rdma(TP, TX.at[j], ts2.at[i], tr2.at[i], at_z(j))

    def t3(m, c):
        ref = tail_ref.at[plane]
        return rdma(ref, ref, ts3.at[m, c], tr3.at[plane], at_plane(m, c))

    def w3(v):
        ref = tail_ref.at[v]
        return rdma(ref, ref, ts3.at[0, 0], tr3.at[v], owner(v))

    def others(f):
        def one(i):
            m, c = i >> 1, i & 1
            @pl.when((m != plane) | (c != core))
            def _():
                f(m, c)
        each(0, 32, one)

    def foreign(f):
        def one(v):
            @pl.when((v != plane) | ((v & 1) != core))
            def _():
                f(v)
        each(0, TAIL, one)

    foreign(lambda v: t1(v).start())

    @pl.when(mine)
    def _():
        TR[plane, core] = TG[plane]
        others(lambda m, c: w1(m, c).wait_recv())
        acc = TR[0, 0]
        for i in range(1, 32):
            acc = acc + TR[i >> 1, i & 1]
        TP[...] = acc
        TX[z] = acc
        each(1, 8, lambda i: t2(i).start())

    step(len(STEPS) + 2)

    @pl.when(mine)
    def _():
        each(1, 8, lambda i: w2(i).wait_recv())
        acc = TX[0]
        for j in range(1, 8):
            acc = acc + TX[j]
        tail_ref[plane] = acc
        others(lambda m, c: t3(m, c).start())

    step(len(STEPS) + 3)
    foreign(lambda v: t1(v).wait_send())
    step(len(STEPS) + 4)
    foreign(lambda v: w3(v).wait_recv())

    @pl.when(mine)
    def _():
        each(1, 8, lambda i: t2(i).wait_send())
        others(lambda m, c: t3(m, c).wait_send())

    out_copy.wait()
    for group in range(len(GROUPS)):
        for bucket_at in range(2):
            tile_copy(bucket_at, group).wait_send()
    row_copy(True).wait_send()
    row_copy(False).wait_send()
    for i in range(len(NEAR)):
        edge_copy(i).wait_send()
    for group in (1, 2):
        for i in range(2):
            mid_copy(group, i).wait_send()


def whole_call(*args):
    vm = pl.BlockSpec(memory_space=pltpu.VMEM)
    hbm = pl.BlockSpec(memory_space=pltpu.HBM)
    s = jax.ShapeDtypeStruct
    n_send = INFO + 3 * H
    near = len(NEAR)

    def v(*shape, dtype=f32):
        return pltpu.VMEM(shape, dtype)

    buf = [
        v(2 * XR, 2 * W, dtype=bf16), v(2 * W, 2 * W, dtype=bf16), v(HID, 2 * W), v(HID, 2 * W),
        v(2 * HID, 2 * W, dtype=bf16), v(2 * HID, 2 * W, dtype=bf16), v(2, C, W), v(2, 8, W),
    ]
    return pl.pallas_call(
        whole_kernel,
        out_shape=(s((C * H, W), f32), s((2, 16, 3, 8, W), f32), s((TAIL, 8, W), f32)),
        in_specs=[hbm] * 14,
        out_specs=[hbm, vm, vm],
        scratch_shapes=[
            v(EXT, KK, W), v(2, KK, W), v(8, W), v(TAPS, C, W), v(21, C, W), v(5, C, W),
            v(C, 3 * KK, dtype=bf16), v(2 * HID, 2 * XR, dtype=bf16), v(2 * HID, 2 * W, dtype=bf16),
            v(C, 3 * HID, dtype=bf16), v(C, 3 * HID, dtype=bf16),
            v(8, PIX), v(1, 8, dtype=jnp.int32), v(1, 8, dtype=jnp.int32),
            v(KK, C), v(TAPS, C), v(1, C), v(1, C), v(1, C), v(1, C), v(C, HID), v(HID), v(C, HID), v(1, C),
            v(2, n_send, 8, W), v(2, n_send, 8, W), v(3, KK, W), v(near, KK, W), v(2, 2, KK, W), v(W, W), v(C * H, W),
            DMA((12,)), DMA((12,)), DMA((2, 3)), DMA((2, 3)), DMA((2,)), DMA((2,)),
            DMA((near,)), DMA((near,)), DMA((2, 2)), DMA((2, 2)), DMA(()), DMA(()),
            v(EXT, C, W), v(2, C, W), v(H, C, W), v(6, H, C, W), v(H, C, W), v(HID, W), v(HID, W), v(4, C, W),
            v(EXT * C, 2 * W, dtype=bf16), v(6, EXT, C, W), v(2 * W, 6 * W, dtype=bf16), v(C * H, W),
            v(2, 16, 3, 8, W), v(16, 3, 8, W), v(16, 3, 8, W), v(16, 3, 8, W), v(3, 8, W), v(8, 3, 8, W),
            v(TAIL, 8, W), v(16, 2, 8, W), v(8, W), v(8, 8, W), v(EXT, C, W), v(2, C, W), v(C, W),
            DMA(()), DMA(()), DMA((16,)), DMA((16,)), DMA((8,)), DMA((8,)), DMA((16,)), DMA((16,)), DMA(()), DMA(()),
            DMA((TAIL,)), DMA((16, 2)), DMA((8,)), DMA((8,)), DMA((16, 2)), DMA((TAIL,)), v(21, C, W),
            *buf, *buf,
        ],
        compiler_params=pltpu.CompilerParams(
            collective_id=0, has_side_effects=True, vmem_limit_bytes=56 * 1024 * 1024),
        name="whole",
    )(*args)


PIECES = 4


def unpack_kernel(
    sum_hbm, tail_hbm, block_hbm, out_hbm, gstem_ref, gstem_b_ref, gdepth_ref, gdepth_b_ref, ggain_ref, gnbias_ref,
    gexp_ref, gexp_b_ref, gshr_ref, gshr_b_ref, held, sum_ref, tail_ref, sem,
):
    rows = C * H // PIECES

    def piece(i, back):
        at = pl.ds(i * rows, rows)
        if back:
            return pltpu.make_async_copy(held.at[at], out_hbm.at[at], sem.at[1, i])
        return pltpu.make_async_copy(block_hbm.at[at], held.at[at], sem.at[0, i])

    total = pltpu.make_async_copy(sum_hbm, sum_ref, sem.at[2, 0])
    last = pltpu.make_async_copy(tail_hbm, tail_ref, sem.at[2, 1])
    total.start()
    last.start()
    for i in range(PIECES):
        piece(i, False).start()
    total.wait()
    last.wait()

    def at(v):
        return sum_ref[v // 48, v % 48 // 3, v % 3]

    v = 0
    for j in range(3):
        for i in range(12):
            gexp_ref[8 * i : 8 * i + 8, W * j : W * j + W] = at(v)
            v += 1
        gexp_b_ref[W * j : W * j + W] = at(v)[0]
        v += 1
    for j in range(3):
        for i in range(12):
            gshr_ref[8 * i : 8 * i + 8, W * j : W * j + W] = at(v)
            v += 1
    for i in range(PIECES):
        piece(i, False).wait()
        piece(i, True).start()
    for i in range(6):
        gstem_ref[8 * i : 8 * i + 8, :] = tail_ref[i][:, :C]
        gdepth_ref[8 * i : 8 * i + 8, :] = tail_ref[6 + i][:, :C]
    last = tail_ref[12][:, :C]
    gdepth_ref[48:49, :] = last[0:1]
    for k, ref in enumerate((gstem_b_ref, gdepth_b_ref, ggain_ref, gnbias_ref, gshr_b_ref)):
        ref[...] = last[k + 1 : k + 2]
    for i in range(PIECES):
        piece(i, True).wait()


def unpack_call(block, total, tail):
    vm = pl.BlockSpec(memory_space=pltpu.VMEM)
    hbm = pl.BlockSpec(memory_space=pltpu.HBM)
    shapes = ((KK, C), (1, C), (TAPS, C), (1, C), (1, C), (1, C), (C, HID), (HID,), (C, HID), (1, C))
    return pl.pallas_call(
        unpack_kernel,
        out_shape=tuple(jax.ShapeDtypeStruct(s, f32) for s in ((C * H, W),) + shapes),
        in_specs=[hbm] * 3,
        out_specs=[hbm] + [vm] * len(shapes),
        scratch_shapes=[
            pltpu.VMEM((C * H, W), f32), pltpu.VMEM((2, 16, 3, 8, W), f32), pltpu.VMEM((TAIL, 8, W), f32), DMA((3, PIECES))],
        compiler_params=pltpu.CompilerParams(vmem_limit_bytes=56 * 1024 * 1024),
        name="unpack",
    )(total, tail, block)


def local(
    stored_tiles, tile_target, tile_mask,
    stem_weight, stem_bias, depth_weight, depth_bias, norm_gain, norm_bias,
    expand_weight, expand_bias, shrink_weight, shrink_bias, cotangent,
):
    def row(v):
        return v.reshape(1, -1)

    block, total, tail = whole_call(
        stored_tiles[0], tile_target, tile_mask, stem_weight, depth_weight, row(stem_bias), row(depth_bias),
        row(norm_gain), row(norm_bias), expand_weight, expand_bias, shrink_weight.T, row(shrink_bias),
        cotangent.reshape(C * H, W))
    out, gs, gsb, gd, gdb, gg, gn, ge, geb, gh, ghb = unpack_call(block, total, tail)
    return (
        out.reshape(C, H, W), gs, gsb[0], gd, gdb[0], gg[0], gn[0], ge, geb, gh.T, ghb[0],
    )


def solution(mesh):
    placed = (P("gy", "gx", None), P("gy", "gx"), P("gy", "gx")) + (P(),) * 10 + (P(None, "gy", "gx"),)
    return jax.shard_map(
        local, mesh=mesh, in_specs=placed,
        out_specs=(P(None, "gy", "gx"),) + (P(),) * 10,
        check_vma=False,
    )
```

```python
import jax
import jax.numpy as jnp
from jax import lax
from jax.experimental import pallas as pl
from jax.experimental.pallas import tpu as pltpu
from jax.sharding import PartitionSpec as P

C = 96
HID = 384
NB = C // 8
H = 16
W = 128
EXT = H + 6
KK = 48
TAPS = 49
PIX = 12288
f32 = jnp.float32
bf16 = jnp.bfloat16
EPS = 1e-6
MESH = pl.DeviceIdType.MESH
DMA = pltpu.SemaphoreType.DMA

NN = (((1,), (0,)), ((), ()))
NT = (((1,), (1,)), ((), ()))


def split(x):
    hi = x.astype(bf16)
    return hi, (x - hi.astype(f32)).astype(bf16)


def dot(a, b, dims=NN):
    return lax.dot_general(a, b, dims, preferred_element_type=f32)


def lanes(shape=(8, W)):
    return lax.broadcasted_iota(jnp.int32, shape, len(shape) - 1)


def roll(x, by):
    by = by % W
    return x if by == 0 else pltpu.roll(x, by, x.ndim - 1)


STEM_B, DEPTH_B, GAIN, NBIAS, SHRINK_B = 49, 50, 51, 52, 53
GROUPS = ((0, 1, 2, 13, 14, 15), (3, 4, 5, 6, 7, 8), (9, 10, 11, 12))
ORDER = tuple(h for group in GROUPS for h in group)
INFO = 2
NEAR = ((0, -1), (0, 1), (-1, -1), (-1, 1), (1, -1), (1, 1))


def payload_range(group):
    before = sum(len(g) for g in GROUPS[:group])
    after = before + len(GROUPS[group])
    return (0 if group == 0 else INFO + 3 * before), INFO + 3 * after


def row_ranges(group):
    rows = GROUPS[group]
    if group == 0:
        return ((rows[0], 3), (rows[3], 3))
    return ((rows[0], len(rows)),)


def take(x, index, axis):
    return jnp.take_along_axis(x, index, axis=axis)


def each(low, high, f):
    def one(i, _):
        f(i)
        return 0
    lax.fori_loop(low, high, one, 0)


XR = W
CH = 16
SLOTS = 96
TAIL = 13
SHIFTS = (0, 1, 2, 4, 5, 6)
STEPS = (3,)

def validity(gy, gx):
    ny = lax.axis_size("gy")
    nx = lax.axis_size("gx")
    lane = lanes()
    pos = lane & 7
    prow = lane >> 3
    top_ok = (gy > 0).astype(f32)
    bot_ok = (gy < ny - 1).astype(f32)
    left_ok = (gx > 0).astype(f32)
    right_ok = (gx < nx - 1).astype(f32)
    col_ok = jnp.where(pos < 3, left_ok, jnp.where(pos < 6, right_ok, 0.0))
    col_ok = jnp.where(prow < 11, col_ok, 0.0)
    ok0 = col_ok * jnp.where(prow < 3, top_ok, 1.0)
    ok1 = col_ok * jnp.where(prow >= 8, bot_ok, 1.0)
    return top_ok, bot_ok, ok0, ok1


def whole_kernel(
    tiles_hbm, target_hbm, marks_hbm, stem_hbm, dw_hbm, sb_hbm, db_hbm, ga_hbm, nb_hbm, ew_hbm, eb_hbm, sw_hbm, hb_hbm, cot_hbm,
    out_hbm, sum_ref, tail_ref,
    pat_ref, side_ref, fm_ref, wb_ref, wbs_ref, pb_ref, stem3_ref, up2_ref, dnn2_ref, dn3_ref, upn3_ref, tiles,
    target, marks, stem_v, dw_v, sb_v, db_v, ga_v, nb_v, ew_v, eb_v, sw_v, hb_v, send, recv, edge, edges,
    edges_mid, ct, cot_ref, in_sem, par_sem, tile_send, tile_recv, row_send, row_recv, edge_send, edge_recv,
    mid_send, mid_recv, cot_sem, out_sem, F, FS, D, DSH, DY, GE, GS, ACC, FHL, FSH, SH, OUT, G, R0, B0, R1, B1,
    R2, TG, TR, TP, TX, DF, DFS, GV, s0, r0, s1, r1, s2, r2, s3, r3, s4, r4, ts1, tr1, ts2, tr2, ts3, tr3, SPX, *bufs,
):
    gy = lax.axis_index("gy")
    gx = lax.axis_index("gx")
    ny = lax.axis_size("gy")
    nx = lax.axis_size("gx")

    def device(dy, dx):
        return (lax.rem(gy + dy + ny, ny), lax.rem(gx + dx + nx, nx))

    y_hi, xx, core = gy >> 3, (gy >> 1) & 3, gy & 1
    y_lo, z = gx >> 3, gx & 7
    plane = (y_hi * 2 + y_lo) * 4 + xx

    def at_plane(m, c):
        return ((m >> 3) * 8 + (m & 3) * 2 + c, ((m >> 2) & 1) * 8 + z)

    def at_z(j):
        return (gy, y_lo * 8 + j)

    barrier = pltpu.get_barrier_semaphore()

    def greet(to):
        pl.semaphore_signal(barrier, inc=1, device_id=to, device_id_type=MESH)

    peers = [(0, 1), (0, -1), (0, 9), (0, -9)] + [(dy, dx) for dy in (-1, 1) for dx in (-1, 0, 1)]
    for dy, dx in peers:
        greet(device(dy, dx))
    each(1, 16, lambda i: greet(at_plane((plane + i) & 15, core)))
    each(0, 16, lambda i: greet(at_plane((plane + i) & 15, 1 - core)))
    each(1, 8, lambda i: greet(at_z((z + i) & 7)))
    greetings = len(peers) + 15 + 16 + 7

    params = [
        pltpu.make_async_copy(src, dst, par_sem.at[i])
        for i, (src, dst) in enumerate((
            (target_hbm, target), (marks_hbm, marks), (stem_hbm, stem_v), (dw_hbm, dw_v), (sb_hbm, sb_v),
            (db_hbm, db_v), (ga_hbm, ga_v), (nb_hbm, nb_v), (ew_hbm, ew_v), (eb_hbm, eb_v), (sw_hbm, sw_v),
            (hb_hbm, hb_v)))
    ]
    params[0].start()
    params[1].start()
    loads = []
    for group in range(len(GROUPS)):
        for lo, n in row_ranges(group):
            for k in range(3):
                at = pl.ds(k * 4096 + lo * 256, n * 256)
                loads.append((group, pltpu.make_async_copy(
                    tiles_hbm.at[:, at], tiles.at[:, at], in_sem.at[len(loads)])))
                loads[-1][1].start()
    for copy in params[2:]:
        copy.start()
    cot_copy = pltpu.make_async_copy(cot_hbm, cot_ref, cot_sem)
    cot_copy.start()

    sub = lax.broadcasted_iota(jnp.int32, (8, W), 0)
    lane = lanes()
    row8 = lax.broadcasted_iota(jnp.int32, (8, 8), 0)
    col8 = lax.broadcasted_iota(jnp.int32, (8, 8), 1)
    eye = row8 == col8
    params[0].wait()
    params[1].wait()

    def down_column(row):
        return jnp.sum(jnp.where(eye, row, 0.0), axis=1, keepdims=True)

    codes = jnp.broadcast_to(target[...], (8, 8))
    bucket = ((((codes >> 3) - gx - 1) & 15) >> 3).astype(f32)
    place = (codes & 7).astype(f32)
    mark = jnp.broadcast_to(marks[...], (8, 8)).astype(f32)
    bucket_col = down_column(bucket)
    rank = jnp.sum(jnp.where((bucket_col == bucket) & (row8 < col8), 1.0, 0.0), axis=0, keepdims=True)
    slot_pos = bucket[0:1, :] * 4.0 + rank

    def sources(wanted):
        return jnp.sum(jnp.where(slot_pos == wanted.astype(f32), col8.astype(f32), 0.0), axis=1, keepdims=True)

    order = jnp.broadcast_to(sources(row8), (8, W)).astype(jnp.int32)
    turned = jnp.broadcast_to(sources((row8 + 4) & 7), (8, W)).astype(jnp.int32)
    place_col = jnp.broadcast_to(down_column(place), (8, W))
    mark_col = jnp.broadcast_to(down_column(mark), (8, W))
    low = sub < 4

    def put(q, x0, x1):
        g0 = take(x0, order, 0)
        g1 = take(x1, turned, 0)
        send[0, q] = jnp.where(low, g0, g1)
        send[1, q] = jnp.where(low, g1, g0)

    def tile_copy(bucket_at, group):
        lo, hi = payload_range(group)
        return pltpu.make_async_remote_copy(
            src_ref=send.at[bucket_at, pl.ds(lo, hi - lo)],
            dst_ref=recv.at[bucket_at, pl.ds(lo, hi - lo)],
            send_sem=tile_send.at[bucket_at, group],
            recv_sem=tile_recv.at[bucket_at, group],
            device_id=device(0, 1 + 8 * bucket_at),
            device_id_type=MESH,
        )

    pos = lane & 7
    left = pos < 3

    def prepare():
        src = lax.broadcasted_iota(jnp.int32, (2 * W, W), 0) & (W - 1)
        dst = lax.broadcasted_iota(jnp.int32, (2 * W, W), 1)
        for n, b in enumerate(SHIFTS):
            SH[:, n * W : (n + 1) * W] = jnp.where(src == dst + (b - 3), 1.0, 0.0).astype(bf16)

        for copy in params[2:]:
            copy.wait()
        ct[...] = jnp.zeros_like(ct)
        ct[0:TAPS, 0:C] = dw_v[...]
        for k, ref in enumerate((sb_v, db_v, ga_v, nb_v, hb_v)):
            ct[STEM_B + k : STEM_B + k + 1, 0:C] = ref[...]
        cols = ct[...].T
        ct[...] = cols

        def spread(cb, _):
            cs = pl.ds(pl.multiple_of(cb * 8, 8), 8)
            wc = ct[cs, :]
            for a in range(7):
                taps = []
                for b in range(7):
                    t = 7 * a + b
                    taps.append(jnp.broadcast_to(wc[:, t : t + 1], (8, W)))
                    wb_ref[t, cs, :] = taps[-1]
                for k in range(3):
                    wbs_ref[3 * a + k, cs, :] = jnp.where(left, taps[k], taps[6 - k])
            for k in range(5):
                pb_ref[k, cs, :] = jnp.broadcast_to(wc[:, STEM_B + k : STEM_B + k + 1], (8, W))
            return 0

        lax.fori_loop(0, NB, spread, 0)

        def turned_over(x):
            n = x.shape[0]
            return jnp.concatenate([x, jnp.zeros((W - n, x.shape[1]), f32)], axis=0).T

        stem_pad = jnp.concatenate([stem_v[...], jnp.zeros((KK, W - C), f32)], axis=1)
        hi, lo = split(turned_over(stem_pad)[:C, :KK])
        stem3_ref[:, 0:KK] = hi
        stem3_ref[:, KK : 2 * KK] = hi
        stem3_ref[:, 2 * KK :] = lo
        ew = ew_v[...]
        sw = sw_v[...]
        for src, ref in ((sw, dn3_ref), (ew, upn3_ref)):
            hi, lo = split(src)
            ref[:, 0:HID] = hi
            ref[:, HID : 2 * HID] = hi
            ref[:, 2 * HID :] = lo
        hi, lo = split(turned_over(sw)[:, :C])
        dnn2_ref[0:HID, 0:C] = hi
        dnn2_ref[0:HID, W : W + C] = hi
        dnn2_ref[HID:, 0:C] = lo
        dnn2_ref[HID:, W:] = jnp.zeros((HID, W), bf16)
        dnn2_ref[:, C:W] = jnp.zeros((2 * HID, W - C), bf16)
        dnn2_ref[0:HID, W + C :] = jnp.zeros((HID, W - C), bf16)
        up = jnp.concatenate([ew, eb_v[...].reshape(1, HID), jnp.zeros((W - C - 1, HID), f32)], axis=0).T
        hi, lo = split(up[:, : W])
        up2_ref[0:HID, 0 : W] = hi
        up2_ref[0:HID, W :] = hi
        up2_ref[HID:, 0 : W] = lo
        up2_ref[HID:, W :] = jnp.zeros((HID, W), bf16)


    put(0, place_col, place_col)
    put(1, mark_col, mark_col)
    for group, rows in enumerate(GROUPS):
        for at, copy in loads:
            if at == group:
                copy.wait()
        for h in rows:
            for k in range(3):
                r = k * 32 + h * 2
                x0 = tiles[:, r * W : (r + 1) * W] * mark_col
                x1 = tiles[:, (r + 1) * W : (r + 2) * W] * mark_col
                put(INFO + 3 * ORDER.index(h) + k, x0, x1)
        if group > 0:
            for bucket_at in range(2):
                tile_copy(bucket_at, group).start()
            continue
        pl.semaphore_wait(barrier, greetings)
        for bucket_at in range(2):
            tile_copy(bucket_at, group).start()

    prepare()
    top_ok, bot_ok, ok0, ok1 = validity(gy, gx)

    def stem_of(p, bias):
        hi, lo = split(p)
        return dot(stem3_ref[...], jnp.concatenate([hi, lo, hi], axis=0)) + bias

    bias2 = jnp.concatenate([pb_ref[0], pb_ref[0]], axis=1)

    def row_ok(r):
        return top_ok if r < 3 else bot_ok if r >= H + 3 else None

    def stem_pair(pair):
        parts = []
        for q in range(2):
            ok = row_ok(pair[q])
            p = pat_ref[pair[q]]
            parts.append(p if ok is None else jnp.where(ok > 0.0, p, 0.0))
        y = stem_of(jnp.concatenate(parts, axis=1), bias2)
        for q in range(2):
            r = pair[q]
            ok = row_ok(r)
            v = y[:, q * W : (q + 1) * W]
            if ok is not None:
                v = v * ok
            F[r] = v
            hi, lo = split(v)
            FHL[r * C : (r + 1) * C, 0:W] = hi
            FHL[r * C : (r + 1) * C, W:] = lo
    def shift_rows(ref, starts, rows):
        for n in range(3):
            for at in starts:
                y = dot(FHL[at : at + rows, :], SH[:, 2 * n * W : (2 * n + 2) * W])
                for r in range(rows // C):
                    ref[2 * n, at // C + r] = y[r * C : (r + 1) * C, :W]
                    ref[2 * n + 1, at // C + r] = y[r * C : (r + 1) * C, W:]

    w16 = lane & 15
    beta = lane >> 4
    prow = lane >> 3

    def row_copy(up):
        src, dst, dy = (3, H + 3, -1) if up else (H, 0, 1)
        return pltpu.make_async_remote_copy(
            src_ref=pat_ref.at[pl.ds(src, 3)],
            dst_ref=pat_ref.at[pl.ds(dst, 3)],
            send_sem=row_send.at[int(up)],
            recv_sem=row_recv.at[int(up)],
            device_id=device(dy, 0),
            device_id_type=MESH,
        )

    def edge_copy(i):
        dy, dx = NEAR[i]
        return pltpu.make_async_remote_copy(
            src_ref=edge.at[0], dst_ref=edges.at[i], send_sem=edge_send.at[i], recv_sem=edge_recv.at[i],
            device_id=device(dy, dx), device_id_type=MESH)

    def mid_copy(group, i):
        dy, dx = NEAR[i]
        return pltpu.make_async_remote_copy(
            src_ref=edge.at[group], dst_ref=edges_mid.at[group - 1, i],
            send_sem=mid_send.at[group - 1, i], recv_sem=mid_recv.at[group - 1, i],
            device_id=device(dy, dx), device_id_type=MESH)

    for group, rows in enumerate(GROUPS):
        for bucket_at in range(2):
            tile_copy(bucket_at, group).wait_recv()
        if group == 0:
            places = (recv[0, 0], recv[1, 0])
            marks_in = (recv[0, 1], recv[1, 1])
            first = []
            for p in places:
                g = (beta - p.astype(jnp.int32)) & 7
                first.append((g >> 2) * 64 + w16 * 4 + (g & 3))
            wanted = ((beta - sub) & 7).astype(f32)
            wanted_t = beta.astype(f32)
            found = []
            fm = jnp.zeros((8, W), f32)
            for j, off in ((0, 0), (1, 4)):
                at = jnp.zeros((8, W), f32)
                hit = jnp.zeros((8, W), f32)
                for k in range(4):
                    p = jnp.broadcast_to(places[j][off + k : off + k + 1, :], (8, W))
                    m = jnp.broadcast_to(marks_in[j][off + k : off + k + 1, :], (8, W))
                    at = jnp.where(p == wanted, float(k), at)
                    hit = jnp.where(p == wanted, 1.0, hit)
                    fm = jnp.where(p == wanted_t, m, fm)
                found.append((at.astype(jnp.int32), hit))
            fm_ref[...] = fm
            in_a = found[0][1] > 0.0
            second = [(found[0][0] + 4 * a, found[1][0] + 4 * (1 - a)) for a in range(2)]
            third = ((sub + beta) & 7) * 16 + w16
        for h in rows:
            for k in range(3):
                q = INFO + 3 * ORDER.index(h) + k
                ya = take(recv[0, q], first[0], 1)
                yb = take(recv[1, q], first[1], 1)
                for a in range(2):
                    v = jnp.where(in_a, take(ya, second[a][0], 0), take(yb, second[a][1], 0))
                    pat_ref[h + 3, pl.ds(16 * k + 8 * a, 8), :] = take(v, third, 1)
        if group == 0:
            row_copy(True).start()
            row_copy(False).start()
        for j in range(KK // 8):
            js = pl.ds(8 * j, 8)
            v = jnp.zeros((8, W), f32)
            for h in rows:
                v = jnp.where(prow == h, roll(pat_ref[h + 3, js, :], 8 * h + 3), v)
            edge[group, js, :] = v
        if group == 0:
            for i in range(len(NEAR)):
                edge_copy(i).start()
        else:
            for i in range(2):
                mid_copy(group, i).start()
        for n in range(0, len(rows), 2):
            stem_pair((rows[n] + 3, rows[n + 1] + 3))
        for lo, n in row_ranges(group):
            shift_rows(FSH, ((lo + 3) * C,), n * C)

    def feature_rows(b, which, cs):
        if b == 3:
            return {r: F[r, cs, :] for r in which}
        return {r: FSH[SHIFTS.index(b), r, cs, :] for r in which}

    def conv_block(cb, _):
        cs = pl.ds(pl.multiple_of(cb * 8, 8), 8)
        acc = [pb_ref[1, cs, :]] * H
        for b in range(7):
            rows = feature_rows(b, range(3, H + 3), cs)
            for a in range(7):
                w = wb_ref[7 * a + b, cs, :]
                for h in range(H):
                    if h + a in rows:
                        acc[h] = acc[h] + w * rows[h + a]
        for h in range(H):
            D[h, cs, :] = acc[h]
        return 0

    lax.fori_loop(0, NB, conv_block, 0)

    for i in range(len(NEAR)):
        edge_copy(i).wait_recv()
    for group in (1, 2):
        for i in range(2):
            mid_copy(group, i).wait_recv()
    up_left, up_right = edges.at[5], edges.at[4]
    down_left, down_right = edges.at[3], edges.at[2]
    for j in range(KK // 8):
        js = pl.ds(8 * j, 8)
        from_left = edges[1, js, :] + (edges_mid[0, 1, js, :] + edges_mid[1, 1, js, :])
        from_right = edges[0, js, :] + (edges_mid[0, 0, js, :] + edges_mid[1, 0, js, :])
        mid = jnp.where(left, from_left, from_right)
        top = jnp.where(left, up_left[js, :], up_right[js, :])
        bottom = jnp.where(left, down_left[js, :], down_right[js, :])
        side_ref[0, js, :] = jnp.where(prow < 3, roll(top, -104), roll(mid, 24))
        side_ref[1, js, :] = jnp.where(prow < 8, roll(mid, -64), roll(bottom, 64))
    row_copy(True).wait_recv()
    row_copy(False).wait_recv()
    for r in (0, 2, 20):
        stem_pair((r, r + 1) if r != 2 else (2, 19))
    parts = []
    for i, ok in enumerate((ok0, ok1)):
        okk = jnp.concatenate([ok] * (KK // 8), axis=0)
        parts.append(jnp.where(okk > 0.0, side_ref[i], 0.0))
    y = stem_of(jnp.concatenate(parts, axis=1), bias2)
    for i, ok in enumerate((ok0, ok1)):
        FS[i] = y[:, i * W : (i + 1) * W] * jnp.concatenate([ok] * NB, axis=0)

    for r in (0, H + 3):
        shift_rows(FSH, (r * C,), 3 * C)

    def window(a, lo, hi):
        return jnp.where(prow96 < 11 - a, roll(lo, -8 * a), roll(hi, 8 * (11 - a)))

    lane96 = lanes((C, W))
    pos96 = lane96 & 7
    prow96 = lane96 >> 3
    left96 = pos96 < 3
    right96 = (pos96 >= 3) & (pos96 < 6)
    edge96 = (lane96 < 3) | (lane96 >= W - 3)
    part = [None] * 3
    for a in range(7):
        win = window(a, FS[0], FS[1])
        for k in range(3):
            t = wbs_ref[3 * a + k] * win
            part[k] = t if part[k] is None else part[k] + t
    q = part[0]
    for k in (1, 2):
        q = q + jnp.where(left96, jnp.where(pos96 < 3 - k, roll(part[k], -k), 0.0),
                          jnp.where((pos96 >= 3 + k) & (pos96 < 6), roll(part[k], k), 0.0))
    q = jnp.where(left96, roll(q, -3), roll(q, 3))
    for h in range(H):
        D[h] += jnp.where(edge96, roll(q, 125 - 8 * h), 0.0)

    def conv_edge(cb, _):
        cs = pl.ds(pl.multiple_of(cb * 8, 8), 8)
        inner = (0, 1, 2, H - 3, H - 2, H - 1)
        outer = (0, 1, 2, H + 3, H + 4, H + 5)
        acc = {h: D[h, cs, :] for h in inner}
        for b in range(7):
            rows = feature_rows(b, outer, cs)
            for a in range(7):
                w = wb_ref[7 * a + b, cs, :]
                for h in inner:
                    if h + a in rows:
                        acc[h] = acc[h] + w * rows[h + a]
        for h in inner:
            D[h, cs, :] = acc[h]
        return 0

    lax.fori_loop(0, NB, conv_edge, 0)

    fmc = jnp.concatenate([fm_ref[...]] * NB, axis=0)
    ones_row = jnp.where(lax.broadcasted_iota(jnp.int32, (W - C, 2 * W), 0) == 0, 1.0, 0.0)
    lanesets = [bufs[: len(bufs) // 2], bufs[len(bufs) // 2 :]]
    none = jnp.zeros((W - C, 2 * W), bf16)
    for XHL, YHL, *_ in lanesets:
        YHL[C:W, :] = none
        YHL[W + C :, :] = none
        XHL[C:XR, :] = ones_row.astype(bf16)
        XHL[XR + C :, :] = none
    GE[...] = jnp.zeros_like(GE)
    GS[...] = jnp.zeros_like(GS)
    ACC[...] = jnp.zeros_like(ACC)

    def stage_a(i, buf):
        XHL, YHL, U, DA, AHL, GHL, XN, RS = buf
        for q in range(2):
            h = 2 * i + q
            qs = slice(q * W, (q + 1) * W)
            x = D[h]
            m = jnp.mean(x, axis=0, keepdims=True)
            xc = x - m
            v = jnp.mean(xc * xc, axis=0, keepdims=True)
            rs = lax.rsqrt(v + EPS)
            xn = xc * rs
            XN[q] = xn
            RS[q] = jnp.broadcast_to(rs, (8, W))
            hi, lo = split(xn * pb_ref[2] + pb_ref[3])
            XHL[0:C, qs] = hi
            XHL[XR : XR + C, qs] = lo
            dy = cot_ref[pl.ds(h, C, stride=H), :] * fmc
            DY[h] = dy
            ACC[3] += dy
            hi, lo = split(dy)
            YHL[0:C, qs] = hi
            YHL[W : W + C, qs] = lo
        t = dot(up2_ref[...], XHL[...])
        U[...] = t[:HID] + t[HID:]
        t = dot(dnn2_ref[...], YHL[...])
        DA[...] = t[:HID] + t[HID:]

    def stage_b(buf):
        XHL, YHL, U, DA, AHL, GHL, XN, RS = buf
        for k in range(HID // CH):
            ks = slice(k * CH, (k + 1) * CH)
            kl = slice(HID + k * CH, HID + (k + 1) * CH)
            u = U[ks, :]
            x = 1.0 + (0.3275911 * 0.7071067811865476) * jnp.abs(u)
            t = pl.reciprocal(x, approx=True)
            t = t * (2.0 - x * t)
            e = jnp.exp2(-0.7213475204444817 * (u * u))
            poly = t * (0.5 * 0.254829592 + t * (0.5 * -0.284496736 + t * (0.5 * 1.421413741 + t * (0.5 * -1.453152027 + t * (0.5 * 1.061405429)))))
            q = poly * e
            phi = jnp.where(u >= 0.0, 1.0 - q, q)
            g = phi + (0.3989422804014327 * u) * e
            hi, lo = split(u * phi)
            AHL[ks, :] = hi
            AHL[kl, :] = lo
            hi, lo = split(DA[ks, :] * g)
            GHL[ks, :] = hi
            GHL[kl, :] = lo

    def stage_c(i, buf):
        XHL, YHL, U, DA, AHL, GHL, XN, RS = buf
        y = dot(dn3_ref[:, : 2 * HID], AHL[...]) + dot(dn3_ref[:, 2 * HID :], AHL[0:HID, :])
        for q in range(2):
            h = 2 * i + q
            OUT[pl.ds(h, C, stride=H), :] = fmc * (F[h + 3] + (y[:, q * W : (q + 1) * W] + pb_ref[4]))
        for total, wide, tall in ((GS, YHL, AHL), (GE, XHL, GHL)):
            t = dot(tall[0:HID, :], wide[...], NT)
            total[...] += t[:, :W] + (t[:, W:] + dot(tall[HID:, :], wide[0:W, :], NT))
        dx = dot(upn3_ref[:, : 2 * HID], GHL[...]) + dot(upn3_ref[:, 2 * HID :], GHL[0:HID, :])
        for q in range(2):
            h = 2 * i + q
            d = dx[:, q * W : (q + 1) * W]
            xn = XN[q]
            ACC[0] += d * xn
            ACC[1] += d
            d = d * pb_ref[2]
            m1 = jnp.mean(d, axis=0, keepdims=True)
            m2 = jnp.mean(d * xn, axis=0, keepdims=True)
            d = (d - m1 - xn * m2) * RS[q, 0:1, :]
            D[h] = d
            ACC[2] += d
            hi, lo = split(d)
            hs = pl.ds(pl.multiple_of(h * C, C), C)
            FHL[hs, 0:W] = hi
            FHL[hs, W:] = lo

    def tiles(i, _):
        b0, b1 = lanesets
        stage_a(2 * i, b0)
        stage_a(2 * i + 1, b1)
        stage_b(b0)
        stage_c(2 * i, b0)
        stage_b(b1)
        stage_c(2 * i + 1, b1)
        return 0

    cot_copy.wait()
    lax.fori_loop(0, H // 4, tiles, 0)
    out_copy = pltpu.make_async_copy(OUT, out_hbm, out_sem)
    out_copy.start()

    def shift_gradient():
        shift_rows(DSH, (0, 8 * C), 8 * C)

    def slot(v):
        return v // 48, v % 48 // 3, v % 3

    v = 0
    for total, count in ((GE, 13), (GS, 12)):
        for j in range(3):
            t = total[W * j : W * j + W, :].T
            for i in range(count):
                G[slot(v)] = t[8 * i : 8 * i + 8, :]
                v += 1
    while v < SLOTS:
        G[slot(v)] = jnp.zeros((8, W), f32)
        v += 1

    def rdma(src, dst, send, recv, to):
        return pltpu.make_async_remote_copy(
            src_ref=src, dst_ref=dst, send_sem=send, recv_sem=recv, device_id=to, device_id_type=MESH)

    sibling = (gy + 1 - 2 * core, gx)

    def c0():
        return rdma(G.at[1 - core], R0, s0, r0, sibling)

    def c1(i):
        m = (plane + i) & 15
        return rdma(B0.at[m], R1.at[i], s1.at[i], r1.at[i], at_plane(m, core))

    def c2(i):
        return rdma(B1, R2.at[z], s2.at[i], r2.at[i], at_z((z + i) & 7))

    def g2(i):
        j = (z - i) & 7
        return rdma(B1, R2.at[j], s2.at[i], r2.at[i], at_z(j))

    def c3(i):
        ref = sum_ref.at[core, plane]
        return rdma(ref, ref, s3.at[i], r3.at[i], at_plane((plane + i) & 15, core))

    def g3(i):
        m = (plane - i) & 15
        ref = sum_ref.at[core, m]
        return rdma(ref, ref, s3.at[i], r3.at[i], at_plane(m, core))

    def c4():
        ref = sum_ref.at[core]
        return rdma(ref, ref, s4, r4, sibling)

    def g4():
        ref = sum_ref.at[1 - core]
        return rdma(ref, ref, s4, r4, sibling)

    def step(k):
        if k == 0:
            c0().start()
        elif k == 1:
            c0().wait_recv()
            B0[...] = G[core] + R0[...]
            each(1, 16, lambda i: c1(i).start())
        elif k == 2:
            each(1, 16, lambda i: c1(i).wait_recv())
            acc = B0[plane]
            for i in range(1, 16):
                acc = acc + R1[i]
            B1[...] = acc
            R2[z] = acc
            each(1, 8, lambda i: c2(i).start())
        elif k == 3:
            each(1, 8, lambda i: g2(i).wait_recv())
            acc = R2[0]
            for j in range(1, 8):
                acc = acc + R2[j]
            sum_ref[core, plane] = acc
            each(1, 16, lambda i: c3(i).start())
        elif k == 4:
            each(1, 16, lambda i: g3(i).wait_recv())
            c4().start()
        else:
            g4().wait_recv()
            c0().wait_send()
            each(1, 16, lambda i: c1(i).wait_send())
            each(1, 8, lambda i: c2(i).wait_send())
            each(1, 16, lambda i: c3(i).wait_send())
            c4().wait_send()


    def back_block(cb, _):
        for k, when in enumerate(STEPS):
            @pl.when(cb == when)
            def _(k=k):
                step(k + 1)

        cs = pl.ds(pl.multiple_of(cb * 8, 8), 8)
        def gradient_rows(b):
            if b == 3:
                return [D[h, cs, :] for h in range(H)]
            n = SHIFTS.index(6 - b)
            return [DSH[n, h, cs, :] for h in range(H)]

        grads = jnp.zeros((8, W), f32)
        odd = [F[2 * r + 1, cs, :] for r in range(11)]
        same = [F[2 * r, cs, :] - odd[r] for r in range(11)]
        next_ = [F[2 * r + 2, cs, :] - odd[r] for r in range(10)]

        def correlate(x, y, j):
            t = x[0] * y[j]
            for m in range(1, 8):
                t = t + x[m] * y[m + j]
            return t

        for b in range(7):
            dd = gradient_rows(b)
            d0, d1 = dd[0::2], dd[1::2]
            both = [d0[m] + d1[m] for m in range(8)]
            for j in range(4):
                shared = correlate(both, odd, j)
                for a, part in ((2 * j, (d0, same)), (2 * j + 1, (d1, next_))):
                    if a == 7:
                        continue
                    t = shared + correlate(*part, j)
                    if b < 3:
                        t = t + jnp.where(left, SPX[3 * a + b, cs, :], 0.0)
                    elif b > 3:
                        t = t + jnp.where(left, 0.0, SPX[3 * a + 6 - b, cs, :])
                    total = jnp.sum(t, axis=1, keepdims=True)
                    grads = jnp.where(lane == 7 * a + b, total, grads)

        p0 = [None] * 11
        p1 = [None] * 10
        p2 = [None] * 11

        def convolve(p, x, j, w):
            for m in range(8):
                t = w * x[m]
                p[m + j] = t if p[m + j] is None else p[m + j] + t

        for b in range(7):
            dd = gradient_rows(b)
            d0, d1 = dd[0::2], dd[1::2]
            both = [d0[m] + d1[m] for m in range(8)]
            for j in range(4):
                w0 = wb_ref[7 * (2 * j) + b, cs, :]
                convolve(p0, d0, j, w0)
                if j < 3:
                    w1 = wb_ref[7 * (2 * j + 1) + b, cs, :]
                    convolve(p1, d1, j, w1)
                    w0 = w0 + w1
                convolve(p2, both, j, w0)
        acc = []
        for m in range(11):
            even = p0[m] if m == 0 else p0[m] + p1[m - 1]
            other_row = p2[m] - p0[m]
            if m < 10:
                other_row = other_row - p1[m]
            acc += [even, other_row]
        acc = [t + DY[r - 3, cs, :] if 3 <= r < H + 3 else t for r, t in enumerate(acc)]
        for k, src in enumerate((2, 0, 1, 3)):
            total = jnp.sum(ACC[src, cs, :], axis=1, keepdims=True)
            grads = jnp.where(lane == DEPTH_B + k, total, grads)
        total = DFS[0, cs, :] + DFS[1, cs, :]
        for r in range(EXT):
            t = acc[r]
            if r < 3:
                t = t * top_ok
            elif r >= H + 3:
                t = t * bot_ok
            DF[r, cs, :] = t
            total = total + t
        total = jnp.sum(total, axis=1, keepdims=True)
        GV[cs, :] = jnp.where(lane == STEM_B, total, grads)
        return 0

    step(0)
    shift_gradient()

    packed = jnp.zeros((C, W), f32)
    for h in range(H):
        packed = jnp.where(prow96 == h, roll(D[h], 8 * h + 3), packed)
    packed = jnp.where(left96, roll(packed, -3), jnp.where(right96, roll(packed, 3), 0.0))
    vs = [packed]
    for k in (1, 2):
        vs.append(jnp.where(left96, jnp.where(pos96 >= k, roll(packed, k), 0.0),
                            jnp.where(right96 & (pos96 < 6 - k), roll(packed, -k), 0.0)))
    o0 = jnp.zeros((C, W), f32)
    o1 = jnp.zeros((C, W), f32)
    for a in range(7):
        win = window(a, FS[0], FS[1])
        t = None
        for k in range(3):
            u = wbs_ref[3 * a + k] * vs[k]
            t = u if t is None else t + u
            SPX[3 * a + k] = vs[k] * win
        o0 = o0 + jnp.where((prow96 >= a) & (prow96 < 11), roll(t, 8 * a), 0.0)
        o1 = o1 + jnp.where(prow96 < 5 + a, roll(t, 8 * (a - 11)), 0.0)
    DFS[0] = o0 * jnp.concatenate([ok0] * NB, axis=0)
    DFS[1] = o1 * jnp.concatenate([ok1] * NB, axis=0)

    lax.fori_loop(0, NB, back_block, 0)
    step(len(STEPS) + 1)

    def rows2(p0, p1, d0, d1):
        ph, plo = split(jnp.concatenate([p0, p1], axis=1))
        dh, dlo = split(jnp.concatenate([d0, d1], axis=1))
        t = dot(jnp.concatenate([ph, plo], axis=0), dh, NT)
        return t[:KK] + (t[KK:] + dot(ph, dlo, NT))

    def okpat(p, ok):
        return p if ok is None else jnp.where(ok > 0.0, p, 0.0)

    def row_ok(r):
        return top_ok if r < 3 else bot_ok if r >= H + 3 else None

    okk = [jnp.concatenate([ok] * (KK // 8), axis=0) for ok in (ok0, ok1)]
    gstem = rows2(okpat(side_ref[0], okk[0]), okpat(side_ref[1], okk[1]), DFS[0], DFS[1])
    for r in range(0, EXT, 2):
        gstem = gstem + rows2(
            okpat(pat_ref[r], row_ok(r)), okpat(pat_ref[r + 1], row_ok(r + 1)), DF[r], DF[r + 1])

    zero = jnp.zeros((KK, W - C), f32)
    gs = jnp.concatenate([gstem, zero], axis=1)
    vec = jnp.concatenate([GV[...], jnp.zeros((W - C, W), f32)], axis=0).T
    tail = [gs[8 * i : 8 * i + 8, :] for i in range(6)] + [vec[8 * i : 8 * i + 8, :] for i in range(7)]
    for i, v in enumerate(tail):
        TG[i] = v

    def owner(v):
        return at_plane(v, v & 1)

    mine = ((plane & 1) == core) & (plane < TAIL)

    def t1(v):
        return rdma(TG.at[v], TR.at[plane, core], ts1.at[v], tr1.at[plane, core], owner(v))

    def w1(m, c):
        return rdma(TP, TR.at[m, c], ts1.at[0], tr1.at[m, c], at_plane(m, c))

    def t2(i):
        return rdma(TP, TX.at[z], ts2.at[i], tr2.at[i], at_z((z + i) & 7))

    def w2(i):
        j = (z - i) & 7
        return rdma(TP, TX.at[j], ts2.at[i], tr2.at[i], at_z(j))

    def t3(m, c):
        ref = tail_ref.at[plane]
        return rdma(ref, ref, ts3.at[m, c], tr3.at[plane], at_plane(m, c))

    def w3(v):
        ref = tail_ref.at[v]
        return rdma(ref, ref, ts3.at[0, 0], tr3.at[v], owner(v))

    def others(f):
        def one(i):
            m, c = i >> 1, i & 1
            @pl.when((m != plane) | (c != core))
            def _():
                f(m, c)
        each(0, 32, one)

    def foreign(f):
        def one(v):
            @pl.when((v != plane) | ((v & 1) != core))
            def _():
                f(v)
        each(0, TAIL, one)

    foreign(lambda v: t1(v).start())

    @pl.when(mine)
    def _():
        TR[plane, core] = TG[plane]
        others(lambda m, c: w1(m, c).wait_recv())
        acc = TR[0, 0]
        for i in range(1, 32):
            acc = acc + TR[i >> 1, i & 1]
        TP[...] = acc
        TX[z] = acc
        each(1, 8, lambda i: t2(i).start())

    step(len(STEPS) + 2)

    @pl.when(mine)
    def _():
        each(1, 8, lambda i: w2(i).wait_recv())
        acc = TX[0]
        for j in range(1, 8):
            acc = acc + TX[j]
        tail_ref[plane] = acc
        others(lambda m, c: t3(m, c).start())

    step(len(STEPS) + 3)
    foreign(lambda v: t1(v).wait_send())
    step(len(STEPS) + 4)
    foreign(lambda v: w3(v).wait_recv())

    @pl.when(mine)
    def _():
        each(1, 8, lambda i: t2(i).wait_send())
        others(lambda m, c: t3(m, c).wait_send())

    out_copy.wait()
    for group in range(len(GROUPS)):
        for bucket_at in range(2):
            tile_copy(bucket_at, group).wait_send()
    row_copy(True).wait_send()
    row_copy(False).wait_send()
    for i in range(len(NEAR)):
        edge_copy(i).wait_send()
    for group in (1, 2):
        for i in range(2):
            mid_copy(group, i).wait_send()


def whole_call(*args):
    vm = pl.BlockSpec(memory_space=pltpu.VMEM)
    hbm = pl.BlockSpec(memory_space=pltpu.HBM)
    s = jax.ShapeDtypeStruct
    n_send = INFO + 3 * H
    near = len(NEAR)

    def v(*shape, dtype=f32):
        return pltpu.VMEM(shape, dtype)

    buf = [
        v(2 * XR, 2 * W, dtype=bf16), v(2 * W, 2 * W, dtype=bf16), v(HID, 2 * W), v(HID, 2 * W),
        v(2 * HID, 2 * W, dtype=bf16), v(2 * HID, 2 * W, dtype=bf16), v(2, C, W), v(2, 8, W),
    ]
    return pl.pallas_call(
        whole_kernel,
        out_shape=(s((C * H, W), f32), s((2, 16, 3, 8, W), f32), s((TAIL, 8, W), f32)),
        in_specs=[hbm] * 14,
        out_specs=[hbm, vm, vm],
        scratch_shapes=[
            v(EXT, KK, W), v(2, KK, W), v(8, W), v(TAPS, C, W), v(21, C, W), v(5, C, W),
            v(C, 3 * KK, dtype=bf16), v(2 * HID, 2 * XR, dtype=bf16), v(2 * HID, 2 * W, dtype=bf16),
            v(C, 3 * HID, dtype=bf16), v(C, 3 * HID, dtype=bf16),
            v(8, PIX), v(1, 8, dtype=jnp.int32), v(1, 8, dtype=jnp.int32),
            v(KK, C), v(TAPS, C), v(1, C), v(1, C), v(1, C), v(1, C), v(C, HID), v(HID), v(C, HID), v(1, C),
            v(2, n_send, 8, W), v(2, n_send, 8, W), v(3, KK, W), v(near, KK, W), v(2, 2, KK, W), v(W, W), v(C * H, W),
            DMA((12,)), DMA((12,)), DMA((2, 3)), DMA((2, 3)), DMA((2,)), DMA((2,)),
            DMA((near,)), DMA((near,)), DMA((2, 2)), DMA((2, 2)), DMA(()), DMA(()),
            v(EXT, C, W), v(2, C, W), v(H, C, W), v(6, H, C, W), v(H, C, W), v(HID, W), v(HID, W), v(4, C, W),
            v(EXT * C, 2 * W, dtype=bf16), v(6, EXT, C, W), v(2 * W, 6 * W, dtype=bf16), v(C * H, W),
            v(2, 16, 3, 8, W), v(16, 3, 8, W), v(16, 3, 8, W), v(16, 3, 8, W), v(3, 8, W), v(8, 3, 8, W),
            v(TAIL, 8, W), v(16, 2, 8, W), v(8, W), v(8, 8, W), v(EXT, C, W), v(2, C, W), v(C, W),
            DMA(()), DMA(()), DMA((16,)), DMA((16,)), DMA((8,)), DMA((8,)), DMA((16,)), DMA((16,)), DMA(()), DMA(()),
            DMA((TAIL,)), DMA((16, 2)), DMA((8,)), DMA((8,)), DMA((16, 2)), DMA((TAIL,)), v(21, C, W),
            *buf, *buf,
        ],
        compiler_params=pltpu.CompilerParams(
            collective_id=0, has_side_effects=True, vmem_limit_bytes=56 * 1024 * 1024),
        name="whole",
    )(*args)


PIECES = 4


def unpack_kernel(
    sum_hbm, tail_hbm, block_hbm, out_hbm, gstem_ref, gstem_b_ref, gdepth_ref, gdepth_b_ref, ggain_ref, gnbias_ref,
    gexp_ref, gexp_b_ref, gshr_ref, gshr_b_ref, held, sum_ref, tail_ref, sem,
):
    rows = C * H // PIECES

    def piece(i, back):
        at = pl.ds(i * rows, rows)
        if back:
            return pltpu.make_async_copy(held.at[at], out_hbm.at[at], sem.at[1, i])
        return pltpu.make_async_copy(block_hbm.at[at], held.at[at], sem.at[0, i])

    total = pltpu.make_async_copy(sum_hbm, sum_ref, sem.at[2, 0])
    last = pltpu.make_async_copy(tail_hbm, tail_ref, sem.at[2, 1])
    total.start()
    last.start()
    for i in range(PIECES):
        piece(i, False).start()
    total.wait()
    last.wait()

    def at(v):
        return sum_ref[v // 48, v % 48 // 3, v % 3]

    v = 0
    for j in range(3):
        for i in range(12):
            gexp_ref[8 * i : 8 * i + 8, W * j : W * j + W] = at(v)
            v += 1
        gexp_b_ref[W * j : W * j + W] = at(v)[0]
        v += 1
    for j in range(3):
        for i in range(12):
            gshr_ref[8 * i : 8 * i + 8, W * j : W * j + W] = at(v)
            v += 1
    for i in range(PIECES):
        piece(i, False).wait()
        piece(i, True).start()
    for i in range(6):
        gstem_ref[8 * i : 8 * i + 8, :] = tail_ref[i][:, :C]
        gdepth_ref[8 * i : 8 * i + 8, :] = tail_ref[6 + i][:, :C]
    last = tail_ref[12][:, :C]
    gdepth_ref[48:49, :] = last[0:1]
    for k, ref in enumerate((gstem_b_ref, gdepth_b_ref, ggain_ref, gnbias_ref, gshr_b_ref)):
        ref[...] = last[k + 1 : k + 2]
    for i in range(PIECES):
        piece(i, True).wait()


def unpack_call(block, total, tail):
    vm = pl.BlockSpec(memory_space=pltpu.VMEM)
    hbm = pl.BlockSpec(memory_space=pltpu.HBM)
    shapes = ((KK, C), (1, C), (TAPS, C), (1, C), (1, C), (1, C), (C, HID), (HID,), (C, HID), (1, C))
    return pl.pallas_call(
        unpack_kernel,
        out_shape=tuple(jax.ShapeDtypeStruct(s, f32) for s in ((C * H, W),) + shapes),
        in_specs=[hbm] * 3,
        out_specs=[hbm] + [vm] * len(shapes),
        scratch_shapes=[
            pltpu.VMEM((C * H, W), f32), pltpu.VMEM((2, 16, 3, 8, W), f32), pltpu.VMEM((TAIL, 8, W), f32), DMA((3, PIECES))],
        compiler_params=pltpu.CompilerParams(vmem_limit_bytes=56 * 1024 * 1024),
        name="unpack",
    )(total, tail, block)


def local(
    stored_tiles, tile_target, tile_mask,
    stem_weight, stem_bias, depth_weight, depth_bias, norm_gain, norm_bias,
    expand_weight, expand_bias, shrink_weight, shrink_bias, cotangent,
):
    def row(v):
        return v.reshape(1, -1)

    block, total, tail = whole_call(
        stored_tiles[0], tile_target, tile_mask, stem_weight, depth_weight, row(stem_bias), row(depth_bias),
        row(norm_gain), row(norm_bias), expand_weight, expand_bias, shrink_weight.T, row(shrink_bias),
        cotangent.reshape(C * H, W))
    out, gs, gsb, gd, gdb, gg, gn, ge, geb, gh, ghb = unpack_call(block, total, tail)
    return (
        out.reshape(C, H, W), gs, gsb[0], gd, gdb[0], gg[0], gn[0], ge, geb, gh.T, ghb[0],
    )


def solution(mesh):
    placed = (P("gy", "gx", None), P("gy", "gx"), P("gy", "gx")) + (P(),) * 10 + (P(None, "gy", "gx"),)
    return jax.shard_map(
        local, mesh=mesh, in_specs=placed,
        out_specs=(P(None, "gy", "gx"),) + (P(),) * 10,
        check_vma=False,
    )
```

```python
import jax
import jax.numpy as jnp
from jax import lax
from jax.experimental import pallas as pl
from jax.experimental.pallas import tpu as pltpu
from jax.sharding import PartitionSpec as P

C = 96
HID = 384
NB = C // 8
H = 16
W = 128
EXT = H + 6
KK = 48
TAPS = 49
PIX = 12288
f32 = jnp.float32
bf16 = jnp.bfloat16
EPS = 1e-6
MESH = pl.DeviceIdType.MESH
DMA = pltpu.SemaphoreType.DMA

NN = (((1,), (0,)), ((), ()))
NT = (((1,), (1,)), ((), ()))


def split(x):
    hi = x.astype(bf16)
    return hi, (x - hi.astype(f32)).astype(bf16)


def dot(a, b, dims=NN):
    return lax.dot_general(a, b, dims, preferred_element_type=f32)


def lanes(shape=(8, W)):
    return lax.broadcasted_iota(jnp.int32, shape, len(shape) - 1)


def roll(x, by):
    by = by % W
    return x if by == 0 else pltpu.roll(x, by, x.ndim - 1)


STEM_B, DEPTH_B, GAIN, NBIAS, SHRINK_B = 49, 50, 51, 52, 53
GROUPS = ((0, 1, 2, 13, 14, 15), (3, 4, 5, 6, 7, 8), (9, 10, 11, 12))
ORDER = tuple(h for group in GROUPS for h in group)
INFO = 2
NEAR = ((0, -1), (0, 1), (-1, -1), (-1, 1), (1, -1), (1, 1))


def payload_range(group):
    before = sum(len(g) for g in GROUPS[:group])
    after = before + len(GROUPS[group])
    return (0 if group == 0 else INFO + 3 * before), INFO + 3 * after


def row_ranges(group):
    rows = GROUPS[group]
    if group == 0:
        return ((rows[0], 3), (rows[3], 3))
    return ((rows[0], len(rows)),)


def take(x, index, axis):
    return jnp.take_along_axis(x, index, axis=axis)


def each(low, high, f):
    def one(i, _):
        f(i)
        return 0
    lax.fori_loop(low, high, one, 0)


XR = W
CH = 16
SLOTS = 96
TAIL = 13
SHIFTS = (0, 1, 2, 4, 5, 6)
STEPS = (0,)

def validity(gy, gx):
    ny = lax.axis_size("gy")
    nx = lax.axis_size("gx")
    lane = lanes()
    pos = lane & 7
    prow = lane >> 3
    top_ok = (gy > 0).astype(f32)
    bot_ok = (gy < ny - 1).astype(f32)
    left_ok = (gx > 0).astype(f32)
    right_ok = (gx < nx - 1).astype(f32)
    col_ok = jnp.where(pos < 3, left_ok, jnp.where(pos < 6, right_ok, 0.0))
    col_ok = jnp.where(prow < 11, col_ok, 0.0)
    ok0 = col_ok * jnp.where(prow < 3, top_ok, 1.0)
    ok1 = col_ok * jnp.where(prow >= 8, bot_ok, 1.0)
    return top_ok, bot_ok, ok0, ok1


def whole_kernel(
    tiles_hbm, target_hbm, marks_hbm, stem_hbm, dw_hbm, sb_hbm, db_hbm, ga_hbm, nb_hbm, ew_hbm, eb_hbm, sw_hbm, hb_hbm, cot_hbm,
    out_hbm, sum_ref, tail_ref,
    pat_ref, side_ref, fm_ref, wb_ref, wbs_ref, pb_ref, stem3_ref, up2_ref, dnn2_ref, dn3_ref, upn3_ref, tiles,
    target, marks, stem_v, dw_v, sb_v, db_v, ga_v, nb_v, ew_v, eb_v, sw_v, hb_v, send, recv, edge, edges,
    edges_mid, ct, cot_ref, in_sem, par_sem, tile_send, tile_recv, row_send, row_recv, edge_send, edge_recv,
    mid_send, mid_recv, cot_sem, out_sem, F, FS, D, DSH, DY, GE, GS, ACC, FHL, FSH, SH, OUT, G, R0, B0, R1, B1,
    R2, TG, TR, TP, TX, DF, DFS, GV, s0, r0, s1, r1, s2, r2, s3, r3, s4, r4, ts1, tr1, ts2, tr2, ts3, tr3, SPX, *bufs,
):
    gy = lax.axis_index("gy")
    gx = lax.axis_index("gx")
    ny = lax.axis_size("gy")
    nx = lax.axis_size("gx")

    def device(dy, dx):
        return (lax.rem(gy + dy + ny, ny), lax.rem(gx + dx + nx, nx))

    y_hi, xx, core = gy >> 3, (gy >> 1) & 3, gy & 1
    y_lo, z = gx >> 3, gx & 7
    plane = (y_hi * 2 + y_lo) * 4 + xx

    def at_plane(m, c):
        return ((m >> 3) * 8 + (m & 3) * 2 + c, ((m >> 2) & 1) * 8 + z)

    def at_z(j):
        return (gy, y_lo * 8 + j)

    barrier = pltpu.get_barrier_semaphore()

    def greet(to):
        pl.semaphore_signal(barrier, inc=1, device_id=to, device_id_type=MESH)

    peers = [(0, 1), (0, -1), (0, 9), (0, -9)] + [(dy, dx) for dy in (-1, 1) for dx in (-1, 0, 1)]
    for dy, dx in peers:
        greet(device(dy, dx))
    each(1, 16, lambda i: greet(at_plane((plane + i) & 15, core)))
    each(0, 16, lambda i: greet(at_plane((plane + i) & 15, 1 - core)))
    each(1, 8, lambda i: greet(at_z((z + i) & 7)))
    greetings = len(peers) + 15 + 16 + 7

    params = [
        pltpu.make_async_copy(src, dst, par_sem.at[i])
        for i, (src, dst) in enumerate((
            (target_hbm, target), (marks_hbm, marks), (stem_hbm, stem_v), (dw_hbm, dw_v), (sb_hbm, sb_v),
            (db_hbm, db_v), (ga_hbm, ga_v), (nb_hbm, nb_v), (ew_hbm, ew_v), (eb_hbm, eb_v), (sw_hbm, sw_v),
            (hb_hbm, hb_v)))
    ]
    params[0].start()
    params[1].start()
    loads = []
    for group in range(len(GROUPS)):
        for lo, n in row_ranges(group):
            for k in range(3):
                at = pl.ds(k * 4096 + lo * 256, n * 256)
                loads.append((group, pltpu.make_async_copy(
                    tiles_hbm.at[:, at], tiles.at[:, at], in_sem.at[len(loads)])))
                loads[-1][1].start()
    for copy in params[2:]:
        copy.start()
    cot_copy = pltpu.make_async_copy(cot_hbm, cot_ref, cot_sem)
    cot_copy.start()

    sub = lax.broadcasted_iota(jnp.int32, (8, W), 0)
    lane = lanes()
    row8 = lax.broadcasted_iota(jnp.int32, (8, 8), 0)
    col8 = lax.broadcasted_iota(jnp.int32, (8, 8), 1)
    eye = row8 == col8
    params[0].wait()
    params[1].wait()

    def down_column(row):
        return jnp.sum(jnp.where(eye, row, 0.0), axis=1, keepdims=True)

    codes = jnp.broadcast_to(target[...], (8, 8))
    bucket = ((((codes >> 3) - gx - 1) & 15) >> 3).astype(f32)
    place = (codes & 7).astype(f32)
    mark = jnp.broadcast_to(marks[...], (8, 8)).astype(f32)
    bucket_col = down_column(bucket)
    rank = jnp.sum(jnp.where((bucket_col == bucket) & (row8 < col8), 1.0, 0.0), axis=0, keepdims=True)
    slot_pos = bucket[0:1, :] * 4.0 + rank

    def sources(wanted):
        return jnp.sum(jnp.where(slot_pos == wanted.astype(f32), col8.astype(f32), 0.0), axis=1, keepdims=True)

    order = jnp.broadcast_to(sources(row8), (8, W)).astype(jnp.int32)
    turned = jnp.broadcast_to(sources((row8 + 4) & 7), (8, W)).astype(jnp.int32)
    place_col = jnp.broadcast_to(down_column(place), (8, W))
    mark_col = jnp.broadcast_to(down_column(mark), (8, W))
    low = sub < 4

    def put(q, x0, x1):
        g0 = take(x0, order, 0)
        g1 = take(x1, turned, 0)
        send[0, q] = jnp.where(low, g0, g1)
        send[1, q] = jnp.where(low, g1, g0)

    def tile_copy(bucket_at, group):
        lo, hi = payload_range(group)
        return pltpu.make_async_remote_copy(
            src_ref=send.at[bucket_at, pl.ds(lo, hi - lo)],
            dst_ref=recv.at[bucket_at, pl.ds(lo, hi - lo)],
            send_sem=tile_send.at[bucket_at, group],
            recv_sem=tile_recv.at[bucket_at, group],
            device_id=device(0, 1 + 8 * bucket_at),
            device_id_type=MESH,
        )

    pos = lane & 7
    left = pos < 3

    def prepare():
        src = lax.broadcasted_iota(jnp.int32, (2 * W, W), 0) & (W - 1)
        dst = lax.broadcasted_iota(jnp.int32, (2 * W, W), 1)
        for n, b in enumerate(SHIFTS):
            SH[:, n * W : (n + 1) * W] = jnp.where(src == dst + (b - 3), 1.0, 0.0).astype(bf16)

        for copy in params[2:]:
            copy.wait()
        ct[...] = jnp.zeros_like(ct)
        ct[0:TAPS, 0:C] = dw_v[...]
        for k, ref in enumerate((sb_v, db_v, ga_v, nb_v, hb_v)):
            ct[STEM_B + k : STEM_B + k + 1, 0:C] = ref[...]
        cols = ct[...].T
        ct[...] = cols

        def spread(cb, _):
            cs = pl.ds(pl.multiple_of(cb * 8, 8), 8)
            wc = ct[cs, :]
            for a in range(7):
                taps = []
                for b in range(7):
                    t = 7 * a + b
                    taps.append(jnp.broadcast_to(wc[:, t : t + 1], (8, W)))
                    wb_ref[t, cs, :] = taps[-1]
                for k in range(3):
                    wbs_ref[3 * a + k, cs, :] = jnp.where(left, taps[k], taps[6 - k])
            for k in range(5):
                pb_ref[k, cs, :] = jnp.broadcast_to(wc[:, STEM_B + k : STEM_B + k + 1], (8, W))
            return 0

        lax.fori_loop(0, NB, spread, 0)

        def turned_over(x):
            n = x.shape[0]
            return jnp.concatenate([x, jnp.zeros((W - n, x.shape[1]), f32)], axis=0).T

        stem_pad = jnp.concatenate([stem_v[...], jnp.zeros((KK, W - C), f32)], axis=1)
        hi, lo = split(turned_over(stem_pad)[:C, :KK])
        stem3_ref[:, 0:KK] = hi
        stem3_ref[:, KK : 2 * KK] = hi
        stem3_ref[:, 2 * KK :] = lo
        ew = ew_v[...]
        sw = sw_v[...]
        for src, ref in ((sw, dn3_ref), (ew, upn3_ref)):
            hi, lo = split(src)
            ref[:, 0:HID] = hi
            ref[:, HID : 2 * HID] = hi
            ref[:, 2 * HID :] = lo
        hi, lo = split(turned_over(sw)[:, :C])
        dnn2_ref[0:HID, 0:C] = hi
        dnn2_ref[0:HID, W : W + C] = hi
        dnn2_ref[HID:, 0:C] = lo
        dnn2_ref[HID:, W:] = jnp.zeros((HID, W), bf16)
        dnn2_ref[:, C:W] = jnp.zeros((2 * HID, W - C), bf16)
        dnn2_ref[0:HID, W + C :] = jnp.zeros((HID, W - C), bf16)
        up = jnp.concatenate([ew, eb_v[...].reshape(1, HID), jnp.zeros((W - C - 1, HID), f32)], axis=0).T
        hi, lo = split(up[:, : W])
        up2_ref[0:HID, 0 : W] = hi
        up2_ref[0:HID, W :] = hi
        up2_ref[HID:, 0 : W] = lo
        up2_ref[HID:, W :] = jnp.zeros((HID, W), bf16)


    put(0, place_col, place_col)
    put(1, mark_col, mark_col)
    for group, rows in enumerate(GROUPS):
        for at, copy in loads:
            if at == group:
                copy.wait()
        for h in rows:
            for k in range(3):
                r = k * 32 + h * 2
                x0 = tiles[:, r * W : (r + 1) * W] * mark_col
                x1 = tiles[:, (r + 1) * W : (r + 2) * W] * mark_col
                put(INFO + 3 * ORDER.index(h) + k, x0, x1)
        if group > 0:
            for bucket_at in range(2):
                tile_copy(bucket_at, group).start()
            continue
        pl.semaphore_wait(barrier, greetings)
        for bucket_at in range(2):
            tile_copy(bucket_at, group).start()

    prepare()
    top_ok, bot_ok, ok0, ok1 = validity(gy, gx)

    def stem_of(p, bias):
        hi, lo = split(p)
        return dot(stem3_ref[...], jnp.concatenate([hi, lo, hi], axis=0)) + bias

    bias2 = jnp.concatenate([pb_ref[0], pb_ref[0]], axis=1)

    def row_ok(r):
        return top_ok if r < 3 else bot_ok if r >= H + 3 else None

    def stem_pair(pair):
        parts = []
        for q in range(2):
            ok = row_ok(pair[q])
            p = pat_ref[pair[q]]
            parts.append(p if ok is None else jnp.where(ok > 0.0, p, 0.0))
        y = stem_of(jnp.concatenate(parts, axis=1), bias2)
        for q in range(2):
            r = pair[q]
            ok = row_ok(r)
            v = y[:, q * W : (q + 1) * W]
            if ok is not None:
                v = v * ok
            F[r] = v
            hi, lo = split(v)
            FHL[r * C : (r + 1) * C, 0:W] = hi
            FHL[r * C : (r + 1) * C, W:] = lo
    def shift_rows(ref, starts, rows):
        for n in range(3):
            for at in starts:
                y = dot(FHL[at : at + rows, :], SH[:, 2 * n * W : (2 * n + 2) * W])
                for r in range(rows // C):
                    ref[2 * n, at // C + r] = y[r * C : (r + 1) * C, :W]
                    ref[2 * n + 1, at // C + r] = y[r * C : (r + 1) * C, W:]

    w16 = lane & 15
    beta = lane >> 4
    prow = lane >> 3

    def row_copy(up):
        src, dst, dy = (3, H + 3, -1) if up else (H, 0, 1)
        return pltpu.make_async_remote_copy(
            src_ref=pat_ref.at[pl.ds(src, 3)],
            dst_ref=pat_ref.at[pl.ds(dst, 3)],
            send_sem=row_send.at[int(up)],
            recv_sem=row_recv.at[int(up)],
            device_id=device(dy, 0),
            device_id_type=MESH,
        )

    def edge_copy(i):
        dy, dx = NEAR[i]
        return pltpu.make_async_remote_copy(
            src_ref=edge.at[0], dst_ref=edges.at[i], send_sem=edge_send.at[i], recv_sem=edge_recv.at[i],
            device_id=device(dy, dx), device_id_type=MESH)

    def mid_copy(group, i):
        dy, dx = NEAR[i]
        return pltpu.make_async_remote_copy(
            src_ref=edge.at[group], dst_ref=edges_mid.at[group - 1, i],
            send_sem=mid_send.at[group - 1, i], recv_sem=mid_recv.at[group - 1, i],
            device_id=device(dy, dx), device_id_type=MESH)

    for group, rows in enumerate(GROUPS):
        for bucket_at in range(2):
            tile_copy(bucket_at, group).wait_recv()
        if group == 0:
            places = (recv[0, 0], recv[1, 0])
            marks_in = (recv[0, 1], recv[1, 1])
            first = []
            for p in places:
                g = (beta - p.astype(jnp.int32)) & 7
                first.append((g >> 2) * 64 + w16 * 4 + (g & 3))
            wanted = ((beta - sub) & 7).astype(f32)
            wanted_t = beta.astype(f32)
            found = []
            fm = jnp.zeros((8, W), f32)
            for j, off in ((0, 0), (1, 4)):
                at = jnp.zeros((8, W), f32)
                hit = jnp.zeros((8, W), f32)
                for k in range(4):
                    p = jnp.broadcast_to(places[j][off + k : off + k + 1, :], (8, W))
                    m = jnp.broadcast_to(marks_in[j][off + k : off + k + 1, :], (8, W))
                    at = jnp.where(p == wanted, float(k), at)
                    hit = jnp.where(p == wanted, 1.0, hit)
                    fm = jnp.where(p == wanted_t, m, fm)
                found.append((at.astype(jnp.int32), hit))
            fm_ref[...] = fm
            in_a = found[0][1] > 0.0
            second = [(found[0][0] + 4 * a, found[1][0] + 4 * (1 - a)) for a in range(2)]
            third = ((sub + beta) & 7) * 16 + w16
        for h in rows:
            for k in range(3):
                q = INFO + 3 * ORDER.index(h) + k
                ya = take(recv[0, q], first[0], 1)
                yb = take(recv[1, q], first[1], 1)
                for a in range(2):
                    v = jnp.where(in_a, take(ya, second[a][0], 0), take(yb, second[a][1], 0))
                    pat_ref[h + 3, pl.ds(16 * k + 8 * a, 8), :] = take(v, third, 1)
        if group == 0:
            row_copy(True).start()
            row_copy(False).start()
        for j in range(KK // 8):
            js = pl.ds(8 * j, 8)
            v = jnp.zeros((8, W), f32)
            for h in rows:
                v = jnp.where(prow == h, roll(pat_ref[h + 3, js, :], 8 * h + 3), v)
            edge[group, js, :] = v
        if group == 0:
            for i in range(len(NEAR)):
                edge_copy(i).start()
        else:
            for i in range(2):
                mid_copy(group, i).start()
        for n in range(0, len(rows), 2):
            stem_pair((rows[n] + 3, rows[n + 1] + 3))
        for lo, n in row_ranges(group):
            shift_rows(FSH, ((lo + 3) * C,), n * C)

    def feature_rows(b, which, cs):
        if b == 3:
            return {r: F[r, cs, :] for r in which}
        return {r: FSH[SHIFTS.index(b), r, cs, :] for r in which}

    def conv_block(cb, _):
        cs = pl.ds(pl.multiple_of(cb * 8, 8), 8)
        acc = [pb_ref[1, cs, :]] * H
        for b in range(7):
            rows = feature_rows(b, range(3, H + 3), cs)
            for a in range(7):
                w = wb_ref[7 * a + b, cs, :]
                for h in range(H):
                    if h + a in rows:
                        acc[h] = acc[h] + w * rows[h + a]
        for h in range(H):
            D[h, cs, :] = acc[h]
        return 0

    lax.fori_loop(0, NB, conv_block, 0)

    for i in range(len(NEAR)):
        edge_copy(i).wait_recv()
    for group in (1, 2):
        for i in range(2):
            mid_copy(group, i).wait_recv()
    up_left, up_right = edges.at[5], edges.at[4]
    down_left, down_right = edges.at[3], edges.at[2]
    for j in range(KK // 8):
        js = pl.ds(8 * j, 8)
        from_left = edges[1, js, :] + (edges_mid[0, 1, js, :] + edges_mid[1, 1, js, :])
        from_right = edges[0, js, :] + (edges_mid[0, 0, js, :] + edges_mid[1, 0, js, :])
        mid = jnp.where(left, from_left, from_right)
        top = jnp.where(left, up_left[js, :], up_right[js, :])
        bottom = jnp.where(left, down_left[js, :], down_right[js, :])
        side_ref[0, js, :] = jnp.where(prow < 3, roll(top, -104), roll(mid, 24))
        side_ref[1, js, :] = jnp.where(prow < 8, roll(mid, -64), roll(bottom, 64))
    row_copy(True).wait_recv()
    row_copy(False).wait_recv()
    for r in (0, 2, 20):
        stem_pair((r, r + 1) if r != 2 else (2, 19))
    parts = []
    for i, ok in enumerate((ok0, ok1)):
        okk = jnp.concatenate([ok] * (KK // 8), axis=0)
        parts.append(jnp.where(okk > 0.0, side_ref[i], 0.0))
    y = stem_of(jnp.concatenate(parts, axis=1), bias2)
    for i, ok in enumerate((ok0, ok1)):
        FS[i] = y[:, i * W : (i + 1) * W] * jnp.concatenate([ok] * NB, axis=0)

    for r in (0, H + 3):
        shift_rows(FSH, (r * C,), 3 * C)

    def window(a, lo, hi):
        return jnp.where(prow96 < 11 - a, roll(lo, -8 * a), roll(hi, 8 * (11 - a)))

    lane96 = lanes((C, W))
    pos96 = lane96 & 7
    prow96 = lane96 >> 3
    left96 = pos96 < 3
    right96 = (pos96 >= 3) & (pos96 < 6)
    edge96 = (lane96 < 3) | (lane96 >= W - 3)
    part = [None] * 3
    for a in range(7):
        win = window(a, FS[0], FS[1])
        for k in range(3):
            t = wbs_ref[3 * a + k] * win
            part[k] = t if part[k] is None else part[k] + t
    q = part[0]
    for k in (1, 2):
        q = q + jnp.where(left96, jnp.where(pos96 < 3 - k, roll(part[k], -k), 0.0),
                          jnp.where((pos96 >= 3 + k) & (pos96 < 6), roll(part[k], k), 0.0))
    q = jnp.where(left96, roll(q, -3), roll(q, 3))
    for h in range(H):
        D[h] += jnp.where(edge96, roll(q, 125 - 8 * h), 0.0)

    def conv_edge(cb, _):
        cs = pl.ds(pl.multiple_of(cb * 8, 8), 8)
        inner = (0, 1, 2, H - 3, H - 2, H - 1)
        outer = (0, 1, 2, H + 3, H + 4, H + 5)
        acc = {h: D[h, cs, :] for h in inner}
        for b in range(7):
            rows = feature_rows(b, outer, cs)
            for a in range(7):
                w = wb_ref[7 * a + b, cs, :]
                for h in inner:
                    if h + a in rows:
                        acc[h] = acc[h] + w * rows[h + a]
        for h in inner:
            D[h, cs, :] = acc[h]
        return 0

    lax.fori_loop(0, NB, conv_edge, 0)

    fmc = jnp.concatenate([fm_ref[...]] * NB, axis=0)
    ones_row = jnp.where(lax.broadcasted_iota(jnp.int32, (W - C, 2 * W), 0) == 0, 1.0, 0.0)
    lanesets = [bufs[: len(bufs) // 2], bufs[len(bufs) // 2 :]]
    none = jnp.zeros((W - C, 2 * W), bf16)
    for XHL, YHL, *_ in lanesets:
        YHL[C:W, :] = none
        YHL[W + C :, :] = none
        XHL[C:XR, :] = ones_row.astype(bf16)
        XHL[XR + C :, :] = none
    GE[...] = jnp.zeros_like(GE)
    GS[...] = jnp.zeros_like(GS)
    ACC[...] = jnp.zeros_like(ACC)

    def stage_a(i, buf):
        XHL, YHL, U, DA, AHL, GHL, XN, RS = buf
        for q in range(2):
            h = 2 * i + q
            qs = slice(q * W, (q + 1) * W)
            x = D[h]
            m = jnp.mean(x, axis=0, keepdims=True)
            xc = x - m
            v = jnp.mean(xc * xc, axis=0, keepdims=True)
            rs = lax.rsqrt(v + EPS)
            xn = xc * rs
            XN[q] = xn
            RS[q] = jnp.broadcast_to(rs, (8, W))
            hi, lo = split(xn * pb_ref[2] + pb_ref[3])
            XHL[0:C, qs] = hi
            XHL[XR : XR + C, qs] = lo
            dy = cot_ref[pl.ds(h, C, stride=H), :] * fmc
            DY[h] = dy
            ACC[3] += dy
            hi, lo = split(dy)
            YHL[0:C, qs] = hi
            YHL[W : W + C, qs] = lo
        t = dot(up2_ref[...], XHL[...])
        U[...] = t[:HID] + t[HID:]
        t = dot(dnn2_ref[...], YHL[...])
        DA[...] = t[:HID] + t[HID:]

    def stage_b(buf):
        XHL, YHL, U, DA, AHL, GHL, XN, RS = buf
        for k in range(HID // CH):
            ks = slice(k * CH, (k + 1) * CH)
            kl = slice(HID + k * CH, HID + (k + 1) * CH)
            u = U[ks, :]
            x = 1.0 + (0.3275911 * 0.7071067811865476) * jnp.abs(u)
            t = pl.reciprocal(x, approx=True)
            t = t * (2.0 - x * t)
            e = jnp.exp2(-0.7213475204444817 * (u * u))
            poly = t * (0.5 * 0.254829592 + t * (0.5 * -0.284496736 + t * (0.5 * 1.421413741 + t * (0.5 * -1.453152027 + t * (0.5 * 1.061405429)))))
            q = poly * e
            phi = jnp.where(u >= 0.0, 1.0 - q, q)
            g = phi + (0.3989422804014327 * u) * e
            hi, lo = split(u * phi)
            AHL[ks, :] = hi
            AHL[kl, :] = lo
            hi, lo = split(DA[ks, :] * g)
            GHL[ks, :] = hi
            GHL[kl, :] = lo

    def stage_c(i, buf):
        XHL, YHL, U, DA, AHL, GHL, XN, RS = buf
        y = dot(dn3_ref[:, : 2 * HID], AHL[...]) + dot(dn3_ref[:, 2 * HID :], AHL[0:HID, :])
        for q in range(2):
            h = 2 * i + q
            OUT[pl.ds(h, C, stride=H), :] = fmc * (F[h + 3] + (y[:, q * W : (q + 1) * W] + pb_ref[4]))
        for total, wide, tall in ((GS, YHL, AHL), (GE, XHL, GHL)):
            t = dot(tall[0:HID, :], wide[...], NT)
            total[...] += t[:, :W] + (t[:, W:] + dot(tall[HID:, :], wide[0:W, :], NT))
        dx = dot(upn3_ref[:, : 2 * HID], GHL[...]) + dot(upn3_ref[:, 2 * HID :], GHL[0:HID, :])
        for q in range(2):
            h = 2 * i + q
            d = dx[:, q * W : (q + 1) * W]
            xn = XN[q]
            ACC[0] += d * xn
            ACC[1] += d
            d = d * pb_ref[2]
            m1 = jnp.mean(d, axis=0, keepdims=True)
            m2 = jnp.mean(d * xn, axis=0, keepdims=True)
            d = (d - m1 - xn * m2) * RS[q, 0:1, :]
            D[h] = d
            ACC[2] += d
            hi, lo = split(d)
            hs = pl.ds(pl.multiple_of(h * C, C), C)
            FHL[hs, 0:W] = hi
            FHL[hs, W:] = lo

    def tiles(i, _):
        b0, b1 = lanesets
        stage_a(2 * i, b0)
        stage_a(2 * i + 1, b1)
        stage_b(b0)
        stage_c(2 * i, b0)
        stage_b(b1)
        stage_c(2 * i + 1, b1)
        return 0

    cot_copy.wait()
    lax.fori_loop(0, H // 4, tiles, 0)
    out_copy = pltpu.make_async_copy(OUT, out_hbm, out_sem)
    out_copy.start()

    def shift_gradient():
        shift_rows(DSH, (0, 8 * C), 8 * C)

    def slot(v):
        return v // 48, v % 48 // 3, v % 3

    v = 0
    for total, count in ((GE, 13), (GS, 12)):
        for j in range(3):
            t = total[W * j : W * j + W, :].T
            for i in range(count):
                G[slot(v)] = t[8 * i : 8 * i + 8, :]
                v += 1
    while v < SLOTS:
        G[slot(v)] = jnp.zeros((8, W), f32)
        v += 1

    def rdma(src, dst, send, recv, to):
        return pltpu.make_async_remote_copy(
            src_ref=src, dst_ref=dst, send_sem=send, recv_sem=recv, device_id=to, device_id_type=MESH)

    sibling = (gy + 1 - 2 * core, gx)

    def c0():
        return rdma(G.at[1 - core], R0, s0, r0, sibling)

    def c1(i):
        m = (plane + i) & 15
        return rdma(B0.at[m], R1.at[i], s1.at[i], r1.at[i], at_plane(m, core))

    def c2(i):
        return rdma(B1, R2.at[z], s2.at[i], r2.at[i], at_z((z + i) & 7))

    def g2(i):
        j = (z - i) & 7
        return rdma(B1, R2.at[j], s2.at[i], r2.at[i], at_z(j))

    def c3(i):
        ref = sum_ref.at[core, plane]
        return rdma(ref, ref, s3.at[i], r3.at[i], at_plane((plane + i) & 15, core))

    def g3(i):
        m = (plane - i) & 15
        ref = sum_ref.at[core, m]
        return rdma(ref, ref, s3.at[i], r3.at[i], at_plane(m, core))

    def c4():
        ref = sum_ref.at[core]
        return rdma(ref, ref, s4, r4, sibling)

    def g4():
        ref = sum_ref.at[1 - core]
        return rdma(ref, ref, s4, r4, sibling)

    def step(k):
        if k == 0:
            c0().start()
        elif k == 1:
            c0().wait_recv()
            B0[...] = G[core] + R0[...]
            each(1, 16, lambda i: c1(i).start())
        elif k == 2:
            each(1, 16, lambda i: c1(i).wait_recv())
            acc = B0[plane]
            for i in range(1, 16):
                acc = acc + R1[i]
            B1[...] = acc
            R2[z] = acc
            each(1, 8, lambda i: c2(i).start())
        elif k == 3:
            each(1, 8, lambda i: g2(i).wait_recv())
            acc = R2[0]
            for j in range(1, 8):
                acc = acc + R2[j]
            sum_ref[core, plane] = acc
            each(1, 16, lambda i: c3(i).start())
        elif k == 4:
            each(1, 16, lambda i: g3(i).wait_recv())
            c4().start()
        else:
            g4().wait_recv()
            c0().wait_send()
            each(1, 16, lambda i: c1(i).wait_send())
            each(1, 8, lambda i: c2(i).wait_send())
            each(1, 16, lambda i: c3(i).wait_send())
            c4().wait_send()


    def back_block(cb, _):
        for k, when in enumerate(STEPS):
            @pl.when(cb == when)
            def _(k=k):
                step(k + 1)

        cs = pl.ds(pl.multiple_of(cb * 8, 8), 8)
        def gradient_rows(b):
            if b == 3:
                return [D[h, cs, :] for h in range(H)]
            n = SHIFTS.index(6 - b)
            return [DSH[n, h, cs, :] for h in range(H)]

        grads = jnp.zeros((8, W), f32)
        odd = [F[2 * r + 1, cs, :] for r in range(11)]
        same = [F[2 * r, cs, :] - odd[r] for r in range(11)]
        next_ = [F[2 * r + 2, cs, :] - odd[r] for r in range(10)]

        def correlate(x, y, j):
            t = x[0] * y[j]
            for m in range(1, 8):
                t = t + x[m] * y[m + j]
            return t

        for b in range(7):
            dd = gradient_rows(b)
            d0, d1 = dd[0::2], dd[1::2]
            both = [d0[m] + d1[m] for m in range(8)]
            for j in range(4):
                shared = correlate(both, odd, j)
                for a, part in ((2 * j, (d0, same)), (2 * j + 1, (d1, next_))):
                    if a == 7:
                        continue
                    t = shared + correlate(*part, j)
                    if b < 3:
                        t = t + jnp.where(left, SPX[3 * a + b, cs, :], 0.0)
                    elif b > 3:
                        t = t + jnp.where(left, 0.0, SPX[3 * a + 6 - b, cs, :])
                    total = jnp.sum(t, axis=1, keepdims=True)
                    grads = jnp.where(lane == 7 * a + b, total, grads)

        p0 = [None] * 11
        p1 = [None] * 10
        p2 = [None] * 11

        def convolve(p, x, j, w):
            for m in range(8):
                t = w * x[m]
                p[m + j] = t if p[m + j] is None else p[m + j] + t

        for b in range(7):
            dd = gradient_rows(b)
            d0, d1 = dd[0::2], dd[1::2]
            both = [d0[m] + d1[m] for m in range(8)]
            for j in range(4):
                w0 = wb_ref[7 * (2 * j) + b, cs, :]
                convolve(p0, d0, j, w0)
                if j < 3:
                    w1 = wb_ref[7 * (2 * j + 1) + b, cs, :]
                    convolve(p1, d1, j, w1)
                    w0 = w0 + w1
                convolve(p2, both, j, w0)
        acc = []
        for m in range(11):
            even = p0[m] if m == 0 else p0[m] + p1[m - 1]
            other_row = p2[m] - p0[m]
            if m < 10:
                other_row = other_row - p1[m]
            acc += [even, other_row]
        acc = [t + DY[r - 3, cs, :] if 3 <= r < H + 3 else t for r, t in enumerate(acc)]
        for k, src in enumerate((2, 0, 1, 3)):
            total = jnp.sum(ACC[src, cs, :], axis=1, keepdims=True)
            grads = jnp.where(lane == DEPTH_B + k, total, grads)
        total = DFS[0, cs, :] + DFS[1, cs, :]
        for r in range(EXT):
            t = acc[r]
            if r < 3:
                t = t * top_ok
            elif r >= H + 3:
                t = t * bot_ok
            DF[r, cs, :] = t
            total = total + t
        total = jnp.sum(total, axis=1, keepdims=True)
        GV[cs, :] = jnp.where(lane == STEM_B, total, grads)
        return 0

    step(0)
    shift_gradient()

    packed = jnp.zeros((C, W), f32)
    for h in range(H):
        packed = jnp.where(prow96 == h, roll(D[h], 8 * h + 3), packed)
    packed = jnp.where(left96, roll(packed, -3), jnp.where(right96, roll(packed, 3), 0.0))
    vs = [packed]
    for k in (1, 2):
        vs.append(jnp.where(left96, jnp.where(pos96 >= k, roll(packed, k), 0.0),
                            jnp.where(right96 & (pos96 < 6 - k), roll(packed, -k), 0.0)))
    o0 = jnp.zeros((C, W), f32)
    o1 = jnp.zeros((C, W), f32)
    for a in range(7):
        win = window(a, FS[0], FS[1])
        t = None
        for k in range(3):
            u = wbs_ref[3 * a + k] * vs[k]
            t = u if t is None else t + u
            SPX[3 * a + k] = vs[k] * win
        o0 = o0 + jnp.where((prow96 >= a) & (prow96 < 11), roll(t, 8 * a), 0.0)
        o1 = o1 + jnp.where(prow96 < 5 + a, roll(t, 8 * (a - 11)), 0.0)
    DFS[0] = o0 * jnp.concatenate([ok0] * NB, axis=0)
    DFS[1] = o1 * jnp.concatenate([ok1] * NB, axis=0)

    lax.fori_loop(0, NB, back_block, 0)
    step(len(STEPS) + 1)

    def rows2(p0, p1, d0, d1):
        ph, plo = split(jnp.concatenate([p0, p1], axis=1))
        dh, dlo = split(jnp.concatenate([d0, d1], axis=1))
        t = dot(jnp.concatenate([ph, plo], axis=0), dh, NT)
        return t[:KK] + (t[KK:] + dot(ph, dlo, NT))

    def okpat(p, ok):
        return p if ok is None else jnp.where(ok > 0.0, p, 0.0)

    def row_ok(r):
        return top_ok if r < 3 else bot_ok if r >= H + 3 else None

    okk = [jnp.concatenate([ok] * (KK // 8), axis=0) for ok in (ok0, ok1)]
    gstem = rows2(okpat(side_ref[0], okk[0]), okpat(side_ref[1], okk[1]), DFS[0], DFS[1])
    for r in range(0, EXT, 2):
        gstem = gstem + rows2(
            okpat(pat_ref[r], row_ok(r)), okpat(pat_ref[r + 1], row_ok(r + 1)), DF[r], DF[r + 1])

    zero = jnp.zeros((KK, W - C), f32)
    gs = jnp.concatenate([gstem, zero], axis=1)
    vec = jnp.concatenate([GV[...], jnp.zeros((W - C, W), f32)], axis=0).T
    tail = [gs[8 * i : 8 * i + 8, :] for i in range(6)] + [vec[8 * i : 8 * i + 8, :] for i in range(7)]
    for i, v in enumerate(tail):
        TG[i] = v

    def owner(v):
        return at_plane(v, v & 1)

    mine = ((plane & 1) == core) & (plane < TAIL)

    def t1(v):
        return rdma(TG.at[v], TR.at[plane, core], ts1.at[v], tr1.at[plane, core], owner(v))

    def w1(m, c):
        return rdma(TP, TR.at[m, c], ts1.at[0], tr1.at[m, c], at_plane(m, c))

    def t2(i):
        return rdma(TP, TX.at[z], ts2.at[i], tr2.at[i], at_z((z + i) & 7))

    def w2(i):
        j = (z - i) & 7
        return rdma(TP, TX.at[j], ts2.at[i], tr2.at[i], at_z(j))

    def t3(m, c):
        ref = tail_ref.at[plane]
        return rdma(ref, ref, ts3.at[m, c], tr3.at[plane], at_plane(m, c))

    def w3(v):
        ref = tail_ref.at[v]
        return rdma(ref, ref, ts3.at[0, 0], tr3.at[v], owner(v))

    def others(f):
        def one(i):
            m, c = i >> 1, i & 1
            @pl.when((m != plane) | (c != core))
            def _():
                f(m, c)
        each(0, 32, one)

    def foreign(f):
        def one(v):
            @pl.when((v != plane) | ((v & 1) != core))
            def _():
                f(v)
        each(0, TAIL, one)

    foreign(lambda v: t1(v).start())

    @pl.when(mine)
    def _():
        TR[plane, core] = TG[plane]
        others(lambda m, c: w1(m, c).wait_recv())
        acc = TR[0, 0]
        for i in range(1, 32):
            acc = acc + TR[i >> 1, i & 1]
        TP[...] = acc
        TX[z] = acc
        each(1, 8, lambda i: t2(i).start())

    step(len(STEPS) + 2)

    @pl.when(mine)
    def _():
        each(1, 8, lambda i: w2(i).wait_recv())
        acc = TX[0]
        for j in range(1, 8):
            acc = acc + TX[j]
        tail_ref[plane] = acc
        others(lambda m, c: t3(m, c).start())

    step(len(STEPS) + 3)
    foreign(lambda v: t1(v).wait_send())
    step(len(STEPS) + 4)
    foreign(lambda v: w3(v).wait_recv())

    @pl.when(mine)
    def _():
        each(1, 8, lambda i: t2(i).wait_send())
        others(lambda m, c: t3(m, c).wait_send())

    out_copy.wait()
    for group in range(len(GROUPS)):
        for bucket_at in range(2):
            tile_copy(bucket_at, group).wait_send()
    row_copy(True).wait_send()
    row_copy(False).wait_send()
    for i in range(len(NEAR)):
        edge_copy(i).wait_send()
    for group in (1, 2):
        for i in range(2):
            mid_copy(group, i).wait_send()


def whole_call(*args):
    vm = pl.BlockSpec(memory_space=pltpu.VMEM)
    hbm = pl.BlockSpec(memory_space=pltpu.HBM)
    s = jax.ShapeDtypeStruct
    n_send = INFO + 3 * H
    near = len(NEAR)

    def v(*shape, dtype=f32):
        return pltpu.VMEM(shape, dtype)

    buf = [
        v(2 * XR, 2 * W, dtype=bf16), v(2 * W, 2 * W, dtype=bf16), v(HID, 2 * W), v(HID, 2 * W),
        v(2 * HID, 2 * W, dtype=bf16), v(2 * HID, 2 * W, dtype=bf16), v(2, C, W), v(2, 8, W),
    ]
    return pl.pallas_call(
        whole_kernel,
        out_shape=(s((C * H, W), f32), s((2, 16, 3, 8, W), f32), s((TAIL, 8, W), f32)),
        in_specs=[hbm] * 14,
        out_specs=[hbm, vm, vm],
        scratch_shapes=[
            v(EXT, KK, W), v(2, KK, W), v(8, W), v(TAPS, C, W), v(21, C, W), v(5, C, W),
            v(C, 3 * KK, dtype=bf16), v(2 * HID, 2 * XR, dtype=bf16), v(2 * HID, 2 * W, dtype=bf16),
            v(C, 3 * HID, dtype=bf16), v(C, 3 * HID, dtype=bf16),
            v(8, PIX), v(1, 8, dtype=jnp.int32), v(1, 8, dtype=jnp.int32),
            v(KK, C), v(TAPS, C), v(1, C), v(1, C), v(1, C), v(1, C), v(C, HID), v(HID), v(C, HID), v(1, C),
            v(2, n_send, 8, W), v(2, n_send, 8, W), v(3, KK, W), v(near, KK, W), v(2, 2, KK, W), v(W, W), v(C * H, W),
            DMA((12,)), DMA((12,)), DMA((2, 3)), DMA((2, 3)), DMA((2,)), DMA((2,)),
            DMA((near,)), DMA((near,)), DMA((2, 2)), DMA((2, 2)), DMA(()), DMA(()),
            v(EXT, C, W), v(2, C, W), v(H, C, W), v(6, H, C, W), v(H, C, W), v(HID, W), v(HID, W), v(4, C, W),
            v(EXT * C, 2 * W, dtype=bf16), v(6, EXT, C, W), v(2 * W, 6 * W, dtype=bf16), v(C * H, W),
            v(2, 16, 3, 8, W), v(16, 3, 8, W), v(16, 3, 8, W), v(16, 3, 8, W), v(3, 8, W), v(8, 3, 8, W),
            v(TAIL, 8, W), v(16, 2, 8, W), v(8, W), v(8, 8, W), v(EXT, C, W), v(2, C, W), v(C, W),
            DMA(()), DMA(()), DMA((16,)), DMA((16,)), DMA((8,)), DMA((8,)), DMA((16,)), DMA((16,)), DMA(()), DMA(()),
            DMA((TAIL,)), DMA((16, 2)), DMA((8,)), DMA((8,)), DMA((16, 2)), DMA((TAIL,)), v(21, C, W),
            *buf, *buf,
        ],
        compiler_params=pltpu.CompilerParams(
            collective_id=0, has_side_effects=True, vmem_limit_bytes=56 * 1024 * 1024),
        name="whole",
    )(*args)


PIECES = 4


def unpack_kernel(
    sum_hbm, tail_hbm, block_hbm, out_hbm, gstem_ref, gstem_b_ref, gdepth_ref, gdepth_b_ref, ggain_ref, gnbias_ref,
    gexp_ref, gexp_b_ref, gshr_ref, gshr_b_ref, held, sum_ref, tail_ref, sem,
):
    rows = C * H // PIECES

    def piece(i, back):
        at = pl.ds(i * rows, rows)
        if back:
            return pltpu.make_async_copy(held.at[at], out_hbm.at[at], sem.at[1, i])
        return pltpu.make_async_copy(block_hbm.at[at], held.at[at], sem.at[0, i])

    total = pltpu.make_async_copy(sum_hbm, sum_ref, sem.at[2, 0])
    last = pltpu.make_async_copy(tail_hbm, tail_ref, sem.at[2, 1])
    total.start()
    last.start()
    for i in range(PIECES):
        piece(i, False).start()
    total.wait()
    last.wait()

    def at(v):
        return sum_ref[v // 48, v % 48 // 3, v % 3]

    v = 0
    for j in range(3):
        for i in range(12):
            gexp_ref[8 * i : 8 * i + 8, W * j : W * j + W] = at(v)
            v += 1
        gexp_b_ref[W * j : W * j + W] = at(v)[0]
        v += 1
    for j in range(3):
        for i in range(12):
            gshr_ref[8 * i : 8 * i + 8, W * j : W * j + W] = at(v)
            v += 1
    for i in range(PIECES):
        piece(i, False).wait()
        piece(i, True).start()
    for i in range(6):
        gstem_ref[8 * i : 8 * i + 8, :] = tail_ref[i][:, :C]
        gdepth_ref[8 * i : 8 * i + 8, :] = tail_ref[6 + i][:, :C]
    last = tail_ref[12][:, :C]
    gdepth_ref[48:49, :] = last[0:1]
    for k, ref in enumerate((gstem_b_ref, gdepth_b_ref, ggain_ref, gnbias_ref, gshr_b_ref)):
        ref[...] = last[k + 1 : k + 2]
    for i in range(PIECES):
        piece(i, True).wait()


def unpack_call(block, total, tail):
    vm = pl.BlockSpec(memory_space=pltpu.VMEM)
    hbm = pl.BlockSpec(memory_space=pltpu.HBM)
    shapes = ((KK, C), (1, C), (TAPS, C), (1, C), (1, C), (1, C), (C, HID), (HID,), (C, HID), (1, C))
    return pl.pallas_call(
        unpack_kernel,
        out_shape=tuple(jax.ShapeDtypeStruct(s, f32) for s in ((C * H, W),) + shapes),
        in_specs=[hbm] * 3,
        out_specs=[hbm] + [vm] * len(shapes),
        scratch_shapes=[
            pltpu.VMEM((C * H, W), f32), pltpu.VMEM((2, 16, 3, 8, W), f32), pltpu.VMEM((TAIL, 8, W), f32), DMA((3, PIECES))],
        compiler_params=pltpu.CompilerParams(vmem_limit_bytes=56 * 1024 * 1024),
        name="unpack",
    )(total, tail, block)


def local(
    stored_tiles, tile_target, tile_mask,
    stem_weight, stem_bias, depth_weight, depth_bias, norm_gain, norm_bias,
    expand_weight, expand_bias, shrink_weight, shrink_bias, cotangent,
):
    def row(v):
        return v.reshape(1, -1)

    block, total, tail = whole_call(
        stored_tiles[0], tile_target, tile_mask, stem_weight, depth_weight, row(stem_bias), row(depth_bias),
        row(norm_gain), row(norm_bias), expand_weight, expand_bias, shrink_weight.T, row(shrink_bias),
        cotangent.reshape(C * H, W))
    out, gs, gsb, gd, gdb, gg, gn, ge, geb, gh, ghb = unpack_call(block, total, tail)
    return (
        out.reshape(C, H, W), gs, gsb[0], gd, gdb[0], gg[0], gn[0], ge, geb, gh.T, ghb[0],
    )


def solution(mesh):
    placed = (P("gy", "gx", None), P("gy", "gx"), P("gy", "gx")) + (P(),) * 10 + (P(None, "gy", "gx"),)
    return jax.shard_map(
        local, mesh=mesh, in_specs=placed,
        out_specs=(P(None, "gy", "gx"),) + (P(),) * 10,
        check_vma=False,
    )
```
